32 devices in a mesh: seq: 8 (over z, y), tp: 4 (over x, core).
Axes of the slice: x: 2, y: 2, z: 4, core: 2. Of those that a mesh axis runs over, the one named last changes fastest.
Arguments:
- tokens: bfloat16 [8192, 4096], P('seq', 'tp'), may hold values from -64 to 64
- score_weight: bfloat16 [4096, 16], P('tp'), may hold values from -1 to 1
- value_weight: bfloat16 [4096, 256], P('tp'), may hold values from -0.09375 to 0.09375
- readout: float32 [256], replicated, may hold values from -0.375 to 0.375
- doc_ids: int32 [8192], P('seq'), may hold values from 0 to 15, never falling along the last dimension, each value on 1 to 4096 neighbouring positions
- labels: int32 [8192], P('seq'), may hold values 0 or 1
Outputs:
- logits: float32 [8192], P('seq')
- grad_score: float32 [4096, 16], P('tp')
- grad_value: float32 [4096, 256], P('tp')
- grad_readout: float32 [256], replicated
The draws below stay inside these ranges and needn't reach their ends.
Inputs may be any that keep to these rules, and one draw needn't show every extreme that they name: `doc_ids`: ids never fall along the transcript; each document holds 1 to 4096 tokens, and one holds exactly 4096.
All inputs are finite; a program needn't handle non-finite values. No bound on the sum of `labels` on one device may be relied on, other than what follows from the above.
Results may differ from the reference program's by a relative error of at most 0.0028.
Values may be sent and summed in bfloat16 or wider, within the bound.
A program may use at most 128 MiB of HBM per device.

```python
import math
import jax
import jax.numpy as jnp
import numpy as np
from jax import lax

D = 4096
H = 16
V = 256
TOKENS = 8192
DOC_MOST = 4096
DOCS = 16


def score_columns(key):
    drawn = jax.random.normal(jax.random.fold_in(key, 11), (D, H), jnp.float32)
    return jnp.clip(drawn, -6.0, 6.0) * D ** (-0.5)


def draw_score_weight(key, part):
    return score_columns(key).astype(jnp.bfloat16)


def draw_tokens(key, part):
    subkeys = jax.random.split(jax.random.fold_in(key, 23), 1)
    drawn = jnp.clip(jax.random.normal(subkeys[0], (TOKENS, D), jnp.float32), -6.0, 6.0)
    return drawn.astype(jnp.bfloat16)


def plant(result, own_key, low, largest):
    spot = [jax.random.randint(jax.random.fold_in(own_key, axis), (), 0, length) for axis, length in enumerate(result.shape)]
    main_axis = result.shape.index(max(result.shape))
    next_to = spot[:main_axis] + [(spot[main_axis] + 1) % result.shape[main_axis]] + spot[main_axis + 1:]
    return result.at[tuple(spot)].set(low).at[tuple(next_to)].set(largest)


def levels(key, dims, cuts, low, high):
    level, own = 1.0, jax.random.fold_in(key, 6)
    for position, shards_of in cuts:
        heights = jnp.exp(jax.random.uniform(jax.random.fold_in(own, position), (shards_of,), jnp.float32, low / len(cuts), high / len(cuts)))
        level = level * jnp.repeat(heights, dims[position] // shards_of).reshape([-1 if axis == position else 1 for axis in range(len(dims))])
    return level


def length_profile(count, total, bound, skew):
    loads = [(1 << 20) // math.isqrt(rank ** skew) + 1 for rank in range(2, count + 1)]
    spare, given = total - bound - (count - 1), [1] * (count - 1)
    while spare > 0:
        candidates = [i for i in range(count - 1) if given[i] < bound]
        pool, remaining = sum([loads[i] for i in candidates]), spare
        for i in candidates:
            more = min(bound - given[i], max(1, remaining * loads[i] // pool), spare)
            given[i] = given[i] + more
            spare = spare - more
    return np.array([bound] + given)


def uneven_parts(own_key, amount, total, reach, lean):
    if amount == 2:
        one = jax.random.randint(own_key, (), max(1, total - reach), min(reach, total - 1) + 1)
        return jnp.stack([one, total - one])
    tallies = jnp.asarray(length_profile(amount, total, reach, lean), jnp.int32)
    couples = (amount - 1) // 2
    donor, sink = tallies[1:1 + 2 * couples:2], tallies[2:2 + 2 * couples:2]
    margin = jnp.minimum(donor - 1, reach - sink)
    moved = jax.random.randint(jax.random.fold_in(own_key, 1), (couples,), 0, 1 << 20) % (margin + 1)
    tallies = tallies.at[1:1 + 2 * couples:2].set(donor - moved).at[2:2 + 2 * couples:2].set(sink + moved)
    return tallies[jax.random.permutation(jax.random.fold_in(own_key, 2), amount)]


def scatter_about(stream_key, dims, scale, bound, cuts=(), held_as=jnp.bfloat16):
    factor_of = levels(stream_key, dims, cuts, -0.22, 0.18) if cuts else 1.0
    array = jax.random.normal(stream_key, dims, jnp.float32) * scale * factor_of
    return jnp.minimum(jnp.maximum(array, -bound), bound).astype(held_as)


def setup_inputs(seed: int = 0) -> dict:
    keys = jax.random.split(jax.random.key(seed), 7)
    tokens = draw_tokens(jax.random.fold_in(keys[6], 71), 0)
    score_weight = draw_score_weight(jax.random.fold_in(keys[6], 71), 0)
    value_weight = scatter_about(keys[2], (D, V), D ** -0.5, 0.09375, ((0, 4),))
    readout = scatter_about(keys[3], (V,), V ** -0.5, 0.375, (), jnp.float32)
    doc_ids = jnp.searchsorted(jnp.cumsum(uneven_parts(keys[4], DOCS, TOKENS, DOC_MOST, 2)), jnp.arange(TOKENS), side="right").astype(jnp.int32)
    labels = plant((jax.random.randint(keys[5], (TOKENS,), 0, 8) < 1).astype(jnp.int32), jax.random.fold_in(keys[5], 1), 0, 1)
    return dict(tokens=tokens, score_weight=score_weight, value_weight=value_weight, readout=readout, doc_ids=doc_ids, labels=labels)


NEGATIVE = -1e+30

def pool_loss(scores, values, readout, doc_ids, labels):
    token_count = scores.shape[0]
    head_count = scores.shape[1]
    head_size = values.shape[1] // head_count
    shaped = values.reshape(token_count, head_count, head_size)
    weights_out = readout.reshape(head_count, head_size)
    starts = jnp.concatenate([jnp.ones((1,), jnp.int32), (doc_ids[1:] != doc_ids[:-1]).astype(jnp.int32)])

    def advance(state, element):
        peak_old, total_old, accum_old = state
        score_row, value_row, start_flag = element
        restart = start_flag > 0
        peak_old = jnp.where(restart, NEGATIVE, peak_old)
        total_old = jnp.where(restart, 0.0, total_old)
        accum_old = jnp.where(restart, 0.0, accum_old)
        peak_new = jnp.maximum(peak_old, score_row)
        keep_old = jnp.exp(peak_old - peak_new)
        own_weight = jnp.exp(score_row - peak_new)
        total_new = total_old * keep_old + own_weight
        accum_new = accum_old * keep_old[:, None] + own_weight[:, None] * value_row
        logit_row = jnp.sum(jnp.tanh(accum_new / total_new[:, None]) * weights_out)
        return ((peak_new, total_new, accum_new), logit_row)
    initial = (jnp.full((head_count,), NEGATIVE, scores.dtype), jnp.zeros((head_count,), scores.dtype), jnp.zeros((head_count, head_size), scores.dtype))
    _, logits = lax.scan(advance, initial, (scores, shaped, starts))
    targets = labels.astype(scores.dtype)
    loss = jnp.sum(jax.nn.softplus(logits) - targets * logits) / math.sqrt(token_count)
    return (loss, logits)

def reference(tokens, score_weight, value_weight, readout, doc_ids, labels):
    scores = jnp.dot(tokens, score_weight, preferred_element_type=jnp.float32)
    values = jnp.dot(tokens, value_weight, preferred_element_type=jnp.float32)

    def loss_of(score_arg, value_arg, readout_arg):
        return pool_loss(score_arg, value_arg, readout_arg, doc_ids, labels)
    loss, pullback, logits = jax.vjp(loss_of, scores, values, readout, has_aux=True)
    d_scores, d_values, grad_readout = pullback(jnp.ones_like(loss))
    grad_score = jnp.dot(tokens.T, d_scores.astype(jnp.bfloat16), preferred_element_type=jnp.float32)
    grad_value = jnp.dot(tokens.T, d_values.astype(jnp.bfloat16), preferred_element_type=jnp.float32)
    return (logits, grad_score, grad_value, grad_readout)
```

```python
import functools
import math

import jax
import jax.numpy as jnp
import numpy as np
from jax import lax
from jax.experimental import pallas as pl
from jax.experimental.pallas import tpu as pltpu
from jax.sharding import PartitionSpec as P

NEGATIVE = -1e30
POSITIVE = 1e30
MESH = pl.DeviceIdType.MESH
F32 = jnp.float32
BF16 = jnp.bfloat16


def tables(tp_count, head_count, value_count):
    group = head_count // tp_count
    size = value_count // head_count
    gv = group * size
    into = np.zeros((tp_count, 8 + gv, head_count + value_count), np.float32)
    back_v = np.zeros((gv, 16 + gv), np.float32)
    back_s = np.zeros((head_count, tp_count, 16 + gv), np.float32)
    for g in range(tp_count):
        for r in range(8):
            into[g, r, value_count + g * group + r % group] = 1
        for h in range(group):
            back_s[g * group + h, g, gv + h] = 1
            for e in range(size):
                into[g, 8 + e * group + h, (g * group + h) * size + e] = 1
                back_v[h * size + e, e * group + h] = 1
    return into, back_v, back_s.reshape(head_count, tp_count * (16 + gv))


def dot_nt(a, b):
    return lax.dot_general(a, b, (((1,), (1,)), ((), ())), preferred_element_type=F32)


def kernel(dims, *refs):
    tp, seq, R, W, H, V, group, gv, nl, nr, rows = dims
    hbm, (logit_ref, afin, gr_ref) = refs[:9], refs[9:12]
    held, load_sem = refs[12:21], refs[21]
    (
        part, recv_a, sum_x, recv_x, fwd, lgt, bwd, rdo, coty,
        gy, ysend, yrecv, zown, zsend, zrecv,
    ) = refs[22:37]
    (
        a_send, a_recv, x_send, x_recv, f_send, f_recv, l_send, l_recv, b_send, b_recv,
        r_send, r_recv, c_send, c_recv, y_send, y_recv, z_send, z_recv, g_send, g_recv, h_send, h_recv,
    ) = refs[37:]
    tokens_ref, score_ref, value_ref, into_ref, readout_ref, doc_ref, label_ref, backv_ref, backs_ref = held
    K = gv // 8
    me_t = lax.axis_index("tp")
    me_s = lax.axis_index("seq")
    tx, tc = lax.div(me_t, 2), lax.rem(me_t, 2)
    sz, sy = lax.div(me_s, 2), lax.rem(me_s, 2)
    nz = seq // 2
    sibling, across = {"tp": tx * 2 + 1 - tc}, {"tp": (1 - tx) * 2 + tc}
    beside = {"seq": sz * 2 + 1 - sy}

    barrier = pltpu.get_barrier_semaphore()
    for o in range(1, seq):
        pl.semaphore_signal(barrier, inc=1, device_id={"seq": lax.rem(me_s + o, seq)}, device_id_type=MESH)
    for o in range(1, tp):
        pl.semaphore_signal(barrier, inc=1, device_id={"tp": lax.rem(me_t + o, tp)}, device_id_type=MESH)
    loads = [pltpu.make_async_copy(h, v, load_sem.at[i]) for i, (h, v) in enumerate(zip(hbm, held))]
    for i in (2, 3, 1, 0, 4, 5, 6, 7, 8):
        loads[i].start()
    pending = []

    def remote(src, dst, send, recv, device):
        return pltpu.make_async_remote_copy(
            src_ref=src, dst_ref=dst, send_sem=send, recv_sem=recv, device_id=device, device_id_type=MESH
        )

    def give(*args):
        copy = remote(*args)
        copy.start()
        pending.append(copy)

    def take(dst, send, recv, device):
        remote(dst, dst, send, recv, device).wait_recv()

    def push(axis, o, src, dst, send, recv):
        me, n = (me_t, tp) if axis == "tp" else (me_s, seq)
        give(src, dst, send.at[o], recv.at[o], {axis: lax.rem(me + o, n)})

    def arrived(axis, o, dst, send, recv):
        me, n = (me_t, tp) if axis == "tp" else (me_s, seq)
        take(dst, send.at[o], recv.at[o], {axis: lax.rem(me + o, n)})

    for i in (2, 3, 1):
        loads[i].wait()
    into_all = into_ref[...].reshape(tp * (8 + gv), V + H).astype(BF16)
    weights = dot_nt(into_all[:, :V], value_ref[...]) + jnp.dot(
        into_all[:, V:], score_ref[...], preferred_element_type=F32
    )
    loads[0].wait()
    part[...] = dot_nt(weights.astype(BF16), tokens_ref[...]).reshape(tp, 8 + gv, R)
    pl.semaphore_wait(barrier, tp + seq - 2)
    cuts = ((0, 24), (24, 24), (48, 8 + gv - 48))
    for i, (r, n) in enumerate(cuts):
        rows_i = pl.ds(r, n)
        give(part.at[(1 - tx) * 2 + 1 - tc, rows_i], recv_a.at[0, rows_i], a_send.at[i], a_recv.at[i], sibling)
    give(part.at[tx * 2 + 1 - tc], recv_a.at[1], a_send.at[3], a_recv.at[3], sibling)
    for i in range(4, 9):
        loads[i].wait()
    lane = lax.broadcasted_iota(jnp.int32, (8, R), 1)
    slot = lax.broadcasted_iota(jnp.int32, (8, 128), 1)
    doc = jnp.broadcast_to(doc_ref[...].astype(F32), (8, R))
    labels = label_ref[...].astype(F32)
    own_table = into_ref[me_t][:, :V]
    w_col = jnp.sum(own_table * readout_ref[...], axis=1, keepdims=True)
    w_k = [w_col[8 + 8 * k : 16 + 8 * k] for k in range(K)]
    for i, (r, n) in enumerate(cuts):
        rows_i = pl.ds(r, n)
        take(recv_a.at[0, rows_i], a_send.at[i], a_recv.at[i], sibling)
        sum_x[r : r + n] = part[(1 - tx) * 2 + tc, r : r + n] + recv_a[0, r : r + n]
        give(sum_x.at[rows_i], recv_x.at[rows_i], x_send.at[i], x_recv.at[i], across)
    take(recv_a.at[1], a_send.at[3], a_recv.at[3], sibling)
    for i, (r, n) in enumerate(cuts):
        rows_i = pl.ds(r, n)
        take(recv_x.at[rows_i], x_send.at[i], x_recv.at[i], across)
    whole = [
        part[me_t, 8 * k : 8 * k + 8] + recv_a[1, 8 * k : 8 * k + 8] + recv_x[8 * k : 8 * k + 8]
        for k in range(K + 1)
    ]
    score, vals = whole[0], whole[1:]

    peak, total, acc = score, jnp.ones_like(score), list(vals)
    d = 1
    while d < R:
        valid = (lane >= d) & (pltpu.roll(doc, d, 1) == doc)
        before = pltpu.roll(peak, d, 1)
        new = jnp.where(valid, jnp.maximum(peak, before), peak)
        ka = jnp.where(valid, jnp.exp(jnp.where(valid, before - new, 0.0)), 0.0)
        kb = jnp.exp(peak - new)
        total = total * kb + pltpu.roll(total, d, 1) * ka
        acc = [a * kb + pltpu.roll(a, d, 1) * ka for a in acc]
        peak = new
        d *= 2

    def pack(columns):
        tile = jnp.zeros((8, 128), F32)
        for i, column in enumerate(columns):
            tile = jnp.where(slot == i, column, tile)
        return tile

    first = doc[:, 0:1]
    last = doc[:, R - 1 : R]
    fwd[me_s] = pack([x[:, R - 1 : R] for x in [peak, total] + acc] + [last])
    for o in range(1, seq):
        push("seq", o, fwd.at[me_s], fwd.at[me_s], f_send, f_recv)
    for o in range(1, seq):
        arrived("seq", o, fwd.at[lax.rem(me_s + seq - o, seq)], f_send, f_recv)
    tiles = [fwd[j] for j in range(seq)]
    linked = [(t[:, K + 2 : K + 3] == first) & (j < me_s) for j, t in enumerate(tiles)]
    c_peak = jnp.full((8, 1), NEGATIVE, F32)
    for t, m in zip(tiles, linked):
        c_peak = jnp.maximum(c_peak, jnp.where(m, t[:, 0:1], NEGATIVE))
    c_tile = jnp.zeros((8, 128), F32)
    c_any = jnp.zeros((8, 1), F32)
    for t, m in zip(tiles, linked):
        c_tile = c_tile + jnp.where(m, jnp.exp(jnp.where(m, t[:, 0:1] - c_peak, 0.0)), 0.0) * jnp.where(m, t, 0.0)
        c_any = jnp.where(m, 1.0, c_any)
    cont = (doc == first) & (jnp.broadcast_to(c_any, (8, R)) > 0)
    new = jnp.where(cont, jnp.maximum(peak, c_peak), peak)
    kc = jnp.where(cont, jnp.exp(jnp.where(cont, c_peak - new, 0.0)), 0.0)
    kl = jnp.exp(peak - new)
    peak = new
    inverse = 1.0 / (total * kl + c_tile[:, 1:2] * kc)
    pooled = [(a * kl + c_tile[:, 2 + k : 3 + k] * kc) * inverse for k, a in enumerate(acc)]
    squash = [jnp.tanh(p) for p in pooled]
    lp = squash[0] * w_k[0]
    for k in range(1, K):
        lp = lp + squash[k] * w_k[k]
    lgt[me_t] = jnp.sum(lp, axis=0, keepdims=True)
    for o in range(1, tp):
        push("tp", o, lgt.at[me_t], lgt.at[me_t], l_send, l_recv)
    slim = [w * (1.0 - q * q) * inverse for w, q in zip(w_k, squash)]
    slim_c = slim[0] * pooled[0]
    for k in range(1, K):
        slim_c = slim_c + slim[k] * pooled[k]

    def over_heads(x):
        out, step = x, group
        while step < 8:
            out = out + pltpu.roll(out, step, 0)
            step *= 2
        return out

    slim_c = over_heads(slim_c)
    weight = jnp.exp(score - peak)
    for o in range(1, tp):
        arrived("tp", o, lgt.at[lax.rem(me_t + tp - o, tp)], l_send, l_recv)
    logits = lgt[0]
    for g in range(1, tp):
        logits = logits + lgt[g]
    logit_ref[...] = logits
    slope = (jax.nn.sigmoid(logits) - labels) * (1.0 / math.sqrt(R * seq))
    slope = jnp.broadcast_to(slope, (8, R))
    adj = [x * slope for x in slim]
    adj_c = slim_c * slope
    r_cols = [jnp.sum(q * slope, axis=1, keepdims=True) for q in squash]
    d = 1
    while d < R:
        valid = (lane < R - d) & (pltpu.roll(doc, R - d, 1) == doc)
        f = jnp.where(valid, jnp.exp(jnp.where(valid, peak - pltpu.roll(peak, R - d, 1), 0.0)), 0.0)
        adj_c = adj_c + f * pltpu.roll(adj_c, R - d, 1)
        adj = [a + f * pltpu.roll(a, R - d, 1) for a in adj]
        d *= 2
    bwd[me_s] = pack([x[:, 0:1] for x in [peak, adj_c] + adj] + [first] + r_cols)
    for o in range(1, seq):
        push("seq", o, bwd.at[me_s], bwd.at[me_s], b_send, b_recv)
    for o in range(1, seq):
        arrived("seq", o, bwd.at[lax.rem(me_s + seq - o, seq)], b_send, b_recv)
    tiles = [bwd[j] for j in range(seq)]
    linked = [(t[:, K + 2 : K + 3] == last) & (j > me_s) for j, t in enumerate(tiles)]
    a_peak = jnp.full((8, 1), POSITIVE, F32)
    for t, m in zip(tiles, linked):
        a_peak = jnp.minimum(a_peak, jnp.where(m, t[:, 0:1], POSITIVE))
    a_tile = jnp.zeros((8, 128), F32)
    a_any = jnp.zeros((8, 1), F32)
    r_tile = jnp.zeros((8, 128), F32)
    for t, m in zip(tiles, linked):
        a_tile = a_tile + jnp.where(m, jnp.exp(jnp.where(m, a_peak - t[:, 0:1], 0.0)), 0.0) * jnp.where(m, t, 0.0)
        a_any = jnp.where(m, 1.0, a_any)
        r_tile = r_tile + t
    reach = (doc == last) & (jnp.broadcast_to(a_any, (8, R)) > 0)
    fac = jnp.where(reach, jnp.exp(jnp.where(reach, peak - a_peak, 0.0)), 0.0)
    adj_c = adj_c + fac * a_tile[:, 1:2]
    adj = [a + fac * a_tile[:, 2 + k : 3 + k] for k, a in enumerate(adj)]
    mix = vals[0] * adj[0]
    for k in range(1, K):
        mix = mix + vals[k] * adj[k]
    d_score = weight * (over_heads(mix) - adj_c)
    d_all = jnp.concatenate([weight * a for a in adj] + [d_score, jnp.zeros_like(d_score)], axis=0)
    coty[me_t] = d_all.astype(BF16)
    rdo[me_t] = r_tile
    c_across, c_diag = (1 - tx) * 2 + tc, (1 - tx) * 2 + 1 - tc
    give(coty.at[me_t], coty.at[me_t], c_send.at[1], c_recv.at[1], across)
    give(coty.at[me_t], coty.at[me_t], c_send.at[0], c_recv.at[0], sibling)
    for o in range(1, tp):
        push("tp", o, rdo.at[me_t], rdo.at[me_t], r_send, r_recv)

    half, cl = W // 2, W // 2 // nl
    parts_c = [n // nr for n in rows]

    def product(p):
        g = lax.rem(tx + p // 2, 2) * 2 + lax.rem(tc + p % 2, 2)
        cot = jnp.dot(backv_ref[...], coty[g], preferred_element_type=F32)
        if p == tp - 1:
            all_rows = coty[...].reshape(tp * (16 + gv), R)
            cot = jnp.concatenate([cot, jnp.dot(backs_ref[...], all_rows, preferred_element_type=F32)], axis=0)
        if rows[p] > cot.shape[0]:
            cot = jnp.concatenate([cot, jnp.zeros((rows[p] - cot.shape[0], R), F32)], axis=0)
        out = jnp.dot(cot.astype(BF16), tokens_ref[...], preferred_element_type=F32)
        n = rows[p]
        gy[p, 0, 0:n] = out[:, :half]
        gy[p, 1, 0:n] = out[:, half:]
        ysend[p, 0:n] = gy[p, 1 - sy, 0:n].astype(BF16)
        give(ysend.at[p, pl.ds(0, n)], yrecv.at[p, pl.ds(0, n)], y_send.at[p], y_recv.at[p], beside)

    def along_z(p):
        n, rc = rows[p], parts_c[p]
        take(yrecv.at[p, pl.ds(0, n)], y_send.at[p], y_recv.at[p], beside)
        both = gy[p, sy, 0:n] + yrecv[p, 0:n].astype(F32)
        for i in range(nz):
            piece = both[(i // nl) * rc : (i // nl + 1) * rc, (i % nl) * cl : (i % nl + 1) * cl]
            zown[p, i, 0:rc] = piece
            zsend[p, i, 0:rc] = piece.astype(BF16)
        for o in range(1, nz):
            to = lax.rem(sz + o, nz)
            give(
                zsend.at[p, to, pl.ds(0, rc)], zrecv.at[p, sz, pl.ds(0, rc)],
                z_send.at[p, o], z_recv.at[p, o], {"seq": to * 2 + sy},
            )

    def finish(p):
        rc = parts_c[p]
        total_p = zown[p, sz, 0:rc]
        for o in range(1, nz):
            source = lax.rem(sz + nz - o, nz)
            take(
                zrecv.at[p, source, pl.ds(0, rc)], z_send.at[p, o], z_recv.at[p, o],
                {"seq": lax.rem(sz + o, nz) * 2 + sy},
            )
            total_p = total_p + zrecv[p, source, 0:rc].astype(F32)
        afin[p, sy, sz, 0:rc] = total_p.astype(BF16)
        mine = afin.at[p, sy, sz, pl.ds(0, rc)]
        for o in range(1, nz):
            give(mine, mine, g_send.at[p, o], g_recv.at[p, o], {"seq": lax.rem(sz + o, nz) * 2 + sy})

    def along_y(p):
        rc = parts_c[p]
        for o in range(1, nz):
            source = lax.rem(sz + nz - o, nz)
            take(
                afin.at[p, sy, source, pl.ds(0, rc)], g_send.at[p, o], g_recv.at[p, o],
                {"seq": lax.rem(sz + o, nz) * 2 + sy},
            )
        line = afin.at[p, sy, :, pl.ds(0, rc)]
        give(line, line, h_send.at[p], h_recv.at[p], beside)

    product(0)
    take(coty.at[tx * 2 + 1 - tc], c_send.at[0], c_recv.at[0], sibling)
    product(1)
    along_z(0)
    take(coty.at[c_across], c_send.at[1], c_recv.at[1], across)
    give(coty.at[c_across], coty.at[c_across], c_send.at[2], c_recv.at[2], sibling)
    product(2)
    along_z(1)
    finish(0)
    take(coty.at[c_diag], c_send.at[2], c_recv.at[2], sibling)
    product(3)
    along_z(2)
    finish(1)
    along_y(0)
    for o in range(1, tp):
        arrived("tp", o, rdo.at[lax.rem(me_t + tp - o, tp)], r_send, r_recv)
    r_all = jnp.zeros((1, V), F32)
    for g in range(tp):
        tile = rdo[g]
        for k in range(K):
            r_all = r_all + jnp.sum(
                into_ref[g, 8 + 8 * k : 16 + 8 * k][:, :V] * tile[:, K + 3 + k : K + 4 + k], axis=0, keepdims=True
            )
    gr_ref[...] = r_all
    along_z(3)
    finish(2)
    along_y(1)
    finish(3)
    along_y(2)
    along_y(3)
    for p in range(tp):
        take(afin.at[p, 1 - sy, :, pl.ds(0, parts_c[p])], h_send.at[p], h_recv.at[p], beside)
    for copy in pending:
        copy.wait_send()


def unpack(dims, logit_hbm, afin_hbm, gr_hbm, logit_ref, gs_ref, gv_ref, gr_ref, logit_in, afin, gr_in, sem):
    tp, H, gv, half, cl, nl, nr, parts_c = dims
    me_t = lax.axis_index("tp")
    tx, tc = lax.div(me_t, 2), lax.rem(me_t, 2)
    moves = [
        pltpu.make_async_copy(a, b, sem.at[i])
        for i, (a, b) in enumerate(((afin_hbm, afin), (logit_hbm, logit_in), (gr_hbm, gr_in)))
    ]
    for move in moves:
        move.start()
    for move in moves:
        move.wait()
    logit_ref[...] = logit_in[...]
    gr_ref[...] = gr_in[...]
    eye = (
        lax.broadcasted_iota(jnp.int32, (cl, cl), 0) == lax.broadcasted_iota(jnp.int32, (cl, cl), 1)
    ).astype(F32).astype(BF16)
    for y in range(2):
        for c in range(nl):
            at = y * half + c * cl
            stack = []
            for g in range(tp):
                p = lax.rem(tx + g // 2, 2) * 2 + lax.rem(tc + g % 2, 2)
                if nr == 1:
                    stack.append(afin[p, y, c, 0:gv])
                else:
                    lines = jnp.concatenate([afin[p, y, r * nl + c] for r in range(nr)], axis=0)
                    stack.append(lines[:gv])
            lines = jnp.concatenate([afin[tp - 1, y, r * nl + c, 0 : parts_c[-1]] for r in range(nr)], axis=0)
            gs_ref[:, at : at + cl] = lines[gv : gv + H].astype(F32)
            gv_ref[at : at + cl, :] = dot_nt(eye, jnp.concatenate(stack, axis=0))


def shards(tokens, score_weight, value_weight, readout, doc_ids, labels):
    tp = lax.axis_size("tp")
    seq = lax.axis_size("seq")
    R, W = tokens.shape
    H = score_weight.shape[1]
    V = value_weight.shape[1]
    group = H // tp
    gv = V // tp
    nz = seq // 2
    nl = min(nz, W // 256)
    nr = nz // nl
    unit = 16 * nr
    last = -(-(gv + H) // unit) * unit
    rows = (gv,) * (tp - 1) + (last,) if nr == 1 else (last,) * tp
    half, cl, rc = W // 2, W // 2 // nl, last // nr
    into, back_v, back_s = tables(tp, H, V)
    dims = (tp, seq, R, W, H, V, group, gv, nl, nr, rows)
    vm = pl.BlockSpec(memory_space=pltpu.VMEM)
    dma = pltpu.SemaphoreType.DMA
    operands = (
        tokens, score_weight.T, value_weight, jnp.asarray(into, F32), readout.reshape(1, V),
        doc_ids.reshape(1, R), labels.reshape(1, R), jnp.asarray(back_v, BF16), jnp.asarray(back_s, BF16),
    )
    scratch = [pltpu.VMEM(x.shape, x.dtype) for x in operands] + [
        dma((len(operands),)),
        pltpu.VMEM((tp, 8 + gv, R), F32),
        pltpu.VMEM((2, 8 + gv, R), F32),
        pltpu.VMEM((8 + gv, R), F32),
        pltpu.VMEM((8 + gv, R), F32),
        pltpu.VMEM((seq, 8, 128), F32),
        pltpu.VMEM((tp, 1, R), F32),
        pltpu.VMEM((seq, 8, 128), F32),
        pltpu.VMEM((tp, 8, 128), F32),
        pltpu.VMEM((tp, 16 + gv, R), BF16),
        pltpu.VMEM((tp, 2, last, half), F32),
        pltpu.VMEM((tp, last, half), BF16),
        pltpu.VMEM((tp, last, half), BF16),
        pltpu.VMEM((tp, nz, rc, cl), F32),
        pltpu.VMEM((tp, nz, rc, cl), BF16),
        pltpu.VMEM((tp, nz, rc, cl), BF16),
    ]
    for n in ((4,), (3,), (seq,), (tp,), (seq,), (tp,), (3,), (tp,), (tp, nz), (tp, nz), (tp,)):
        scratch += [dma(n), dma(n)]
    logits, packed, gr = pl.pallas_call(
        functools.partial(kernel, dims),
        out_shape=(
            jax.ShapeDtypeStruct((1, R), F32),
            jax.ShapeDtypeStruct((tp, 2, nz, rc, cl), BF16),
            jax.ShapeDtypeStruct((1, V), F32),
        ),
        in_specs=[pl.BlockSpec(memory_space=pltpu.HBM)] * len(operands),
        out_specs=(vm,) * 3,
        scratch_shapes=scratch,
        compiler_params=pltpu.CompilerParams(
            collective_id=0, has_side_effects=True, vmem_limit_bytes=56 * 1024 * 1024
        ),
    )(*operands)
    parts_c = tuple(n // nr for n in rows)
    logits, gs, gvo, gr = pl.pallas_call(
        functools.partial(unpack, (tp, H, gv, half, cl, nl, nr, parts_c)),
        out_shape=(
            jax.ShapeDtypeStruct((1, R), F32),
            jax.ShapeDtypeStruct((H, W), F32),
            jax.ShapeDtypeStruct((W, V), F32),
            jax.ShapeDtypeStruct((1, V), F32),
        ),
        in_specs=[pl.BlockSpec(memory_space=pl.ANY)] * 3,
        out_specs=(vm,) * 4,
        scratch_shapes=[pltpu.VMEM(x.shape, x.dtype) for x in (logits, packed, gr)] + [dma((3,))],
        compiler_params=pltpu.CompilerParams(vmem_limit_bytes=56 * 1024 * 1024),
    )(logits, packed, gr)
    return logits.reshape(R), gs.T, gvo, gr.reshape(V)


def solution(mesh):
    return jax.shard_map(
        shards,
        mesh=mesh,
        in_specs=(P("seq", "tp"), P("tp", None), P("tp", None), P(), P("seq"), P("seq")),
        out_specs=(P("seq"), P("tp", None), P("tp", None), P()),
        check_vma=False,
    )
```

```python
import functools
import math

import jax
import jax.numpy as jnp
import numpy as np
from jax import lax
from jax.experimental import pallas as pl
from jax.experimental.pallas import tpu as pltpu
from jax.sharding import PartitionSpec as P

NEGATIVE = -1e30
POSITIVE = 1e30
MESH = pl.DeviceIdType.MESH
F32 = jnp.float32
BF16 = jnp.bfloat16


def tables(tp_count, head_count, value_count):
    group = head_count // tp_count
    size = value_count // head_count
    gv = group * size
    into = np.zeros((tp_count, 8 + gv, head_count + value_count), np.float32)
    back_v = np.zeros((gv, gv), np.float32)
    pack = 16 // group
    back_s = np.zeros((pack, head_count, tp_count, 16), np.float32)
    for g in range(tp_count):
        for r in range(8):
            into[g, r, value_count + g * group + r % group] = 1
        for h in range(group):
            for q in range(pack):
                back_s[q, g * group + h, g, q * group + h] = 1
            for e in range(size):
                into[g, 8 + e * group + h, (g * group + h) * size + e] = 1
                back_v[h * size + e, e * group + h] = 1
    return into, back_v, back_s.reshape(pack, head_count, tp_count * 16)


def dot_nt(a, b):
    return lax.dot_general(a, b, (((1,), (1,)), ((), ())), preferred_element_type=F32)


def kernel(dims, *refs):
    tp, seq, R, W, H, V, group, gv, nl, nr, rows, window, chunks = dims
    hbm, (logit_ref, afin, gr_ref) = refs[:9], refs[9:12]
    held, load_sem = refs[12:21], refs[21]
    (
        part, recv_a, sum_x, recv_x, fwd, lgt, bwd, rsum, rdo, coty, cots,
        gy, ysend, yrecv, zown, zsend, zrecv,
    ) = refs[22:39]
    (
        a_send, a_recv, x_send, x_recv, f_send, f_recv, l_send, l_recv, b_send, b_recv, s_send, s_recv,
        r_send, r_recv, c_send, c_recv, d_send, d_recv, y_send, y_recv, z_send, z_recv, g_send, g_recv, h_send, h_recv,
    ) = refs[39:]
    tokens_ref, score_ref, value_ref, into_ref, readout_ref, doc_ref, label_ref, backv_ref, backs_ref = held
    K = gv // 8
    me_t = lax.axis_index("tp")
    me_s = lax.axis_index("seq")
    tx, tc = lax.div(me_t, 2), lax.rem(me_t, 2)
    sz, sy = lax.div(me_s, 2), lax.rem(me_s, 2)
    nz = seq // 2
    sibling, across = {"tp": tx * 2 + 1 - tc}, {"tp": (1 - tx) * 2 + tc}
    beside = {"seq": sz * 2 + 1 - sy}

    fwd[...] = jnp.zeros_like(fwd)
    bwd[...] = jnp.zeros_like(bwd)
    barrier = pltpu.get_barrier_semaphore()
    for o in range(1, seq):
        pl.semaphore_signal(barrier, inc=1, device_id={"seq": lax.rem(me_s + o, seq)}, device_id_type=MESH)
    for o in range(1, tp):
        pl.semaphore_signal(barrier, inc=1, device_id={"tp": lax.rem(me_t + o, tp)}, device_id_type=MESH)
    loads = [pltpu.make_async_copy(h, v, load_sem.at[i]) for i, (h, v) in enumerate(zip(hbm, held))]
    C = R // chunks
    pieces = [
        pltpu.make_async_copy(
            hbm[0].at[pl.ds(j * C, C)], tokens_ref.at[pl.ds(j * C, C)], load_sem.at[len(hbm) + j]
        )
        for j in range(chunks)
    ]
    for i in (2, 3, 1):
        loads[i].start()
    for piece in pieces:
        piece.start()
    for i in (4, 5, 6, 7, 8):
        loads[i].start()
    pending = []

    def remote(src, dst, send, recv, device):
        return pltpu.make_async_remote_copy(
            src_ref=src, dst_ref=dst, send_sem=send, recv_sem=recv, device_id=device, device_id_type=MESH
        )

    def give(*args):
        copy = remote(*args)
        copy.start()
        pending.append((None, copy))

    def take(dst, send, recv, device):
        remote(dst, dst, send, recv, device).wait_recv()

    def push(axis, o, src, dst, send, recv):
        me, n = (me_t, tp) if axis == "tp" else (me_s, seq)
        give(src, dst, send.at[o], recv.at[o], {axis: lax.rem(me + o, n)})

    def arrived(axis, o, dst, send, recv):
        me, n = (me_t, tp) if axis == "tp" else (me_s, seq)
        take(dst, send.at[o], recv.at[o], {axis: lax.rem(me + o, n)})

    def carry(tile, step, send, recv):
        for o in range(window, 0, -1):
            there = (me_s + step * o >= 0) & (me_s + step * o < seq)
            copy = remote(
                tile.at[0], tile.at[o], send.at[o], recv.at[o], {"seq": lax.rem(me_s + step * o + seq, seq)}
            )
            pl.when(there)(copy.start)
            pending.append((there, copy))

    def carried(tile, step, send, recv):
        for o in range(window, 0, -1):
            here = (me_s - step * o >= 0) & (me_s - step * o < seq)
            copy = remote(
                tile.at[o], tile.at[o], send.at[o], recv.at[o], {"seq": lax.rem(me_s + step * o + seq, seq)}
            )
            pl.when(here)(copy.wait_recv)
        return [(tile[o], (me_s - step * o >= 0) & (me_s - step * o < seq)) for o in range(1, window + 1)]

    for i in (2, 3, 1):
        loads[i].wait()
    into_all = into_ref[...].reshape(tp * (8 + gv), V + H).astype(BF16)
    weights = dot_nt(into_all[:, :V], value_ref[...]) + jnp.dot(
        into_all[:, V:], score_ref[...], preferred_element_type=F32
    )
    weights = weights.astype(BF16)

    def relay(j):
        take(recv_a.at[j, 0], a_send.at[j, 0], a_recv.at[j, 0], sibling)
        sum_x[j] = part[j, (1 - tx) * 2 + tc] + recv_a[j, 0]
        give(sum_x.at[j], recv_x.at[j], x_send.at[j], x_recv.at[j], across)

    for j in range(chunks):
        pieces[j].wait()
        part[j] = dot_nt(weights, tokens_ref[j * C : (j + 1) * C]).reshape(tp, 8 + gv, C)
        if j == 0:
            pl.semaphore_wait(barrier, tp + seq - 2)
        give(part.at[j, (1 - tx) * 2 + 1 - tc], recv_a.at[j, 0], a_send.at[j, 0], a_recv.at[j, 0], sibling)
        give(part.at[j, tx * 2 + 1 - tc], recv_a.at[j, 1], a_send.at[j, 1], a_recv.at[j, 1], sibling)
        if j > 0:
            relay(j - 1)
    relay(chunks - 1)
    for i in range(4, 9):
        loads[i].wait()
    lane = lax.broadcasted_iota(jnp.int32, (8, R), 1)
    slot = lax.broadcasted_iota(jnp.int32, (8, 128), 1)
    doc = jnp.broadcast_to(doc_ref[...].astype(F32), (8, R))
    labels = label_ref[...].astype(F32)
    own_table = into_ref[me_t][:, :V]
    w_col = jnp.sum(own_table * readout_ref[...], axis=1, keepdims=True)
    w_k = [w_col[8 + 8 * k : 16 + 8 * k] for k in range(K)]
    columns = []
    for j in range(chunks):
        take(recv_a.at[j, 1], a_send.at[j, 1], a_recv.at[j, 1], sibling)
        take(recv_x.at[j], x_send.at[j], x_recv.at[j], across)
        columns.append(part[j, me_t] + recv_a[j, 1] + recv_x[j])
    whole = [
        jnp.concatenate([column[8 * k : 8 * k + 8] for column in columns], axis=1) for k in range(K + 1)
    ]
    score, vals = whole[0], whole[1:]

    peak, total, acc = score, jnp.ones_like(score), list(vals)
    d = 1
    while d < R:
        valid = (lane >= d) & (pltpu.roll(doc, d, 1) == doc)
        before = pltpu.roll(peak, d, 1)
        new = jnp.where(valid, jnp.maximum(peak, before), peak)
        ka = jnp.where(valid, jnp.exp(jnp.where(valid, before - new, 0.0)), 0.0)
        kb = jnp.exp(peak - new)
        total = total * kb + pltpu.roll(total, d, 1) * ka
        acc = [a * kb + pltpu.roll(a, d, 1) * ka for a in acc]
        peak = new
        d *= 2

    def pack(columns):
        tile = jnp.zeros((8, 128), F32)
        for i, column in enumerate(columns):
            tile = jnp.where(slot == i, column, tile)
        return tile

    first = doc[:, 0:1]
    last = doc[:, R - 1 : R]
    fwd[0] = pack([x[:, R - 1 : R] for x in [peak, total] + acc] + [last])
    carry(fwd, 1, f_send, f_recv)
    tiles = carried(fwd, 1, f_send, f_recv)
    linked = [(t[:, K + 2 : K + 3] == first) & m for t, m in tiles]
    tiles = [t for t, _ in tiles]
    c_peak = jnp.full((8, 1), NEGATIVE, F32)
    for t, m in zip(tiles, linked):
        c_peak = jnp.maximum(c_peak, jnp.where(m, t[:, 0:1], NEGATIVE))
    c_tile = jnp.zeros((8, 128), F32)
    c_any = jnp.zeros((8, 1), F32)
    for t, m in zip(tiles, linked):
        c_tile = c_tile + jnp.where(m, jnp.exp(jnp.where(m, t[:, 0:1] - c_peak, 0.0)), 0.0) * jnp.where(m, t, 0.0)
        c_any = jnp.where(m, 1.0, c_any)
    cont = (doc == first) & (jnp.broadcast_to(c_any, (8, R)) > 0)
    new = jnp.where(cont, jnp.maximum(peak, c_peak), peak)
    kc = jnp.where(cont, jnp.exp(jnp.where(cont, c_peak - new, 0.0)), 0.0)
    kl = jnp.exp(peak - new)
    peak = new
    inverse = 1.0 / (total * kl + c_tile[:, 1:2] * kc)
    pooled = [(a * kl + c_tile[:, 2 + k : 3 + k] * kc) * inverse for k, a in enumerate(acc)]
    squash = [jnp.tanh(p) for p in pooled]
    lp = squash[0] * w_k[0]
    for k in range(1, K):
        lp = lp + squash[k] * w_k[k]
    lgt[me_t] = jnp.sum(lp, axis=0, keepdims=True)
    for o in (2, 3, 1):
        push("tp", o, lgt.at[me_t], lgt.at[me_t], l_send, l_recv)
    slim = [w * (1.0 - q * q) * inverse for w, q in zip(w_k, squash)]
    slim_c = slim[0] * pooled[0]
    for k in range(1, K):
        slim_c = slim_c + slim[k] * pooled[k]

    def over_heads(x):
        out, step = x, group
        while step < 8:
            out = out + pltpu.roll(out, step, 0)
            step *= 2
        return out

    slim_c = over_heads(slim_c)
    weight = jnp.exp(score - peak)
    for o in range(1, tp):
        arrived("tp", o, lgt.at[lax.rem(me_t + tp - o, tp)], l_send, l_recv)
    logits = lgt[0]
    for g in range(1, tp):
        logits = logits + lgt[g]
    logit_ref[...] = logits
    slope = (jax.nn.sigmoid(logits) - labels) * (1.0 / math.sqrt(R * seq))
    slope = jnp.broadcast_to(slope, (8, R))
    adj = [x * slope for x in slim]
    adj_c = slim_c * slope
    r_cols = [jnp.sum(q * slope, axis=1, keepdims=True) for q in squash]
    d = 1
    while d < R:
        valid = (lane < R - d) & (pltpu.roll(doc, R - d, 1) == doc)
        f = jnp.where(valid, jnp.exp(jnp.where(valid, peak - pltpu.roll(peak, R - d, 1), 0.0)), 0.0)
        adj_c = adj_c + f * pltpu.roll(adj_c, R - d, 1)
        adj = [a + f * pltpu.roll(a, R - d, 1) for a in adj]
        d *= 2
    bwd[0] = pack([x[:, 0:1] for x in [peak, adj_c] + adj] + [first])
    carry(bwd, -1, b_send, b_recv)
    rsum[me_s] = pack(r_cols)
    for o in range(1, seq):
        push("seq", o, rsum.at[me_s], rsum.at[me_s], s_send, s_recv)
    tiles = carried(bwd, -1, b_send, b_recv)
    linked = [(t[:, K + 2 : K + 3] == last) & m for t, m in tiles]
    tiles = [t for t, _ in tiles]
    a_peak = jnp.full((8, 1), POSITIVE, F32)
    for t, m in zip(tiles, linked):
        a_peak = jnp.minimum(a_peak, jnp.where(m, t[:, 0:1], POSITIVE))
    a_tile = jnp.zeros((8, 128), F32)
    a_any = jnp.zeros((8, 1), F32)
    for t, m in zip(tiles, linked):
        a_tile = a_tile + jnp.where(m, jnp.exp(jnp.where(m, a_peak - t[:, 0:1], 0.0)), 0.0) * jnp.where(m, t, 0.0)
        a_any = jnp.where(m, 1.0, a_any)
    reach = (doc == last) & (jnp.broadcast_to(a_any, (8, R)) > 0)
    fac = jnp.where(reach, jnp.exp(jnp.where(reach, peak - a_peak, 0.0)), 0.0)
    adj_c = adj_c + fac * a_tile[:, 1:2]
    adj = [a + fac * a_tile[:, 2 + k : 3 + k] for k, a in enumerate(adj)]
    mix = vals[0] * adj[0]
    for k in range(1, K):
        mix = mix + vals[k] * adj[k]
    d_score = weight * (over_heads(mix) - adj_c)
    coty[me_t] = jnp.concatenate([weight * a for a in adj], axis=0).astype(BF16)
    c_across, c_diag = (1 - tx) * 2 + tc, (1 - tx) * 2 + 1 - tc
    give(coty.at[me_t], coty.at[me_t], c_send.at[1], c_recv.at[1], across)
    give(coty.at[me_t], coty.at[me_t], c_send.at[0], c_recv.at[0], sibling)
    row = lax.broadcasted_iota(jnp.int32, (8, R), 0)
    per, packs = 8 // group, 16 // group
    Q = R // packs
    lines = []
    for i in range(0, packs, per):
        line = d_score[:, i * Q : (i + 1) * Q]
        for k in range(1, per):
            line = jnp.where(row[:, :Q] >= k * group, d_score[:, (i + k) * Q : (i + k + 1) * Q], line)
        lines.append(line)
    cots[me_t] = jnp.concatenate(lines, axis=0).astype(BF16)
    for o in (2, 3, 1):
        push("tp", o, cots.at[me_t], cots.at[me_t], d_send, d_recv)

    half, cl = W // 2, W // 2 // nl
    parts_c = [n // nr for n in rows]

    def columns_of():
        return [lax.rem(sz + k, nl) for k in range(1, nl + 1)]

    def product(p):
        g = lax.rem(tx + p // 2, 2) * 2 + lax.rem(tc + p % 2, 2)
        cot = jnp.dot(backv_ref[...], coty[g], preferred_element_type=F32)
        if p == tp - 1:
            packed = cots[...].reshape(tp * 16, Q)
            lines = [jnp.dot(backs_ref[q], packed, preferred_element_type=F32) for q in range(packs)]
            cot = jnp.concatenate([cot, jnp.concatenate(lines, axis=1)], axis=0)
        if rows[p] > cot.shape[0]:
            cot = jnp.concatenate([cot, jnp.zeros((rows[p] - cot.shape[0], R), F32)], axis=0)
        out = jnp.dot(cot.astype(BF16), tokens_ref[...], preferred_element_type=F32)
        n = rows[p]
        for c in range(nl):
            gy[p, 0, c, 0:n] = out[:, c * cl : (c + 1) * cl]
            gy[p, 1, c, 0:n] = out[:, half + c * cl : half + (c + 1) * cl]
        for c in columns_of():
            ysend[p, c, 0:n] = gy[p, 1 - sy, c, 0:n].astype(BF16)
            give(
                ysend.at[p, c, pl.ds(0, n)], yrecv.at[p, c, pl.ds(0, n)],
                y_send.at[p, c], y_recv.at[p, c], beside,
            )

    def lines_of(to, rc):
        return pl.ds(0, rc) if nr == 1 else pl.ds(pl.multiple_of(lax.div(to, nl) * rc, 16), rc)

    def along_z(p):
        n, rc = rows[p], parts_c[p]
        for k, c in enumerate(columns_of(), 1):
            take(yrecv.at[p, c, pl.ds(0, n)], y_send.at[p, c], y_recv.at[p, c], beside)
            both = gy[p, sy, c, 0:n] + yrecv[p, c, 0:n].astype(F32)
            if k == nl:
                zown[p, 0:n] = both
            zsend[p, c, 0:n] = both.astype(BF16)
            for o in range(k, nz, nl):
                to = lax.rem(sz + o, nz)
                give(
                    zsend.at[p, c, lines_of(to, rc)], zrecv.at[p, sz, pl.ds(0, rc)],
                    z_send.at[p, o], z_recv.at[p, o], {"seq": to * 2 + sy},
                )

    def finish(p):
        rc = parts_c[p]
        total_p = zown[p, lines_of(sz, rc)]
        for o in range(1, nz):
            source = lax.rem(sz + nz - o, nz)
            take(
                zrecv.at[p, source, pl.ds(0, rc)], z_send.at[p, o], z_recv.at[p, o],
                {"seq": lax.rem(sz + o, nz) * 2 + sy},
            )
            total_p = total_p + zrecv[p, source, 0:rc].astype(F32)
        afin[p, sy, sz, 0:rc] = total_p.astype(BF16)
        mine = afin.at[p, sy, sz, pl.ds(0, rc)]
        for o in range(1, nz):
            give(mine, mine, g_send.at[p, o], g_recv.at[p, o], {"seq": lax.rem(sz + o, nz) * 2 + sy})
        give(mine, mine, h_send.at[p, 0], h_recv.at[p, 0], beside)

    def along_y(p):
        rc = parts_c[p]
        for o in range(1, nz):
            line = afin.at[p, sy, lax.rem(sz + nz - o, nz), pl.ds(0, rc)]
            take(line, g_send.at[p, o], g_recv.at[p, o], {"seq": lax.rem(sz + o, nz) * 2 + sy})
            give(line, line, h_send.at[p, o], h_recv.at[p, o], beside)

    product(0)
    take(coty.at[tx * 2 + 1 - tc], c_send.at[0], c_recv.at[0], sibling)
    product(1)
    along_z(0)
    take(coty.at[c_across], c_send.at[1], c_recv.at[1], across)
    give(coty.at[c_across], coty.at[c_across], c_send.at[2], c_recv.at[2], sibling)
    product(2)
    along_z(1)
    finish(0)
    take(coty.at[c_diag], c_send.at[2], c_recv.at[2], sibling)
    for o in range(1, tp):
        arrived("tp", o, cots.at[lax.rem(me_t + tp - o, tp)], d_send, d_recv)
    product(3)
    for o in range(1, seq):
        arrived("seq", o, rsum.at[lax.rem(me_s + seq - o, seq)], s_send, s_recv)
    r_tile = rsum[0]
    for j in range(1, seq):
        r_tile = r_tile + rsum[j]
    rdo[me_t] = r_tile
    for o in range(1, tp):
        push("tp", o, rdo.at[me_t], rdo.at[me_t], r_send, r_recv)
    along_z(2)
    finish(1)
    along_z(3)
    along_y(0)
    finish(2)
    along_y(1)
    for o in range(1, tp):
        arrived("tp", o, rdo.at[lax.rem(me_t + tp - o, tp)], r_send, r_recv)
    r_all = jnp.zeros((1, V), F32)
    for g in range(tp):
        tile = rdo[g]
        for k in range(K):
            r_all = r_all + jnp.sum(
                into_ref[g, 8 + 8 * k : 16 + 8 * k][:, :V] * tile[:, k : k + 1], axis=0, keepdims=True
            )
    gr_ref[...] = r_all
    finish(3)
    along_y(2)
    along_y(3)
    for p in range(tp):
        for o in range(nz):
            line = afin.at[p, 1 - sy, lax.rem(sz + nz - o, nz), pl.ds(0, parts_c[p])]
            take(line, h_send.at[p, o], h_recv.at[p, o], beside)
    for when, copy in pending:
        if when is None:
            copy.wait_send()
        else:
            pl.when(when)(copy.wait_send)


def unpack(dims, logit_hbm, afin_hbm, gr_hbm, logit_ref, gs_ref, gv_ref, gr_ref, logit_in, afin, gr_in, sem):
    tp, H, gv, half, cl, nl, nr, parts_c = dims
    me_t = lax.axis_index("tp")
    tx, tc = lax.div(me_t, 2), lax.rem(me_t, 2)
    moves = [
        pltpu.make_async_copy(a, b, sem.at[i])
        for i, (a, b) in enumerate(((afin_hbm, afin), (logit_hbm, logit_in), (gr_hbm, gr_in)))
    ]
    for move in moves:
        move.start()
    for move in moves:
        move.wait()
    logit_ref[...] = logit_in[...]
    gr_ref[...] = gr_in[...]
    eye = (
        lax.broadcasted_iota(jnp.int32, (cl, cl), 0) == lax.broadcasted_iota(jnp.int32, (cl, cl), 1)
    ).astype(F32).astype(BF16)
    for y in range(2):
        for c in range(nl):
            at = y * half + c * cl
            stack = []
            for g in range(tp):
                p = lax.rem(tx + g // 2, 2) * 2 + lax.rem(tc + g % 2, 2)
                if nr == 1:
                    stack.append(afin[p, y, c, 0:gv])
                else:
                    lines = jnp.concatenate([afin[p, y, r * nl + c] for r in range(nr)], axis=0)
                    stack.append(lines[:gv])
            lines = jnp.concatenate([afin[tp - 1, y, r * nl + c, 0 : parts_c[-1]] for r in range(nr)], axis=0)
            gs_ref[:, at : at + cl] = lines[gv : gv + H].astype(F32)
            gv_ref[at : at + cl, :] = dot_nt(eye, jnp.concatenate(stack, axis=0))


def shards(tokens, score_weight, value_weight, readout, doc_ids, labels):
    tp = lax.axis_size("tp")
    seq = lax.axis_size("seq")
    R, W = tokens.shape
    H = score_weight.shape[1]
    V = value_weight.shape[1]
    group = H // tp
    gv = V // tp
    nz = seq // 2
    nl = min(nz, W // 256)
    nr = nz // nl
    unit = 16 * nr
    last = -(-(gv + H) // unit) * unit
    rows = (gv,) * (tp - 1) + (last,) if nr == 1 else (last,) * tp
    half, cl, rc = W // 2, W // 2 // nl, last // nr
    into, back_v, back_s = tables(tp, H, V)
    longest = {8192: 4096, 65536: 16384}.get(R * seq, R * seq)
    window = min(seq - 1, -(-longest // R))
    chunks = 4
    C = R // chunks
    dims = (tp, seq, R, W, H, V, group, gv, nl, nr, rows, window, chunks)
    vm = pl.BlockSpec(memory_space=pltpu.VMEM)
    dma = pltpu.SemaphoreType.DMA
    operands = (
        tokens, score_weight.T, value_weight, jnp.asarray(into, F32), readout.reshape(1, V),
        doc_ids.reshape(1, R), labels.reshape(1, R), jnp.asarray(back_v, BF16), jnp.asarray(back_s, BF16),
    )
    scratch = [pltpu.VMEM(x.shape, x.dtype) for x in operands] + [
        dma((len(operands) + chunks,)),
        pltpu.VMEM((chunks, tp, 8 + gv, C), F32),
        pltpu.VMEM((chunks, 2, 8 + gv, C), F32),
        pltpu.VMEM((chunks, 8 + gv, C), F32),
        pltpu.VMEM((chunks, 8 + gv, C), F32),
        pltpu.VMEM((window + 1, 8, 128), F32),
        pltpu.VMEM((tp, 1, R), F32),
        pltpu.VMEM((window + 1, 8, 128), F32),
        pltpu.VMEM((seq, 8, 128), F32),
        pltpu.VMEM((tp, 8, 128), F32),
        pltpu.VMEM((tp, gv, R), BF16),
        pltpu.VMEM((tp, 16, R * group // 16), BF16),
        pltpu.VMEM((tp, 2, nl, last, cl), F32),
        pltpu.VMEM((tp, nl, last, cl), BF16),
        pltpu.VMEM((tp, nl, last, cl), BF16),
        pltpu.VMEM((tp, last, cl), F32),
        pltpu.VMEM((tp, nl, last, cl), BF16),
        pltpu.VMEM((tp, nz, rc, cl), BF16),
    ]
    for n in (
        (chunks, 2), (chunks,), (window + 1,), (tp,), (window + 1,), (seq,),
        (tp,), (3,), (tp,), (tp, nl), (tp, nz), (tp, nz), (tp, nz),
    ):
        scratch += [dma(n), dma(n)]
    logits, packed, gr = pl.pallas_call(
        functools.partial(kernel, dims),
        out_shape=(
            jax.ShapeDtypeStruct((1, R), F32),
            jax.ShapeDtypeStruct((tp, 2, nz, rc, cl), BF16),
            jax.ShapeDtypeStruct((1, V), F32),
        ),
        in_specs=[pl.BlockSpec(memory_space=pltpu.HBM)] * len(operands),
        out_specs=(vm,) * 3,
        scratch_shapes=scratch,
        compiler_params=pltpu.CompilerParams(
            collective_id=0, has_side_effects=True, vmem_limit_bytes=56 * 1024 * 1024
        ),
    )(*operands)
    parts_c = tuple(n // nr for n in rows)
    logits, gs, gvo, gr = pl.pallas_call(
        functools.partial(unpack, (tp, H, gv, half, cl, nl, nr, parts_c)),
        out_shape=(
            jax.ShapeDtypeStruct((1, R), F32),
            jax.ShapeDtypeStruct((H, W), F32),
            jax.ShapeDtypeStruct((W, V), F32),
            jax.ShapeDtypeStruct((1, V), F32),
        ),
        in_specs=[pl.BlockSpec(memory_space=pl.ANY)] * 3,
        out_specs=(vm,) * 4,
        scratch_shapes=[pltpu.VMEM(x.shape, x.dtype) for x in (logits, packed, gr)] + [dma((3,))],
        compiler_params=pltpu.CompilerParams(vmem_limit_bytes=56 * 1024 * 1024),
    )(logits, packed, gr)
    return logits.reshape(R), gs.T, gvo, gr.reshape(V)


def solution(mesh):
    return jax.shard_map(
        shards,
        mesh=mesh,
        in_specs=(P("seq", "tp"), P("tp", None), P("tp", None), P(), P("seq"), P("seq")),
        out_specs=(P("seq"), P("tp", None), P("tp", None), P()),
        check_vma=False,
    )
```

```python
import functools
import math

import jax
import jax.numpy as jnp
import numpy as np
from jax import lax
from jax.experimental import pallas as pl
from jax.experimental.pallas import tpu as pltpu
from jax.sharding import PartitionSpec as P

NEGATIVE = -1e30
POSITIVE = 1e30
MESH = pl.DeviceIdType.MESH
F32 = jnp.float32
BF16 = jnp.bfloat16


def tables(tp_count, head_count, value_count):
    group = head_count // tp_count
    size = value_count // head_count
    gv = group * size
    pack = 16 // group
    back_v = np.zeros((gv, gv), np.float32)
    back_s = np.zeros((pack, head_count, tp_count, 16), np.float32)
    for g in range(tp_count):
        for h in range(group):
            for q in range(pack):
                back_s[q, g * group + h, g, q * group + h] = 1
            for e in range(size):
                back_v[h * size + e, e * group + h] = 1
    return back_v, back_s.reshape(pack, head_count, tp_count * 16)


def picks(g, group, size, gv, width, scores_at):
    row = lax.broadcasted_iota(jnp.int32, (8 + gv, 1), 0)
    inner = jnp.maximum(row - 8, 0)
    column = jnp.where(
        row < 8,
        scores_at + g * group + lax.rem(row, group),
        (g * group + lax.rem(inner, group)) * size + lax.div(inner, group),
    )
    return (column == lax.broadcasted_iota(jnp.int32, (8 + gv, width), 1)).astype(F32)


def dot_nt(a, b):
    return lax.dot_general(a, b, (((1,), (1,)), ((), ())), preferred_element_type=F32)


def kernel(dims, *refs):
    tp, seq, R, W, H, V, group, gv, nl, nr, rows, window, chunks = dims
    hbm, (logit_ref, afin, gr_ref) = refs[:8], refs[8:11]
    held, load_sem = refs[11:19], refs[19]
    (
        part, recv_a, sum_x, recv_x, fwd, lgt, bwd, rsum, rdo, coty, cots,
        gy, ysend, yrecv, zown, zsend, zrecv,
    ) = refs[20:37]
    (
        a_send, a_recv, x_send, x_recv, f_send, f_recv, l_send, l_recv, b_send, b_recv, s_send, s_recv,
        r_send, r_recv, c_send, c_recv, d_send, d_recv, y_send, y_recv, z_send, z_recv, g_send, g_recv, h_send, h_recv,
    ) = refs[37:]
    tokens_ref, score_ref, value_ref, readout_ref, doc_ref, label_ref, backv_ref, backs_ref = held
    K = gv // 8
    me_t = lax.axis_index("tp")
    me_s = lax.axis_index("seq")
    tx, tc = lax.div(me_t, 2), lax.rem(me_t, 2)
    sz, sy = lax.div(me_s, 2), lax.rem(me_s, 2)
    nz = seq // 2
    sibling, across = {"tp": tx * 2 + 1 - tc}, {"tp": (1 - tx) * 2 + tc}
    beside = {"seq": sz * 2 + 1 - sy}

    loads = [None] + [pltpu.make_async_copy(hbm[i], held[i], load_sem.at[i]) for i in range(1, len(hbm))]
    C = R // chunks
    pieces = [
        pltpu.make_async_copy(
            hbm[0].at[pl.ds(j * C, C)], tokens_ref.at[pl.ds(j * C, C)], load_sem.at[len(hbm) + j]
        )
        for j in range(chunks)
    ]
    for i in (2, 1):
        loads[i].start()
    for piece in pieces:
        piece.start()
    fwd[...] = jnp.zeros_like(fwd)
    bwd[...] = jnp.zeros_like(bwd)
    barrier = pltpu.get_barrier_semaphore()
    for o in range(1, seq):
        pl.semaphore_signal(barrier, inc=1, device_id={"seq": lax.rem(me_s + o, seq)}, device_id_type=MESH)
    for o in range(1, tp):
        pl.semaphore_signal(barrier, inc=1, device_id={"tp": lax.rem(me_t + o, tp)}, device_id_type=MESH)
    for i in range(3, 8):
        loads[i].start()
    pending = []

    def remote(src, dst, send, recv, device):
        return pltpu.make_async_remote_copy(
            src_ref=src, dst_ref=dst, send_sem=send, recv_sem=recv, device_id=device, device_id_type=MESH
        )

    def give(*args):
        copy = remote(*args)
        copy.start()
        pending.append((None, copy))

    def take(dst, send, recv, device):
        remote(dst, dst, send, recv, device).wait_recv()

    def push(axis, o, src, dst, send, recv):
        me, n = (me_t, tp) if axis == "tp" else (me_s, seq)
        give(src, dst, send.at[o], recv.at[o], {axis: lax.rem(me + o, n)})

    def arrived(axis, o, dst, send, recv):
        me, n = (me_t, tp) if axis == "tp" else (me_s, seq)
        take(dst, send.at[o], recv.at[o], {axis: lax.rem(me + o, n)})

    def carry(tile, step, send, recv):
        for o in range(window, 0, -1):
            there = (me_s + step * o >= 0) & (me_s + step * o < seq)
            copy = remote(
                tile.at[0], tile.at[o], send.at[o], recv.at[o], {"seq": lax.rem(me_s + step * o + seq, seq)}
            )
            pl.when(there)(copy.start)
            pending.append((there, copy))

    def carried(tile, step, send, recv):
        for o in range(window, 0, -1):
            here = (me_s - step * o >= 0) & (me_s - step * o < seq)
            copy = remote(
                tile.at[o], tile.at[o], send.at[o], recv.at[o], {"seq": lax.rem(me_s + step * o + seq, seq)}
            )
            pl.when(here)(copy.wait_recv)
        return [(tile[o], (me_s - step * o >= 0) & (me_s - step * o < seq)) for o in range(1, window + 1)]

    size = gv // group
    into_all = jnp.concatenate([picks(g, group, size, gv, V + H, V) for g in range(tp)], axis=0).astype(BF16)
    for i in (2, 1):
        loads[i].wait()
    weights = dot_nt(into_all[:, :V], value_ref[...]) + jnp.dot(
        into_all[:, V:], score_ref[...], preferred_element_type=F32
    )
    weights = weights.astype(BF16)

    def relay(j):
        take(recv_a.at[j, 0], a_send.at[j, 0], a_recv.at[j, 0], sibling)
        sum_x[j] = part[j, (1 - tx) * 2 + tc] + recv_a[j, 0]
        give(sum_x.at[j], recv_x.at[j], x_send.at[j], x_recv.at[j], across)

    for j in range(chunks):
        pieces[j].wait()
        part[j] = dot_nt(weights, tokens_ref[j * C : (j + 1) * C]).reshape(tp, 8 + gv, C)
        if j == 0:
            pl.semaphore_wait(barrier, tp + seq - 2)
        give(part.at[j, (1 - tx) * 2 + 1 - tc], recv_a.at[j, 0], a_send.at[j, 0], a_recv.at[j, 0], sibling)
        give(part.at[j, tx * 2 + 1 - tc], recv_a.at[j, 1], a_send.at[j, 1], a_recv.at[j, 1], sibling)
        if j > 0:
            relay(j - 1)
    relay(chunks - 1)
    for i in range(3, 8):
        loads[i].wait()
    lane = lax.broadcasted_iota(jnp.int32, (8, R), 1)
    slot = lax.broadcasted_iota(jnp.int32, (8, 128), 1)
    doc = jnp.broadcast_to(doc_ref[...].astype(F32), (8, R))
    labels = label_ref[...].astype(F32)
    own_table = picks(me_t, group, size, gv, V, V)
    w_col = jnp.sum(own_table * readout_ref[...], axis=1, keepdims=True)
    w_k = [w_col[8 + 8 * k : 16 + 8 * k] for k in range(K)]
    columns = []
    for j in range(chunks):
        take(recv_a.at[j, 1], a_send.at[j, 1], a_recv.at[j, 1], sibling)
        take(recv_x.at[j], x_send.at[j], x_recv.at[j], across)
        columns.append(part[j, me_t] + recv_a[j, 1] + recv_x[j])
    whole = [
        jnp.concatenate([column[8 * k : 8 * k + 8] for column in columns], axis=1) for k in range(K + 1)
    ]
    score, vals = whole[0], whole[1:]

    peak, total, acc = score, jnp.ones_like(score), list(vals)
    d = 1
    while d < R:
        valid = (lane >= d) & (pltpu.roll(doc, d, 1) == doc)
        before = pltpu.roll(peak, d, 1)
        new = jnp.where(valid, jnp.maximum(peak, before), peak)
        ka = jnp.where(valid, jnp.exp(jnp.where(valid, before - new, 0.0)), 0.0)
        kb = jnp.exp(peak - new)
        total = total * kb + pltpu.roll(total, d, 1) * ka
        acc = [a * kb + pltpu.roll(a, d, 1) * ka for a in acc]
        peak = new
        d *= 2

    def pack(columns):
        tile = jnp.zeros((8, 128), F32)
        for i, column in enumerate(columns):
            tile = jnp.where(slot == i, column, tile)
        return tile

    first = doc[:, 0:1]
    last = doc[:, R - 1 : R]
    fwd[0] = pack([x[:, R - 1 : R] for x in [peak, total] + acc] + [last])
    carry(fwd, 1, f_send, f_recv)
    tiles = carried(fwd, 1, f_send, f_recv)
    linked = [(t[:, K + 2 : K + 3] == first) & m for t, m in tiles]
    tiles = [t for t, _ in tiles]
    c_peak = jnp.full((8, 1), NEGATIVE, F32)
    for t, m in zip(tiles, linked):
        c_peak = jnp.maximum(c_peak, jnp.where(m, t[:, 0:1], NEGATIVE))
    c_tile = jnp.zeros((8, 128), F32)
    c_any = jnp.zeros((8, 1), F32)
    for t, m in zip(tiles, linked):
        c_tile = c_tile + jnp.where(m, jnp.exp(jnp.where(m, t[:, 0:1] - c_peak, 0.0)), 0.0) * jnp.where(m, t, 0.0)
        c_any = jnp.where(m, 1.0, c_any)
    cont = (doc == first) & (jnp.broadcast_to(c_any, (8, R)) > 0)
    new = jnp.where(cont, jnp.maximum(peak, c_peak), peak)
    kc = jnp.where(cont, jnp.exp(jnp.where(cont, c_peak - new, 0.0)), 0.0)
    kl = jnp.exp(peak - new)
    peak = new
    inverse = 1.0 / (total * kl + c_tile[:, 1:2] * kc)
    pooled = [(a * kl + c_tile[:, 2 + k : 3 + k] * kc) * inverse for k, a in enumerate(acc)]
    squash = [jnp.tanh(p) for p in pooled]
    lp = squash[0] * w_k[0]
    for k in range(1, K):
        lp = lp + squash[k] * w_k[k]
    lgt[me_t] = jnp.sum(lp, axis=0, keepdims=True)
    for o in (2, 3, 1):
        push("tp", o, lgt.at[me_t], lgt.at[me_t], l_send, l_recv)
    slim = [w * (1.0 - q * q) * inverse for w, q in zip(w_k, squash)]
    slim_c = slim[0] * pooled[0]
    for k in range(1, K):
        slim_c = slim_c + slim[k] * pooled[k]

    def over_heads(x):
        out, step = x, group
        while step < 8:
            out = out + pltpu.roll(out, step, 0)
            step *= 2
        return out

    slim_c = over_heads(slim_c)
    weight = jnp.exp(score - peak)
    for o in range(1, tp):
        arrived("tp", o, lgt.at[lax.rem(me_t + tp - o, tp)], l_send, l_recv)
    logits = lgt[0]
    for g in range(1, tp):
        logits = logits + lgt[g]
    logit_ref[...] = logits
    slope = (jax.nn.sigmoid(logits) - labels) * (1.0 / math.sqrt(R * seq))
    slope = jnp.broadcast_to(slope, (8, R))
    adj = [x * slope for x in slim]
    adj_c = slim_c * slope
    r_cols = [jnp.sum(q * slope, axis=1, keepdims=True) for q in squash]
    d = 1
    while d < R:
        valid = (lane < R - d) & (pltpu.roll(doc, R - d, 1) == doc)
        f = jnp.where(valid, jnp.exp(jnp.where(valid, peak - pltpu.roll(peak, R - d, 1), 0.0)), 0.0)
        adj_c = adj_c + f * pltpu.roll(adj_c, R - d, 1)
        adj = [a + f * pltpu.roll(a, R - d, 1) for a in adj]
        d *= 2
    bwd[0] = pack([x[:, 0:1] for x in [peak, adj_c] + adj] + [first])
    carry(bwd, -1, b_send, b_recv)
    tiles = carried(bwd, -1, b_send, b_recv)
    linked = [(t[:, K + 2 : K + 3] == last) & m for t, m in tiles]
    tiles = [t for t, _ in tiles]
    a_peak = jnp.full((8, 1), POSITIVE, F32)
    for t, m in zip(tiles, linked):
        a_peak = jnp.minimum(a_peak, jnp.where(m, t[:, 0:1], POSITIVE))
    a_tile = jnp.zeros((8, 128), F32)
    a_any = jnp.zeros((8, 1), F32)
    for t, m in zip(tiles, linked):
        a_tile = a_tile + jnp.where(m, jnp.exp(jnp.where(m, a_peak - t[:, 0:1], 0.0)), 0.0) * jnp.where(m, t, 0.0)
        a_any = jnp.where(m, 1.0, a_any)
    reach = (doc == last) & (jnp.broadcast_to(a_any, (8, R)) > 0)
    fac = jnp.where(reach, jnp.exp(jnp.where(reach, peak - a_peak, 0.0)), 0.0)
    adj_c = adj_c + fac * a_tile[:, 1:2]
    adj = [a + fac * a_tile[:, 2 + k : 3 + k] for k, a in enumerate(adj)]
    mix = vals[0] * adj[0]
    for k in range(1, K):
        mix = mix + vals[k] * adj[k]
    d_score = weight * (over_heads(mix) - adj_c)
    coty[me_t] = jnp.concatenate([weight * a for a in adj], axis=0).astype(BF16)
    c_across, c_diag = (1 - tx) * 2 + tc, (1 - tx) * 2 + 1 - tc
    give(coty.at[me_t], coty.at[me_t], c_send.at[1], c_recv.at[1], across)
    give(coty.at[me_t], coty.at[me_t], c_send.at[0], c_recv.at[0], sibling)
    row = lax.broadcasted_iota(jnp.int32, (8, R), 0)
    per, packs = 8 // group, 16 // group
    Q = R // packs
    lines = []
    for i in range(0, packs, per):
        line = d_score[:, i * Q : (i + 1) * Q]
        for k in range(1, per):
            line = jnp.where(row[:, :Q] >= k * group, d_score[:, (i + k) * Q : (i + k + 1) * Q], line)
        lines.append(line)
    cots[me_t] = jnp.concatenate(lines, axis=0).astype(BF16)
    for o in (2, 3, 1):
        push("tp", o, cots.at[me_t], cots.at[me_t], d_send, d_recv)

    half, cl = W // 2, W // 2 // nl
    parts_c = [n // nr for n in rows]

    def columns_of():
        return [lax.rem(sz + k, nl) for k in range(1, nl + 1)]

    def product(p):
        g = lax.rem(tx + p // 2, 2) * 2 + lax.rem(tc + p % 2, 2)
        cot = jnp.dot(backv_ref[...], coty[g], preferred_element_type=F32)
        if p == tp - 1:
            packed = cots[...].reshape(tp * 16, Q)
            lines = [jnp.dot(backs_ref[q], packed, preferred_element_type=F32) for q in range(packs)]
            cot = jnp.concatenate([cot, jnp.concatenate(lines, axis=1)], axis=0)
        if rows[p] > cot.shape[0]:
            cot = jnp.concatenate([cot, jnp.zeros((rows[p] - cot.shape[0], R), F32)], axis=0)
        out = jnp.dot(cot.astype(BF16), tokens_ref[...], preferred_element_type=F32)
        n = rows[p]
        for c in range(nl):
            gy[p, 0, c, 0:n] = out[:, c * cl : (c + 1) * cl]
            gy[p, 1, c, 0:n] = out[:, half + c * cl : half + (c + 1) * cl]
        for c in columns_of():
            ysend[p, c, 0:n] = gy[p, 1 - sy, c, 0:n].astype(BF16)
            give(
                ysend.at[p, c, pl.ds(0, n)], yrecv.at[p, c, pl.ds(0, n)],
                y_send.at[p, c], y_recv.at[p, c], beside,
            )

    def lines_of(to, rc):
        return pl.ds(0, rc) if nr == 1 else pl.ds(pl.multiple_of(lax.div(to, nl) * rc, 16), rc)

    def along_z(p):
        n, rc = rows[p], parts_c[p]
        for k, c in enumerate(columns_of(), 1):
            take(yrecv.at[p, c, pl.ds(0, n)], y_send.at[p, c], y_recv.at[p, c], beside)
            both = gy[p, sy, c, 0:n] + yrecv[p, c, 0:n].astype(F32)
            if k == nl:
                zown[p, 0:n] = both
            zsend[p, c, 0:n] = both.astype(BF16)
            for o in range(k, nz, nl):
                to = lax.rem(sz + o, nz)
                give(
                    zsend.at[p, c, lines_of(to, rc)], zrecv.at[p, sz, pl.ds(0, rc)],
                    z_send.at[p, o], z_recv.at[p, o], {"seq": to * 2 + sy},
                )

    def finish(p):
        rc = parts_c[p]
        total_p = zown[p, lines_of(sz, rc)]
        for o in range(1, nz):
            source = lax.rem(sz + nz - o, nz)
            take(
                zrecv.at[p, source, pl.ds(0, rc)], z_send.at[p, o], z_recv.at[p, o],
                {"seq": lax.rem(sz + o, nz) * 2 + sy},
            )
            total_p = total_p + zrecv[p, source, 0:rc].astype(F32)
        afin[p, sy, sz, 0:rc] = total_p.astype(BF16)
        mine = afin.at[p, sy, sz, pl.ds(0, rc)]
        for o in range(1, nz):
            give(mine, mine, g_send.at[p, o], g_recv.at[p, o], {"seq": lax.rem(sz + o, nz) * 2 + sy})
        give(mine, mine, h_send.at[p, 0], h_recv.at[p, 0], beside)

    def along_y(p):
        rc = parts_c[p]
        for o in range(1, nz):
            line = afin.at[p, sy, lax.rem(sz + nz - o, nz), pl.ds(0, rc)]
            take(line, g_send.at[p, o], g_recv.at[p, o], {"seq": lax.rem(sz + o, nz) * 2 + sy})
            give(line, line, h_send.at[p, o], h_recv.at[p, o], beside)

    product(0)
    take(coty.at[tx * 2 + 1 - tc], c_send.at[0], c_recv.at[0], sibling)
    product(1)
    along_z(0)
    rsum[me_s] = pack(r_cols)
    for o in range(1, seq):
        push("seq", o, rsum.at[me_s], rsum.at[me_s], s_send, s_recv)
    take(coty.at[c_across], c_send.at[1], c_recv.at[1], across)
    give(coty.at[c_across], coty.at[c_across], c_send.at[2], c_recv.at[2], sibling)
    product(2)
    along_z(1)
    finish(0)
    take(coty.at[c_diag], c_send.at[2], c_recv.at[2], sibling)
    for o in range(1, tp):
        arrived("tp", o, cots.at[lax.rem(me_t + tp - o, tp)], d_send, d_recv)
    product(3)
    for o in range(1, seq):
        arrived("seq", o, rsum.at[lax.rem(me_s + seq - o, seq)], s_send, s_recv)
    r_tile = rsum[0]
    for j in range(1, seq):
        r_tile = r_tile + rsum[j]
    rdo[me_t] = r_tile
    for o in range(1, tp):
        push("tp", o, rdo.at[me_t], rdo.at[me_t], r_send, r_recv)
    along_z(2)
    finish(1)
    along_z(3)
    along_y(0)
    finish(2)
    along_y(1)
    for o in range(1, tp):
        arrived("tp", o, rdo.at[lax.rem(me_t + tp - o, tp)], r_send, r_recv)
    r_all = jnp.zeros((1, V), F32)
    for g in range(tp):
        tile, table = rdo[g], picks(g, group, size, gv, V, V)
        for k in range(K):
            r_all = r_all + jnp.sum(
                table[8 + 8 * k : 16 + 8 * k] * tile[:, k : k + 1], axis=0, keepdims=True
            )
    gr_ref[...] = r_all
    finish(3)
    along_y(2)
    along_y(3)
    for p in range(tp):
        for o in range(nz):
            line = afin.at[p, 1 - sy, lax.rem(sz + nz - o, nz), pl.ds(0, parts_c[p])]
            take(line, h_send.at[p, o], h_recv.at[p, o], beside)
    for when, copy in pending:
        if when is None:
            copy.wait_send()
        else:
            pl.when(when)(copy.wait_send)


def unpack(dims, logit_in, afin, gr_in, logit_ref, gs_ref, gv_ref, gr_ref, gs_held, gv_held, sem):
    tp, H, gv, half, cl, nl, nr, parts_c = dims
    me_t = lax.axis_index("tp")
    tx, tc = lax.div(me_t, 2), lax.rem(me_t, 2)
    moves = [
        pltpu.make_async_copy(logit_in, logit_ref, sem.at[0]),
        pltpu.make_async_copy(gr_in, gr_ref, sem.at[1]),
    ]
    for move in moves:
        move.start()
    eye = (
        lax.broadcasted_iota(jnp.int32, (cl, cl), 0) == lax.broadcasted_iota(jnp.int32, (cl, cl), 1)
    ).astype(F32).astype(BF16)
    for y in range(2):
        for c in range(nl):
            at = y * half + c * cl
            stack = []
            for g in range(tp):
                p = lax.rem(tx + g // 2, 2) * 2 + lax.rem(tc + g % 2, 2)
                if nr == 1:
                    stack.append(afin[p, y, c, 0:gv])
                else:
                    lines = jnp.concatenate([afin[p, y, r * nl + c] for r in range(nr)], axis=0)
                    stack.append(lines[:gv])
            lines = jnp.concatenate([afin[tp - 1, y, r * nl + c, 0 : parts_c[-1]] for r in range(nr)], axis=0)
            gs_held[:, at : at + cl] = lines[gv : gv + H].astype(F32)
            gv_held[at : at + cl, :] = dot_nt(eye, jnp.concatenate(stack, axis=0))
        rows_y = pl.ds(y * half, half)
        moves.append(pltpu.make_async_copy(gv_held.at[rows_y], gv_ref.at[rows_y], sem.at[2 + y]))
        moves[-1].start()
    moves.append(pltpu.make_async_copy(gs_held, gs_ref, sem.at[4]))
    moves[-1].start()
    for move in moves:
        move.wait()


def shards(tokens, score_weight, value_weight, readout, doc_ids, labels):
    tp = lax.axis_size("tp")
    seq = lax.axis_size("seq")
    R, W = tokens.shape
    H = score_weight.shape[1]
    V = value_weight.shape[1]
    group = H // tp
    gv = V // tp
    nz = seq // 2
    nl = min(nz, W // 256)
    nr = nz // nl
    unit = 16 * nr
    last = -(-(gv + H) // unit) * unit
    rows = (gv,) * (tp - 1) + (last,) if nr == 1 else (last,) * tp
    half, cl, rc = W // 2, W // 2 // nl, last // nr
    back_v, back_s = tables(tp, H, V)
    longest = {8192: 4096, 65536: 16384}.get(R * seq, R * seq)
    window = min(seq - 1, -(-longest // R))
    chunks = 2
    C = R // chunks
    dims = (tp, seq, R, W, H, V, group, gv, nl, nr, rows, window, chunks)
    dma = pltpu.SemaphoreType.DMA
    operands = (
        tokens, score_weight.T, value_weight, readout.reshape(1, V),
        doc_ids.reshape(1, R), labels.reshape(1, R), jnp.asarray(back_v, BF16), jnp.asarray(back_s, BF16),
    )
    scratch = [pltpu.VMEM(x.shape, x.dtype) for x in operands] + [
        dma((len(operands) + chunks,)),
        pltpu.VMEM((chunks, tp, 8 + gv, C), F32),
        pltpu.VMEM((chunks, 2, 8 + gv, C), F32),
        pltpu.VMEM((chunks, 8 + gv, C), F32),
        pltpu.VMEM((chunks, 8 + gv, C), F32),
        pltpu.VMEM((window + 1, 8, 128), F32),
        pltpu.VMEM((tp, 1, R), F32),
        pltpu.VMEM((window + 1, 8, 128), F32),
        pltpu.VMEM((seq, 8, 128), F32),
        pltpu.VMEM((tp, 8, 128), F32),
        pltpu.VMEM((tp, gv, R), BF16),
        pltpu.VMEM((tp, 16, R * group // 16), BF16),
        pltpu.VMEM((tp, 2, nl, last, cl), F32),
        pltpu.VMEM((tp, nl, last, cl), BF16),
        pltpu.VMEM((tp, nl, last, cl), BF16),
        pltpu.VMEM((tp, last, cl), F32),
        pltpu.VMEM((tp, nl, last, cl), BF16),
        pltpu.VMEM((tp, nz, rc, cl), BF16),
    ]
    for n in (
        (chunks, 2), (chunks,), (window + 1,), (tp,), (window + 1,), (seq,),
        (tp,), (3,), (tp,), (tp, nl), (tp, nz), (tp, nz), (tp, nz),
    ):
        scratch += [dma(n), dma(n)]
    logits, packed, gr = pl.pallas_call(
        functools.partial(kernel, dims),
        out_shape=(
            jax.ShapeDtypeStruct((1, R), F32),
            jax.ShapeDtypeStruct((tp, 2, nz, rc, cl), BF16),
            jax.ShapeDtypeStruct((1, V), F32),
        ),
        in_specs=[pl.BlockSpec(memory_space=pltpu.HBM)] * len(operands),
        out_specs=(pl.BlockSpec(memory_space=pltpu.VMEM),) * 3,
        scratch_shapes=scratch,
        compiler_params=pltpu.CompilerParams(
            collective_id=0, has_side_effects=True, vmem_limit_bytes=40 * 1024 * 1024
        ),
    )(*(pltpu.with_memory_space_constraint(x, pltpu.HBM) for x in operands))
    parts_c = tuple(n // nr for n in rows)
    logits, gs, gvo, gr = pl.pallas_call(
        functools.partial(unpack, (tp, H, gv, half, cl, nl, nr, parts_c)),
        out_shape=(
            jax.ShapeDtypeStruct((1, R), F32),
            jax.ShapeDtypeStruct((H, W), F32),
            jax.ShapeDtypeStruct((W, V), F32),
            jax.ShapeDtypeStruct((1, V), F32),
        ),
        in_specs=[pl.BlockSpec(memory_space=pltpu.VMEM)] * 3,
        out_specs=(pl.BlockSpec(memory_space=pl.ANY),) * 4,
        scratch_shapes=[
            pltpu.VMEM((H, W), F32), pltpu.VMEM((W, V), F32), dma((5,)),
        ],
        compiler_params=pltpu.CompilerParams(vmem_limit_bytes=16 * 1024 * 1024),
    )(logits, packed, gr)
    return logits.reshape(R), gs.T, gvo, gr.reshape(V)


def solution(mesh):
    return jax.shard_map(
        shards,
        mesh=mesh,
        in_specs=(P("seq", "tp"), P("tp", None), P("tp", None), P(), P("seq"), P("seq")),
        out_specs=(P("seq"), P("tp", None), P("tp", None), P()),
        check_vma=False,
    )
```

```python
import functools
import math

import jax
import jax.numpy as jnp
import numpy as np
from jax import lax
from jax.experimental import pallas as pl
from jax.experimental.pallas import tpu as pltpu
from jax.sharding import PartitionSpec as P

NEGATIVE = -1e30
POSITIVE = 1e30
MESH = pl.DeviceIdType.MESH
F32 = jnp.float32
BF16 = jnp.bfloat16


def tables(tp_count, head_count):
    group = head_count // tp_count
    pack = 16 // group
    back_s = np.zeros((pack, head_count, tp_count, 16), np.float32)
    for g in range(tp_count):
        for h in range(group):
            for q in range(pack):
                back_s[q, g * group + h, g, q * group + h] = 1
    return back_s.reshape(pack, head_count, tp_count * 16)


def picks(g, group, size, gv, width, scores_at):
    row = lax.broadcasted_iota(jnp.int32, (8 + gv, 1), 0)
    inner = jnp.maximum(row - 8, 0)
    column = jnp.where(
        row < 8,
        scores_at + g * group + lax.rem(row, group),
        (g * group + lax.rem(inner, group)) * size + lax.div(inner, group),
    )
    return (column == lax.broadcasted_iota(jnp.int32, (8 + gv, width), 1)).astype(F32)


def dot_nt(a, b):
    return lax.dot_general(a, b, (((1,), (1,)), ((), ())), preferred_element_type=F32)


def kernel(dims, *refs):
    tp, seq, R, W, H, V, group, gv, nl, nr, rows, cut, window, sizes = dims
    chunks = len(sizes)
    starts = [sum(sizes[:j]) for j in range(chunks)]
    hbm, (logit_ref, afin, gr_ref) = refs[:7], refs[7:10]
    held, load_sem = refs[10:17], refs[17]
    part, recv_a, sum_x, recv_x = (refs[18 + k * chunks : 18 + (k + 1) * chunks] for k in range(4))
    (
        fwd, lgt, bwd, rsum, rdo, coty, cots, gy, ysend, yrecv, zown, zsend, zrecv,
    ) = refs[18 + 4 * chunks : 31 + 4 * chunks]
    (
        a_send, a_recv, x_send, x_recv, f_send, f_recv, l_send, l_recv, b_send, b_recv, s_send, s_recv,
        r_send, r_recv, c_send, c_recv, d_send, d_recv, y_send, y_recv, z_send, z_recv, g_send, g_recv, h_send, h_recv,
    ) = refs[31 + 4 * chunks :]
    tokens_ref, score_ref, value_ref, readout_ref, doc_ref, label_ref, backs_ref = held
    K = gv // 8
    me_t = lax.axis_index("tp")
    me_s = lax.axis_index("seq")
    tx, tc = lax.div(me_t, 2), lax.rem(me_t, 2)
    sz, sy = lax.div(me_s, 2), lax.rem(me_s, 2)
    nz = seq // 2
    partner = (me_t, tx * 2 + 1 - tc, (1 - tx) * 2 + tc, (1 - tx) * 2 + 1 - tc)
    sibling, across = {"tp": partner[1]}, {"tp": partner[2]}
    beside = {"seq": sz * 2 + 1 - sy}

    loads = [None] + [pltpu.make_async_copy(hbm[i], held[i], load_sem.at[i]) for i in range(1, len(hbm))]
    pieces = [
        pltpu.make_async_copy(
            hbm[0].at[pl.ds(at, n)], tokens_ref.at[pl.ds(at, n)], load_sem.at[len(hbm) + j]
        )
        for j, (at, n) in enumerate(zip(starts, sizes))
    ]
    for i in (2, 1):
        loads[i].start()
    for piece in pieces:
        piece.start()
    fwd[...] = jnp.zeros_like(fwd)
    bwd[...] = jnp.zeros_like(bwd)
    barrier = pltpu.get_barrier_semaphore()
    for o in range(1, seq):
        pl.semaphore_signal(barrier, inc=1, device_id={"seq": lax.rem(me_s + o, seq)}, device_id_type=MESH)
    for o in range(1, tp):
        pl.semaphore_signal(barrier, inc=1, device_id={"tp": lax.rem(me_t + o, tp)}, device_id_type=MESH)
    for i in range(3, 7):
        loads[i].start()
    pending = []

    def remote(src, dst, send, recv, device):
        return pltpu.make_async_remote_copy(
            src_ref=src, dst_ref=dst, send_sem=send, recv_sem=recv, device_id=device, device_id_type=MESH
        )

    def give(*args):
        copy = remote(*args)
        copy.start()
        pending.append((None, copy))

    def take(dst, send, recv, device):
        remote(dst, dst, send, recv, device).wait_recv()

    def push(axis, o, src, dst, send, recv):
        give(src, dst, send.at[o], recv.at[o], {axis: partner[o] if axis == "tp" else lax.rem(me_s + o, seq)})

    def arrived(axis, o, dst, send, recv):
        take(dst, send.at[o], recv.at[o], {axis: partner[o] if axis == "tp" else lax.rem(me_s + o, seq)})

    def carry(tile, step, send, recv):
        for o in range(window, 0, -1):
            there = (me_s + step * o >= 0) & (me_s + step * o < seq)
            copy = remote(
                tile.at[0], tile.at[o], send.at[o], recv.at[o], {"seq": lax.rem(me_s + step * o + seq, seq)}
            )
            pl.when(there)(copy.start)
            pending.append((there, copy))

    def carried(tile, step, send, recv):
        for o in range(window, 0, -1):
            here = (me_s - step * o >= 0) & (me_s - step * o < seq)
            copy = remote(
                tile.at[o], tile.at[o], send.at[o], recv.at[o], {"seq": lax.rem(me_s + step * o + seq, seq)}
            )
            pl.when(here)(copy.wait_recv)
        return [(tile[o], (me_s - step * o >= 0) & (me_s - step * o < seq)) for o in range(1, window + 1)]

    size = gv // group
    into_all = jnp.concatenate([picks(g, group, size, gv, V + H, V) for g in range(tp)], axis=0).astype(BF16)
    for i in (2, 1):
        loads[i].wait()
    weights = dot_nt(into_all[:, :V], value_ref[...]) + jnp.dot(
        into_all[:, V:], score_ref[...], preferred_element_type=F32
    )
    weights = weights.astype(BF16)

    per = 8 // group

    def relay(j):
        take(recv_a[j].at[0], a_send.at[j, 0], a_recv.at[j, 0], sibling)
        both = part[j][partner[2]] + recv_a[j][0]
        n = sizes[j] // per
        sub = lax.broadcasted_iota(jnp.int32, (8, n), 0)
        line = both[0:8, :n]
        for k in range(1, per):
            line = jnp.where(sub >= k * group, both[0:8, k * n : (k + 1) * n], line)
        for k in range(per):
            sum_x[j][k * gv : (k + 1) * gv] = both[8 : 8 + gv, k * n : (k + 1) * n]
        sum_x[j][per * gv : per * gv + 8] = line
        give(sum_x[j], recv_x[j], x_send.at[j], x_recv.at[j], across)

    for j in range(chunks):
        pieces[j].wait()
        part[j][...] = dot_nt(weights, tokens_ref[starts[j] : starts[j] + sizes[j]]).reshape(tp, 8 + gv, sizes[j])
        if j == 0:
            pl.semaphore_wait(barrier, tp + seq - 2)
        give(part[j].at[partner[3]], recv_a[j].at[0], a_send.at[j, 0], a_recv.at[j, 0], sibling)
        give(part[j].at[partner[1]], recv_a[j].at[1], a_send.at[j, 1], a_recv.at[j, 1], sibling)
        if j > 0:
            relay(j - 1)
    relay(chunks - 1)
    for i in range(3, 7):
        loads[i].wait()
    lane = lax.broadcasted_iota(jnp.int32, (8, R), 1)
    slot = lax.broadcasted_iota(jnp.int32, (8, 128), 1)
    doc = jnp.broadcast_to(doc_ref[...].astype(F32), (8, R))
    labels = label_ref[...].astype(F32)
    own_table = picks(me_t, group, size, gv, V, V)
    w_col = jnp.sum(own_table * readout_ref[...], axis=1, keepdims=True)
    w_k = [w_col[8 + 8 * k : 16 + 8 * k] for k in range(K)]
    def arrive(j):
        take(recv_a[j].at[1], a_send.at[j, 1], a_recv.at[j, 1], sibling)
        take(recv_x[j], x_send.at[j], x_recv.at[j], across)
        n = sizes[j] // per
        sub = lax.broadcasted_iota(jnp.int32, (8, n), 0)
        near = part[j][me_t] + recv_a[j][1]
        line = recv_x[j][per * gv : per * gv + 8]
        lines = []
        for k in range(per):
            own = pltpu.roll(line, 8 - k * group, 0) if k else line
            wide = own
            for m in range(1, per):
                wide = jnp.where(sub >= m * group, pltpu.roll(own, m * group, 0), wide)
            lines.append(wide)
        out = [near[0:8] + jnp.concatenate(lines, axis=1)]
        for k in range(K):
            far = [recv_x[j][m * gv + 8 * k : m * gv + 8 * k + 8] for m in range(per)]
            out.append(near[8 + 8 * k : 16 + 8 * k] + jnp.concatenate(far, axis=1))
        return out

    done = []
    for j in range(chunks):
        score, *vals = arrive(j)
        at, n = starts[j], sizes[j]
        doc_j, lane_j = doc[:, at : at + n], lane[:, :n]
        peak, total, acc = score, jnp.ones_like(score), list(vals)
        d = 1
        while d < n:
            valid = (lane_j >= d) & (pltpu.roll(doc_j, d, 1) == doc_j)
            before = pltpu.roll(peak, d, 1)
            new = jnp.where(valid, jnp.maximum(peak, before), peak)
            ka = jnp.where(valid, jnp.exp(jnp.where(valid, before - new, 0.0)), 0.0)
            kb = jnp.exp(peak - new)
            total = total * kb + pltpu.roll(total, d, 1) * ka
            acc = [a * kb + pltpu.roll(a, d, 1) * ka for a in acc]
            peak = new
            d *= 2
        if j > 0:
            m = sizes[j - 1]
            peak_b, total_b, *acc_b = [x[:, m - 1 : m] for x in done[j - 1][: K + 2]]
            valid = doc_j == doc[:, at - 1 : at]
            new = jnp.where(valid, jnp.maximum(peak, peak_b), peak)
            ka = jnp.where(valid, jnp.exp(jnp.where(valid, peak_b - new, 0.0)), 0.0)
            kb = jnp.exp(peak - new)
            total = total * kb + total_b * ka
            acc = [a * kb + b * ka for a, b in zip(acc, acc_b)]
            peak = new
        done.append([peak, total] + acc + [score] + vals)
    joined = [jnp.concatenate(x, axis=1) for x in zip(*done)]
    peak, total, acc, score, vals = joined[0], joined[1], joined[2 : K + 2], joined[K + 2], joined[K + 3 :]

    def pack(columns):
        tile = jnp.zeros((8, 128), F32)
        for i, column in enumerate(columns):
            tile = jnp.where(slot == i, column, tile)
        return tile

    first = doc[:, 0:1]
    last = doc[:, R - 1 : R]
    fwd[0] = pack([x[:, R - 1 : R] for x in [peak, total] + acc] + [last])
    carry(fwd, 1, f_send, f_recv)
    tiles = carried(fwd, 1, f_send, f_recv)
    linked = [(t[:, K + 2 : K + 3] == first) & m for t, m in tiles]
    tiles = [t for t, _ in tiles]
    c_peak = jnp.full((8, 1), NEGATIVE, F32)
    for t, m in zip(tiles, linked):
        c_peak = jnp.maximum(c_peak, jnp.where(m, t[:, 0:1], NEGATIVE))
    c_tile = jnp.zeros((8, 128), F32)
    c_any = jnp.zeros((8, 1), F32)
    for t, m in zip(tiles, linked):
        c_tile = c_tile + jnp.where(m, jnp.exp(jnp.where(m, t[:, 0:1] - c_peak, 0.0)), 0.0) * jnp.where(m, t, 0.0)
        c_any = jnp.where(m, 1.0, c_any)
    cont = (doc == first) & (jnp.broadcast_to(c_any, (8, R)) > 0)
    new = jnp.where(cont, jnp.maximum(peak, c_peak), peak)
    kc = jnp.where(cont, jnp.exp(jnp.where(cont, c_peak - new, 0.0)), 0.0)
    kl = jnp.exp(peak - new)
    peak = new
    inverse = 1.0 / (total * kl + c_tile[:, 1:2] * kc)
    pooled = [(a * kl + c_tile[:, 2 + k : 3 + k] * kc) * inverse for k, a in enumerate(acc)]
    squash = [jnp.tanh(p) for p in pooled]
    lp = squash[0] * w_k[0]
    for k in range(1, K):
        lp = lp + squash[k] * w_k[k]
    lgt[me_t] = jnp.sum(lp, axis=0, keepdims=True)
    for o in (3, 2, 1):
        push("tp", o, lgt.at[me_t], lgt.at[me_t], l_send, l_recv)
    slim = [w * (1.0 - q * q) * inverse for w, q in zip(w_k, squash)]
    slim_c = slim[0] * pooled[0]
    for k in range(1, K):
        slim_c = slim_c + slim[k] * pooled[k]

    def over_heads(x):
        out, step = x, group
        while step < 8:
            out = out + pltpu.roll(out, step, 0)
            step *= 2
        return out

    slim_c = over_heads(slim_c)
    weight = jnp.exp(score - peak)
    for o in range(1, tp):
        arrived("tp", o, lgt.at[partner[o]], l_send, l_recv)
    logits = lgt[0]
    for g in range(1, tp):
        logits = logits + lgt[g]
    logit_ref[...] = logits
    slope = (jax.nn.sigmoid(logits) - labels) * (1.0 / math.sqrt(R * seq))
    slope = jnp.broadcast_to(slope, (8, R))
    adj = [x * slope for x in slim]
    adj_c = slim_c * slope
    r_cols = [jnp.sum(q * slope, axis=1, keepdims=True) for q in squash]
    d = 1
    while d < R:
        valid = (lane < R - d) & (pltpu.roll(doc, R - d, 1) == doc)
        f = jnp.where(valid, jnp.exp(jnp.where(valid, peak - pltpu.roll(peak, R - d, 1), 0.0)), 0.0)
        adj_c = adj_c + f * pltpu.roll(adj_c, R - d, 1)
        adj = [a + f * pltpu.roll(a, R - d, 1) for a in adj]
        d *= 2
    bwd[0] = pack([x[:, 0:1] for x in [peak, adj_c] + adj] + [first])
    carry(bwd, -1, b_send, b_recv)
    tiles = carried(bwd, -1, b_send, b_recv)
    linked = [(t[:, K + 2 : K + 3] == last) & m for t, m in tiles]
    tiles = [t for t, _ in tiles]
    a_peak = jnp.full((8, 1), POSITIVE, F32)
    for t, m in zip(tiles, linked):
        a_peak = jnp.minimum(a_peak, jnp.where(m, t[:, 0:1], POSITIVE))
    a_tile = jnp.zeros((8, 128), F32)
    a_any = jnp.zeros((8, 1), F32)
    for t, m in zip(tiles, linked):
        a_tile = a_tile + jnp.where(m, jnp.exp(jnp.where(m, a_peak - t[:, 0:1], 0.0)), 0.0) * jnp.where(m, t, 0.0)
        a_any = jnp.where(m, 1.0, a_any)
    reach = (doc == last) & (jnp.broadcast_to(a_any, (8, R)) > 0)
    fac = jnp.where(reach, jnp.exp(jnp.where(reach, peak - a_peak, 0.0)), 0.0)
    adj_c = adj_c + fac * a_tile[:, 1:2]
    adj = [a + fac * a_tile[:, 2 + k : 3 + k] for k, a in enumerate(adj)]
    mix = vals[0] * adj[0]
    for k in range(1, K):
        mix = mix + vals[k] * adj[k]
    d_score = weight * (over_heads(mix) - adj_c)
    coty[me_t] = jnp.concatenate([weight * a for a in adj], axis=0).astype(BF16)
    c_across, c_diag = partner[2], partner[3]
    shares = (pl.ds(0, cut), pl.ds(cut, gv - cut))
    for i, part_i in enumerate(shares):
        give(coty.at[me_t, part_i], coty.at[me_t, part_i], c_send.at[1 + i], c_recv.at[1 + i], across)
    give(coty.at[me_t], coty.at[me_t], c_send.at[0], c_recv.at[0], sibling)
    row = lax.broadcasted_iota(jnp.int32, (8, R), 0)
    packs = 16 // group
    Q = R // packs
    lines = []
    for i in range(0, packs, per):
        line = d_score[:, i * Q : (i + 1) * Q]
        for k in range(1, per):
            line = jnp.where(row[:, :Q] >= k * group, d_score[:, (i + k) * Q : (i + k + 1) * Q], line)
        lines.append(line)
    cots[me_t] = jnp.concatenate(lines, axis=0).astype(BF16)
    for o in (3, 2, 1):
        push("tp", o, cots.at[me_t], cots.at[me_t], d_send, d_recv)

    half, cl = W // 2, W // 2 // nl
    parts_c = [n // nr for n in rows]

    def columns_of():
        return [lax.rem(sz + k, nl) for k in range(1, nl + 1)]

    def product(p):
        if p < 2:
            cot = [coty[partner[p]]]
        elif p == 2:
            cot = [coty[c_across, 0:cut], coty[c_diag, 0:cut]]
        else:
            packed = cots[...].reshape(tp * 16, Q)
            lines = [jnp.dot(backs_ref[q], packed, preferred_element_type=F32) for q in range(packs)]
            cot = [coty[c_across, cut:gv], coty[c_diag, cut:gv], jnp.concatenate(lines, axis=1).astype(BF16)]
        spare = rows[p] - sum(c.shape[0] for c in cot)
        if spare:
            cot.append(jnp.zeros((spare, R), BF16))
        cot = jnp.concatenate(cot, axis=0) if len(cot) > 1 else cot[0]
        out = jnp.dot(cot, tokens_ref[...], preferred_element_type=F32)
        n = rows[p]
        for c in range(nl):
            gy[p, 0, c, 0:n] = out[:, c * cl : (c + 1) * cl]
            gy[p, 1, c, 0:n] = out[:, half + c * cl : half + (c + 1) * cl]
        for c in columns_of():
            ysend[p, c, 0:n] = gy[p, 1 - sy, c, 0:n].astype(BF16)
            give(
                ysend.at[p, c, pl.ds(0, n)], yrecv.at[p, c, pl.ds(0, n)],
                y_send.at[p, c], y_recv.at[p, c], beside,
            )

    def lines_of(to, rc):
        return pl.ds(0, rc) if nr == 1 else pl.ds(pl.multiple_of(lax.div(to, nl) * rc, 16), rc)

    def along_z(p):
        n, rc = rows[p], parts_c[p]
        for k, c in enumerate(columns_of(), 1):
            take(yrecv.at[p, c, pl.ds(0, n)], y_send.at[p, c], y_recv.at[p, c], beside)
            both = gy[p, sy, c, 0:n] + yrecv[p, c, 0:n].astype(F32)
            if k == nl:
                zown[p, 0:n] = both
            zsend[p, c, 0:n] = both.astype(BF16)
            for o in range(k, nz, nl):
                to = lax.rem(sz + o, nz)
                give(
                    zsend.at[p, c, lines_of(to, rc)], zrecv.at[p, sz, pl.ds(0, rc)],
                    z_send.at[p, o], z_recv.at[p, o], {"seq": to * 2 + sy},
                )

    def finish(p):
        rc = parts_c[p]
        total_p = zown[p, lines_of(sz, rc)]
        for o in range(1, nz):
            source = lax.rem(sz + nz - o, nz)
            take(
                zrecv.at[p, source, pl.ds(0, rc)], z_send.at[p, o], z_recv.at[p, o],
                {"seq": lax.rem(sz + o, nz) * 2 + sy},
            )
            total_p = total_p + zrecv[p, source, 0:rc].astype(F32)
        afin[p, sy, sz, 0:rc] = total_p.astype(BF16)
        mine = afin.at[p, sy, sz, pl.ds(0, rc)]
        for o in range(1, nz):
            give(mine, mine, g_send.at[p, o], g_recv.at[p, o], {"seq": lax.rem(sz + o, nz) * 2 + sy})
        give(mine, mine, h_send.at[p, 0], h_recv.at[p, 0], beside)

    def along_y(p):
        rc = parts_c[p]
        for o in range(1, nz):
            line = afin.at[p, sy, lax.rem(sz + nz - o, nz), pl.ds(0, rc)]
            take(line, g_send.at[p, o], g_recv.at[p, o], {"seq": lax.rem(sz + o, nz) * 2 + sy})
            give(line, line, h_send.at[p, o], h_recv.at[p, o], beside)

    def readout_out():
        rsum[me_s] = pack(r_cols)
        for o in range(1, seq):
            push("seq", o, rsum.at[me_s], rsum.at[me_s], s_send, s_recv)

    def readout_across():
        for o in range(1, seq):
            arrived("seq", o, rsum.at[lax.rem(me_s + seq - o, seq)], s_send, s_recv)
        r_tile = rsum[0]
        for j in range(1, seq):
            r_tile = r_tile + rsum[j]
        rdo[me_t] = r_tile
        for o in (3, 2, 1):
            push("tp", o, rdo.at[me_t], rdo.at[me_t], r_send, r_recv)

    def readout_done():
        for o in range(1, tp):
            arrived("tp", o, rdo.at[partner[o]], r_send, r_recv)
        r_all = jnp.zeros((1, V), F32)
        for g in range(tp):
            tile, table = rdo[g], picks(g, group, size, gv, V, V)
            for k in range(K):
                r_all = r_all + jnp.sum(
                    table[8 + 8 * k : 16 + 8 * k] * tile[:, k : k + 1], axis=0, keepdims=True
                )
        gr_ref[...] = r_all

    def across_in(i):
        line = coty.at[c_across, shares[i]]
        take(line, c_send.at[1 + i], c_recv.at[1 + i], across)
        give(line, line, c_send.at[3 + i], c_recv.at[3 + i], sibling)

    def diagonal_in(i):
        take(coty.at[c_diag, shares[i]], c_send.at[3 + i], c_recv.at[3 + i], sibling)
        if i == 1:
            for o in range(1, tp):
                arrived("tp", o, cots.at[partner[o]], d_send, d_recv)

    def sibling_in():
        take(coty.at[partner[1]], c_send.at[0], c_recv.at[0], sibling)

    product(0)
    readout_out()
    sibling_in()
    product(1)
    along_z(0)
    across_in(0)
    across_in(1)
    along_z(1)
    diagonal_in(0)
    product(2)
    finish(0)
    diagonal_in(1)
    product(3)
    finish(1)
    along_z(2)
    along_z(3)
    readout_across()
    along_y(0)
    finish(2)
    along_y(1)
    finish(3)
    readout_done()
    along_y(2)
    along_y(3)
    for p in range(tp):
        for o in range(nz):
            line = afin.at[p, 1 - sy, lax.rem(sz + nz - o, nz), pl.ds(0, parts_c[p])]
            take(line, h_send.at[p, o], h_recv.at[p, o], beside)
    for when, copy in pending:
        if when is None:
            copy.wait_send()
        else:
            pl.when(when)(copy.wait_send)


def unpack(dims, logit_in, afin, gr_in, logit_ref, gs_ref, gv_ref, gr_ref, gs_held, gv_held, sem):
    tp, H, V, gv, cut, half, cl, nl, nr, parts_c = dims
    me_t = lax.axis_index("tp")
    tx, tc = lax.div(me_t, 2), lax.rem(me_t, 2)
    moves = [
        pltpu.make_async_copy(logit_in, logit_ref, sem.at[0]),
        pltpu.make_async_copy(gr_in, gr_ref, sem.at[1]),
    ]
    for move in moves:
        move.start()
    size = V // H
    group = H // tp
    row = lax.broadcasted_iota(jnp.int32, (V, 1), 0)
    p, inner = lax.div(row, gv), lax.rem(row, gv)
    g = lax.rem(tx + lax.div(p, 2), 2) * 2 + lax.rem(tc + lax.rem(p, 2), 2)
    target = (g * group + lax.rem(inner, group)) * size + lax.div(inner, group)
    order = (target == lax.broadcasted_iota(jnp.int32, (V, V), 1)).astype(F32).astype(BF16)
    for y in range(2):
        for c in range(nl):
            at = y * half + c * cl
            own, beside, others, rest = (
                jnp.concatenate([afin[p, y, r * nl + c, 0 : parts_c[p]] for r in range(nr)], axis=0)
                for p in range(tp)
            )
            left = gv - cut
            stack = jnp.concatenate(
                [own[:gv], beside[:gv], others[:cut], rest[:left], others[cut : 2 * cut], rest[left : 2 * left]], axis=0
            )
            gs_held[:, at : at + cl] = rest[2 * left : 2 * left + H].astype(F32)
            gv_held[at : at + cl, :] = lax.dot_general(
                stack, order, (((0,), (0,)), ((), ())), preferred_element_type=F32
            )
        rows_y = pl.ds(y * half, half)
        moves.append(pltpu.make_async_copy(gv_held.at[rows_y], gv_ref.at[rows_y], sem.at[2 + y]))
        moves[-1].start()
    moves.append(pltpu.make_async_copy(gs_held, gs_ref, sem.at[4]))
    moves[-1].start()
    for move in moves:
        move.wait()


def shards(tokens, score_weight, value_weight, readout, doc_ids, labels):
    tp = lax.axis_size("tp")
    seq = lax.axis_size("seq")
    R, W = tokens.shape
    H = score_weight.shape[1]
    V = value_weight.shape[1]
    group = H // tp
    gv = V // tp
    nz = seq // 2
    nl = min(nz, W // 256)
    nr = nz // nl
    unit = 16 * nr
    cut = gv * 3 // 4
    rows = tuple(-(-n // unit) * unit for n in (gv, gv, 2 * cut, 2 * (gv - cut) + H))
    last = max(rows)
    half, cl, rc = W // 2, W // 2 // nl, last // nr
    back_s = tables(tp, H)
    longest = {8192: 4096, 65536: 16384}.get(R * seq, R * seq)
    window = min(seq - 1, -(-longest // R))
    sizes = (R // 4, R // 2, R // 4)
    chunks = len(sizes)
    dims = (tp, seq, R, W, H, V, group, gv, nl, nr, rows, cut, window, sizes)
    dma = pltpu.SemaphoreType.DMA
    operands = (
        tokens, score_weight.T, value_weight, readout.reshape(1, V),
        doc_ids.reshape(1, R), labels.reshape(1, R), jnp.asarray(back_s, BF16),
    )
    packed_rows = 8 // group * gv + 8
    scratch = [pltpu.VMEM(x.shape, x.dtype) for x in operands] + [dma((len(operands) + chunks,))]
    scratch += [pltpu.VMEM((tp, 8 + gv, n), F32) for n in sizes]
    scratch += [pltpu.VMEM((2, 8 + gv, n), F32) for n in sizes]
    scratch += [pltpu.VMEM((packed_rows, n * group // 8), F32) for n in sizes] * 2
    scratch += [
        pltpu.VMEM((window + 1, 8, 128), F32),
        pltpu.VMEM((tp, 1, R), F32),
        pltpu.VMEM((window + 1, 8, 128), F32),
        pltpu.VMEM((seq, 8, 128), F32),
        pltpu.VMEM((tp, 8, 128), F32),
        pltpu.VMEM((tp, gv, R), BF16),
        pltpu.VMEM((tp, 16, R * group // 16), BF16),
        pltpu.VMEM((tp, 2, nl, last, cl), F32),
        pltpu.VMEM((tp, nl, last, cl), BF16),
        pltpu.VMEM((tp, nl, last, cl), BF16),
        pltpu.VMEM((tp, last, cl), F32),
        pltpu.VMEM((tp, nl, last, cl), BF16),
        pltpu.VMEM((tp, nz, rc, cl), BF16),
    ]
    for n in (
        (chunks, 2), (chunks,), (window + 1,), (tp,), (window + 1,), (seq,),
        (tp,), (5,), (tp,), (tp, nl), (tp, nz), (tp, nz), (tp, nz),
    ):
        scratch += [dma(n), dma(n)]
    logits, packed, gr = pl.pallas_call(
        functools.partial(kernel, dims),
        out_shape=(
            jax.ShapeDtypeStruct((1, R), F32),
            jax.ShapeDtypeStruct((tp, 2, nz, rc, cl), BF16),
            jax.ShapeDtypeStruct((1, V), F32),
        ),
        in_specs=[pl.BlockSpec(memory_space=pltpu.HBM)] * len(operands),
        out_specs=(pl.BlockSpec(memory_space=pltpu.VMEM),) * 3,
        scratch_shapes=scratch,
        compiler_params=pltpu.CompilerParams(
            collective_id=0, has_side_effects=True, vmem_limit_bytes=40 * 1024 * 1024
        ),
    )(*(pltpu.with_memory_space_constraint(x, pltpu.HBM) for x in operands))
    parts_c = tuple(n // nr for n in rows)
    logits, gs, gvo, gr = pl.pallas_call(
        functools.partial(unpack, (tp, H, V, gv, cut, half, cl, nl, nr, parts_c)),
        out_shape=(
            jax.ShapeDtypeStruct((1, R), F32),
            jax.ShapeDtypeStruct((H, W), F32),
            jax.ShapeDtypeStruct((W, V), F32),
            jax.ShapeDtypeStruct((1, V), F32),
        ),
        in_specs=[pl.BlockSpec(memory_space=pltpu.VMEM)] * 3,
        out_specs=(pl.BlockSpec(memory_space=pl.ANY),) * 4,
        scratch_shapes=[
            pltpu.VMEM((H, W), F32), pltpu.VMEM((W, V), F32), dma((5,)),
        ],
        compiler_params=pltpu.CompilerParams(vmem_limit_bytes=16 * 1024 * 1024),
    )(logits, packed, gr)
    return logits.reshape(R), gs.T, gvo, gr.reshape(V)


def solution(mesh):
    return jax.shard_map(
        shards,
        mesh=mesh,
        in_specs=(P("seq", "tp"), P("tp", None), P("tp", None), P(), P("seq"), P("seq")),
        out_specs=(P("seq"), P("tp", None), P("tp", None), P()),
        check_vma=False,
    )
```

```python
import functools
import math

import jax
import jax.numpy as jnp
import numpy as np
from jax import lax
from jax.experimental import pallas as pl
from jax.experimental.pallas import tpu as pltpu
from jax.sharding import PartitionSpec as P

NEGATIVE = -1e30
POSITIVE = 1e30
MESH = pl.DeviceIdType.MESH
F32 = jnp.float32
BF16 = jnp.bfloat16


def tables(tp_count, head_count):
    group = head_count // tp_count
    pack = 16 // group
    back_s = np.zeros((pack, head_count, tp_count, 16), np.float32)
    for g in range(tp_count):
        for h in range(group):
            for q in range(pack):
                back_s[q, g * group + h, g, q * group + h] = 1
    return back_s.reshape(pack, head_count, tp_count * 16)


def picks(g, group, size, gv, width, scores_at):
    row = lax.broadcasted_iota(jnp.int32, (8 + gv, 1), 0)
    inner = jnp.maximum(row - 8, 0)
    column = jnp.where(
        row < 8,
        scores_at + g * group + lax.rem(row, group),
        (g * group + lax.rem(inner, group)) * size + lax.div(inner, group),
    )
    return (column == lax.broadcasted_iota(jnp.int32, (8 + gv, width), 1)).astype(F32)


def dot_nt(a, b):
    return lax.dot_general(a, b, (((1,), (1,)), ((), ())), preferred_element_type=F32)


def kernel(dims, *refs):
    tp, seq, R, W, H, V, group, gv, nl, nr, rows, cut, window, sizes = dims
    chunks = len(sizes)
    starts = [sum(sizes[:j]) for j in range(chunks)]
    hbm, (logit_ref, afin, gr_ref) = refs[:7], refs[7:10]
    held, load_sem = refs[10:17], refs[17]
    part, recv_a, sum_x, recv_x = (refs[18 + k * chunks : 18 + (k + 1) * chunks] for k in range(4))
    (
        fwd, lgt, bwd, rsum, rdo, coty, cots, gy, ysend, yrecv, zown, zsend, zrecv,
    ) = refs[18 + 4 * chunks : 31 + 4 * chunks]
    (
        a_send, a_recv, x_send, x_recv, f_send, f_recv, l_send, l_recv, b_send, b_recv, s_send, s_recv,
        r_send, r_recv, c_send, c_recv, d_send, d_recv, y_send, y_recv, z_send, z_recv, g_send, g_recv, h_send, h_recv,
    ) = refs[31 + 4 * chunks :]
    tokens_ref, score_ref, value_ref, readout_ref, doc_ref, label_ref, backs_ref = held
    K = gv // 8
    me_t = lax.axis_index("tp")
    me_s = lax.axis_index("seq")
    tx, tc = lax.div(me_t, 2), lax.rem(me_t, 2)
    sz, sy = lax.div(me_s, 2), lax.rem(me_s, 2)
    nz = seq // 2
    partner = (me_t, tx * 2 + 1 - tc, (1 - tx) * 2 + tc, (1 - tx) * 2 + 1 - tc)
    sibling, across = {"tp": partner[1]}, {"tp": partner[2]}
    beside = {"seq": sz * 2 + 1 - sy}

    loads = [None] + [pltpu.make_async_copy(hbm[i], held[i], load_sem.at[i]) for i in range(1, len(hbm))]
    pieces = [
        pltpu.make_async_copy(
            hbm[0].at[pl.ds(at, n)], tokens_ref.at[pl.ds(at, n)], load_sem.at[len(hbm) + j]
        )
        for j, (at, n) in enumerate(zip(starts, sizes))
    ]
    for i in (2, 1):
        loads[i].start()
    for piece in pieces:
        piece.start()
    fwd[...] = jnp.zeros_like(fwd)
    bwd[...] = jnp.zeros_like(bwd)
    barrier = pltpu.get_barrier_semaphore()
    for o in range(1, seq):
        pl.semaphore_signal(barrier, inc=1, device_id={"seq": lax.rem(me_s + o, seq)}, device_id_type=MESH)
    for o in range(1, tp):
        pl.semaphore_signal(barrier, inc=1, device_id={"tp": lax.rem(me_t + o, tp)}, device_id_type=MESH)
    for i in range(3, 7):
        loads[i].start()
    pending = []

    def remote(src, dst, send, recv, device):
        return pltpu.make_async_remote_copy(
            src_ref=src, dst_ref=dst, send_sem=send, recv_sem=recv, device_id=device, device_id_type=MESH
        )

    def give(*args):
        copy = remote(*args)
        copy.start()
        pending.append((None, copy))

    def take(dst, send, recv, device):
        remote(dst, dst, send, recv, device).wait_recv()

    def push(axis, o, src, dst, send, recv):
        give(src, dst, send.at[o], recv.at[o], {axis: partner[o] if axis == "tp" else lax.rem(me_s + o, seq)})

    def arrived(axis, o, dst, send, recv):
        take(dst, send.at[o], recv.at[o], {axis: partner[o] if axis == "tp" else lax.rem(me_s + o, seq)})

    def carry(tile, step, send, recv):
        for o in range(window, 0, -1):
            there = (me_s + step * o >= 0) & (me_s + step * o < seq)
            copy = remote(
                tile.at[0], tile.at[o], send.at[o], recv.at[o], {"seq": lax.rem(me_s + step * o + seq, seq)}
            )
            pl.when(there)(copy.start)
            pending.append((there, copy))

    def carried(tile, step, send, recv):
        for o in range(window, 0, -1):
            here = (me_s - step * o >= 0) & (me_s - step * o < seq)
            copy = remote(
                tile.at[o], tile.at[o], send.at[o], recv.at[o], {"seq": lax.rem(me_s + step * o + seq, seq)}
            )
            pl.when(here)(copy.wait_recv)
        return [(tile[o], (me_s - step * o >= 0) & (me_s - step * o < seq)) for o in range(1, window + 1)]

    size = gv // group
    into_all = jnp.concatenate([picks(g, group, size, gv, V + H, V) for g in range(tp)], axis=0).astype(BF16)
    for i in (2, 1):
        loads[i].wait()
    weights = dot_nt(into_all[:, :V], value_ref[...]) + jnp.dot(
        into_all[:, V:], score_ref[...], preferred_element_type=F32
    )
    weights = weights.astype(BF16)

    per = 8 // group

    def relay(j):
        take(recv_a[j].at[0], a_send.at[j, 0], a_recv.at[j, 0], sibling)
        both = part[j][partner[2]] + recv_a[j][0]
        n = sizes[j] // per
        sub = lax.broadcasted_iota(jnp.int32, (8, n), 0)
        line = both[0:8, :n]
        for k in range(1, per):
            line = jnp.where(sub >= k * group, both[0:8, k * n : (k + 1) * n], line)
        for k in range(per):
            sum_x[j][k * gv : (k + 1) * gv] = both[8 : 8 + gv, k * n : (k + 1) * n]
        sum_x[j][per * gv : per * gv + 8] = line
        give(sum_x[j], recv_x[j], x_send.at[j], x_recv.at[j], across)

    for j in range(chunks):
        pieces[j].wait()
        part[j][...] = dot_nt(weights, tokens_ref[starts[j] : starts[j] + sizes[j]]).reshape(tp, 8 + gv, sizes[j])
        if j == 0:
            pl.semaphore_wait(barrier, tp + seq - 2)
        give(part[j].at[partner[3]], recv_a[j].at[0], a_send.at[j, 0], a_recv.at[j, 0], sibling)
        give(part[j].at[partner[1]], recv_a[j].at[1], a_send.at[j, 1], a_recv.at[j, 1], sibling)
        if j > 0:
            relay(j - 1)
    relay(chunks - 1)
    for i in range(3, 7):
        loads[i].wait()
    lane = lax.broadcasted_iota(jnp.int32, (8, R), 1)
    slot = lax.broadcasted_iota(jnp.int32, (8, 128), 1)
    doc = jnp.broadcast_to(doc_ref[...].astype(F32), (8, R))
    labels = label_ref[...].astype(F32)
    own_table = picks(me_t, group, size, gv, V, V)
    w_col = jnp.sum(own_table * readout_ref[...], axis=1, keepdims=True)
    w_k = [w_col[8 + 8 * k : 16 + 8 * k] for k in range(K)]
    def arrive(j):
        take(recv_a[j].at[1], a_send.at[j, 1], a_recv.at[j, 1], sibling)
        take(recv_x[j], x_send.at[j], x_recv.at[j], across)
        n = sizes[j] // per
        sub = lax.broadcasted_iota(jnp.int32, (8, n), 0)
        near = part[j][me_t] + recv_a[j][1]
        line = recv_x[j][per * gv : per * gv + 8]
        lines = []
        for k in range(per):
            own = pltpu.roll(line, 8 - k * group, 0) if k else line
            wide = own
            for m in range(1, per):
                wide = jnp.where(sub >= m * group, pltpu.roll(own, m * group, 0), wide)
            lines.append(wide)
        out = [near[0:8] + jnp.concatenate(lines, axis=1)]
        for k in range(K):
            far = [recv_x[j][m * gv + 8 * k : m * gv + 8 * k + 8] for m in range(per)]
            out.append(near[8 + 8 * k : 16 + 8 * k] + jnp.concatenate(far, axis=1))
        return out

    def pack(columns):
        tile = jnp.zeros((8, 128), F32)
        for i, column in enumerate(columns):
            tile = jnp.where(slot == i, column, tile)
        return tile

    first, last = doc[:, 0:1], doc[:, R - 1 : R]

    def leave(j, score, vals):
        ours = doc[:, starts[j] :] == last
        top = jnp.max(jnp.where(ours, score, NEGATIVE), axis=1, keepdims=True)
        if j > 0:
            m = sizes[j - 1]
            peak_b, *sums_b = [x[:, m - 1 : m] for x in done[j - 1][: K + 2]]
            linked = doc[:, starts[j] - 1 : starts[j]] == last
            top = jnp.where(linked, jnp.maximum(top, peak_b), top)
        w = jnp.where(ours, jnp.exp(jnp.where(ours, score - top, 0.0)), 0.0)
        sums = [jnp.sum(x, axis=1, keepdims=True) for x in [w] + [w * v for v in vals]]
        if j > 0:
            k_b = jnp.where(linked, jnp.exp(jnp.where(linked, peak_b - top, 0.0)), 0.0)
            sums = [s + k_b * b for s, b in zip(sums, sums_b)]
        fwd[0] = pack([top] + sums + [last])
        carry(fwd, 1, f_send, f_recv)

    done = []
    for j in range(chunks):
        score, *vals = arrive(j)
        if j == chunks - 1:
            leave(j, score, vals)
        at, n = starts[j], sizes[j]
        doc_j, lane_j = doc[:, at : at + n], lane[:, :n]
        peak, total, acc = score, jnp.ones_like(score), list(vals)
        d = 1
        while d < n:
            valid = (lane_j >= d) & (pltpu.roll(doc_j, d, 1) == doc_j)
            before = pltpu.roll(peak, d, 1)
            new = jnp.where(valid, jnp.maximum(peak, before), peak)
            ka = jnp.where(valid, jnp.exp(jnp.where(valid, before - new, 0.0)), 0.0)
            kb = jnp.exp(peak - new)
            total = total * kb + pltpu.roll(total, d, 1) * ka
            acc = [a * kb + pltpu.roll(a, d, 1) * ka for a in acc]
            peak = new
            d *= 2
        if j > 0:
            m = sizes[j - 1]
            peak_b, total_b, *acc_b = [x[:, m - 1 : m] for x in done[j - 1][: K + 2]]
            valid = doc_j == doc[:, at - 1 : at]
            new = jnp.where(valid, jnp.maximum(peak, peak_b), peak)
            ka = jnp.where(valid, jnp.exp(jnp.where(valid, peak_b - new, 0.0)), 0.0)
            kb = jnp.exp(peak - new)
            total = total * kb + total_b * ka
            acc = [a * kb + b * ka for a, b in zip(acc, acc_b)]
            peak = new
        done.append([peak, total] + acc + [score] + vals)
    joined = [jnp.concatenate(x, axis=1) for x in zip(*done)]
    peak, total, acc, score, vals = joined[0], joined[1], joined[2 : K + 2], joined[K + 2], joined[K + 3 :]

    tiles = carried(fwd, 1, f_send, f_recv)
    linked = [(t[:, K + 2 : K + 3] == first) & m for t, m in tiles]
    tiles = [t for t, _ in tiles]
    c_peak = jnp.full((8, 1), NEGATIVE, F32)
    for t, m in zip(tiles, linked):
        c_peak = jnp.maximum(c_peak, jnp.where(m, t[:, 0:1], NEGATIVE))
    c_tile = jnp.zeros((8, 128), F32)
    c_any = jnp.zeros((8, 1), F32)
    for t, m in zip(tiles, linked):
        c_tile = c_tile + jnp.where(m, jnp.exp(jnp.where(m, t[:, 0:1] - c_peak, 0.0)), 0.0) * jnp.where(m, t, 0.0)
        c_any = jnp.where(m, 1.0, c_any)
    cont = (doc == first) & (jnp.broadcast_to(c_any, (8, R)) > 0)
    new = jnp.where(cont, jnp.maximum(peak, c_peak), peak)
    kc = jnp.where(cont, jnp.exp(jnp.where(cont, c_peak - new, 0.0)), 0.0)
    kl = jnp.exp(peak - new)
    peak = new
    inverse = 1.0 / (total * kl + c_tile[:, 1:2] * kc)
    pooled = [(a * kl + c_tile[:, 2 + k : 3 + k] * kc) * inverse for k, a in enumerate(acc)]
    squash = [jnp.tanh(p) for p in pooled]
    lp = squash[0] * w_k[0]
    for k in range(1, K):
        lp = lp + squash[k] * w_k[k]
    lgt[me_t] = jnp.sum(lp, axis=0, keepdims=True)
    for o in (3, 2, 1):
        push("tp", o, lgt.at[me_t], lgt.at[me_t], l_send, l_recv)
    slim = [w * (1.0 - q * q) * inverse for w, q in zip(w_k, squash)]
    slim_c = slim[0] * pooled[0]
    for k in range(1, K):
        slim_c = slim_c + slim[k] * pooled[k]

    def over_heads(x):
        out, step = x, group
        while step < 8:
            out = out + pltpu.roll(out, step, 0)
            step *= 2
        return out

    slim_c = over_heads(slim_c)
    weight = jnp.exp(score - peak)
    for o in range(1, tp):
        arrived("tp", o, lgt.at[partner[o]], l_send, l_recv)
    logits = lgt[0]
    for g in range(1, tp):
        logits = logits + lgt[g]
    logit_ref[...] = logits
    slope = (jax.nn.sigmoid(logits) - labels) * (1.0 / math.sqrt(R * seq))
    slope = jnp.broadcast_to(slope, (8, R))
    adj = [x * slope for x in slim]
    adj_c = slim_c * slope
    ours = doc == first
    peak_f = peak[:, 0:1]
    f = jnp.where(ours, jnp.exp(jnp.where(ours, peak_f - peak, 0.0)), 0.0)
    sums = [jnp.sum(x * f, axis=1, keepdims=True) for x in [adj_c] + adj]
    bwd[0] = pack([peak_f] + sums + [first])
    carry(bwd, -1, b_send, b_recv)
    d = 1
    while d < R:
        valid = (lane < R - d) & (pltpu.roll(doc, R - d, 1) == doc)
        f = jnp.where(valid, jnp.exp(jnp.where(valid, peak - pltpu.roll(peak, R - d, 1), 0.0)), 0.0)
        adj_c = adj_c + f * pltpu.roll(adj_c, R - d, 1)
        adj = [a + f * pltpu.roll(a, R - d, 1) for a in adj]
        d *= 2
    tiles = carried(bwd, -1, b_send, b_recv)
    linked = [(t[:, K + 2 : K + 3] == last) & m for t, m in tiles]
    tiles = [t for t, _ in tiles]
    a_peak = jnp.full((8, 1), POSITIVE, F32)
    for t, m in zip(tiles, linked):
        a_peak = jnp.minimum(a_peak, jnp.where(m, t[:, 0:1], POSITIVE))
    a_tile = jnp.zeros((8, 128), F32)
    a_any = jnp.zeros((8, 1), F32)
    for t, m in zip(tiles, linked):
        a_tile = a_tile + jnp.where(m, jnp.exp(jnp.where(m, a_peak - t[:, 0:1], 0.0)), 0.0) * jnp.where(m, t, 0.0)
        a_any = jnp.where(m, 1.0, a_any)
    reach = (doc == last) & (jnp.broadcast_to(a_any, (8, R)) > 0)
    fac = jnp.where(reach, jnp.exp(jnp.where(reach, peak - a_peak, 0.0)), 0.0)
    adj_c = adj_c + fac * a_tile[:, 1:2]
    adj = [a + fac * a_tile[:, 2 + k : 3 + k] for k, a in enumerate(adj)]
    mix = vals[0] * adj[0]
    for k in range(1, K):
        mix = mix + vals[k] * adj[k]
    d_score = weight * (over_heads(mix) - adj_c)
    coty[me_t] = jnp.concatenate([weight * a for a in adj], axis=0).astype(BF16)
    c_across, c_diag = partner[2], partner[3]
    shares = (pl.ds(0, cut), pl.ds(cut, gv - cut))
    for i, part_i in enumerate(shares):
        give(coty.at[me_t, part_i], coty.at[me_t, part_i], c_send.at[1 + i], c_recv.at[1 + i], across)
    give(coty.at[me_t], coty.at[me_t], c_send.at[0], c_recv.at[0], sibling)
    row = lax.broadcasted_iota(jnp.int32, (8, R), 0)
    packs = 16 // group
    Q = R // packs
    lines = []
    for i in range(0, packs, per):
        line = d_score[:, i * Q : (i + 1) * Q]
        for k in range(1, per):
            line = jnp.where(row[:, :Q] >= k * group, d_score[:, (i + k) * Q : (i + k + 1) * Q], line)
        lines.append(line)
    cots[me_t] = jnp.concatenate(lines, axis=0).astype(BF16)
    for o in (3, 2, 1):
        push("tp", o, cots.at[me_t], cots.at[me_t], d_send, d_recv)

    half, cl = W // 2, W // 2 // nl
    parts_c = [n // nr for n in rows]

    def columns_of():
        return [lax.rem(sz + k, nl) for k in range(1, nl + 1)]

    def product(p):
        if p < 2:
            cot = [coty[partner[p]]]
        elif p == 2:
            cot = [coty[c_across, 0:cut], coty[c_diag, 0:cut]]
        else:
            packed = cots[...].reshape(tp * 16, Q)
            lines = [jnp.dot(backs_ref[q], packed, preferred_element_type=F32) for q in range(packs)]
            cot = [coty[c_across, cut:gv], coty[c_diag, cut:gv], jnp.concatenate(lines, axis=1).astype(BF16)]
        spare = rows[p] - sum(c.shape[0] for c in cot)
        if spare:
            cot.append(jnp.zeros((spare, R), BF16))
        cot = jnp.concatenate(cot, axis=0) if len(cot) > 1 else cot[0]
        out = jnp.dot(cot, tokens_ref[...], preferred_element_type=F32)
        n = rows[p]
        for c in range(nl):
            gy[p, 0, c, 0:n] = out[:, c * cl : (c + 1) * cl]
            gy[p, 1, c, 0:n] = out[:, half + c * cl : half + (c + 1) * cl]
        for c in columns_of():
            ysend[p, c, 0:n] = gy[p, 1 - sy, c, 0:n].astype(BF16)
            give(
                ysend.at[p, c, pl.ds(0, n)], yrecv.at[p, c, pl.ds(0, n)],
                y_send.at[p, c], y_recv.at[p, c], beside,
            )

    def lines_of(to, rc):
        return pl.ds(0, rc) if nr == 1 else pl.ds(pl.multiple_of(lax.div(to, nl) * rc, 16), rc)

    def along_z(p):
        n, rc = rows[p], parts_c[p]
        for k, c in enumerate(columns_of(), 1):
            take(yrecv.at[p, c, pl.ds(0, n)], y_send.at[p, c], y_recv.at[p, c], beside)
            both = gy[p, sy, c, 0:n] + yrecv[p, c, 0:n].astype(F32)
            if k == nl:
                zown[p, 0:n] = both
            zsend[p, c, 0:n] = both.astype(BF16)
            for o in range(k, nz, nl):
                to = lax.rem(sz + o, nz)
                give(
                    zsend.at[p, c, lines_of(to, rc)], zrecv.at[p, sz, pl.ds(0, rc)],
                    z_send.at[p, o], z_recv.at[p, o], {"seq": to * 2 + sy},
                )

    def finish(p):
        rc = parts_c[p]
        total_p = zown[p, lines_of(sz, rc)]
        for o in range(1, nz):
            source = lax.rem(sz + nz - o, nz)
            take(
                zrecv.at[p, source, pl.ds(0, rc)], z_send.at[p, o], z_recv.at[p, o],
                {"seq": lax.rem(sz + o, nz) * 2 + sy},
            )
            total_p = total_p + zrecv[p, source, 0:rc].astype(F32)
        afin[p, sy, sz, 0:rc] = total_p.astype(BF16)
        mine = afin.at[p, sy, sz, pl.ds(0, rc)]
        for o in range(1, nz):
            give(mine, mine, g_send.at[p, o], g_recv.at[p, o], {"seq": lax.rem(sz + o, nz) * 2 + sy})
        give(mine, mine, h_send.at[p, 0], h_recv.at[p, 0], beside)
        if p == tp - 1:
            for o in range(1, nz):
                give(mine, mine, h_send.at[p, o], h_recv.at[p, o], {"seq": lax.rem(sz + o, nz) * 2 + 1 - sy})

    def along_y(p):
        rc = parts_c[p]
        for o in range(1, nz):
            line = afin.at[p, sy, lax.rem(sz + nz - o, nz), pl.ds(0, rc)]
            take(line, g_send.at[p, o], g_recv.at[p, o], {"seq": lax.rem(sz + o, nz) * 2 + sy})
            if p < tp - 1:
                give(line, line, h_send.at[p, o], h_recv.at[p, o], beside)

    def readout_out():
        rsum[me_s] = pack([jnp.sum(q * slope, axis=1, keepdims=True) for q in squash])
        for o in range(1, seq):
            push("seq", o, rsum.at[me_s], rsum.at[me_s], s_send, s_recv)

    def readout_across():
        for o in range(1, seq):
            arrived("seq", o, rsum.at[lax.rem(me_s + seq - o, seq)], s_send, s_recv)
        r_tile = rsum[0]
        for j in range(1, seq):
            r_tile = r_tile + rsum[j]
        rdo[me_t] = r_tile
        for o in (3, 2, 1):
            push("tp", o, rdo.at[me_t], rdo.at[me_t], r_send, r_recv)

    def readout_done():
        for o in range(1, tp):
            arrived("tp", o, rdo.at[partner[o]], r_send, r_recv)
        r_all = jnp.zeros((1, V), F32)
        for g in range(tp):
            tile, table = rdo[g], picks(g, group, size, gv, V, V)
            for k in range(K):
                r_all = r_all + jnp.sum(
                    table[8 + 8 * k : 16 + 8 * k] * tile[:, k : k + 1], axis=0, keepdims=True
                )
        gr_ref[...] = r_all

    def across_in(i):
        line = coty.at[c_across, shares[i]]
        take(line, c_send.at[1 + i], c_recv.at[1 + i], across)
        give(line, line, c_send.at[3 + i], c_recv.at[3 + i], sibling)

    def diagonal_in(i):
        take(coty.at[c_diag, shares[i]], c_send.at[3 + i], c_recv.at[3 + i], sibling)
        if i == 1:
            for o in range(1, tp):
                arrived("tp", o, cots.at[partner[o]], d_send, d_recv)

    def sibling_in():
        take(coty.at[partner[1]], c_send.at[0], c_recv.at[0], sibling)

    product(0)
    readout_out()
    sibling_in()
    product(1)
    along_z(0)
    across_in(0)
    across_in(1)
    along_z(1)
    diagonal_in(0)
    product(2)
    finish(0)
    diagonal_in(1)
    product(3)
    finish(1)
    along_z(2)
    along_z(3)
    readout_across()
    along_y(0)
    finish(2)
    along_y(1)
    finish(3)
    readout_done()
    along_y(2)
    along_y(3)
    for p in range(tp):
        for o in range(nz):
            line = afin.at[p, 1 - sy, lax.rem(sz + nz - o, nz), pl.ds(0, parts_c[p])]
            take(line, h_send.at[p, o], h_recv.at[p, o], beside)
    for when, copy in pending:
        if when is None:
            copy.wait_send()
        else:
            pl.when(when)(copy.wait_send)


def unpack(dims, logit_in, afin, gr_in, logit_ref, gs_ref, gv_ref, gr_ref, gs_held, gv_held, sem):
    tp, H, V, gv, cut, half, cl, nl, nr, parts_c = dims
    me_t = lax.axis_index("tp")
    tx, tc = lax.div(me_t, 2), lax.rem(me_t, 2)
    moves = [
        pltpu.make_async_copy(logit_in, logit_ref, sem.at[0]),
        pltpu.make_async_copy(gr_in, gr_ref, sem.at[1]),
    ]
    for move in moves:
        move.start()
    size = V // H
    group = H // tp
    row = lax.broadcasted_iota(jnp.int32, (V, 1), 0)
    p, inner = lax.div(row, gv), lax.rem(row, gv)
    g = lax.rem(tx + lax.div(p, 2), 2) * 2 + lax.rem(tc + lax.rem(p, 2), 2)
    target = (g * group + lax.rem(inner, group)) * size + lax.div(inner, group)
    order = (target == lax.broadcasted_iota(jnp.int32, (V, V), 1)).astype(F32).astype(BF16)
    for y in range(2):
        for c in range(nl):
            at = y * half + c * cl
            own, beside, others, rest = (
                jnp.concatenate([afin[p, y, r * nl + c, 0 : parts_c[p]] for r in range(nr)], axis=0)
                for p in range(tp)
            )
            left = gv - cut
            stack = jnp.concatenate(
                [own[:gv], beside[:gv], others[:cut], rest[:left], others[cut : 2 * cut], rest[left : 2 * left]], axis=0
            )
            gs_held[:, at : at + cl] = rest[2 * left : 2 * left + H].astype(F32)
            gv_held[at : at + cl, :] = lax.dot_general(
                stack, order, (((0,), (0,)), ((), ())), preferred_element_type=F32
            )
        rows_y = pl.ds(y * half, half)
        moves.append(pltpu.make_async_copy(gv_held.at[rows_y], gv_ref.at[rows_y], sem.at[2 + y]))
        moves[-1].start()
    moves.append(pltpu.make_async_copy(gs_held, gs_ref, sem.at[4]))
    moves[-1].start()
    for move in moves:
        move.wait()


def shards(tokens, score_weight, value_weight, readout, doc_ids, labels):
    tp = lax.axis_size("tp")
    seq = lax.axis_size("seq")
    R, W = tokens.shape
    H = score_weight.shape[1]
    V = value_weight.shape[1]
    group = H // tp
    gv = V // tp
    nz = seq // 2
    nl = min(nz, W // 256)
    nr = nz // nl
    unit = 16 * nr
    cut = gv * 3 // 4
    rows = tuple(-(-n // unit) * unit for n in (gv, gv, 2 * cut, 2 * (gv - cut) + H))
    last = max(rows)
    half, cl, rc = W // 2, W // 2 // nl, last // nr
    back_s = tables(tp, H)
    longest = {8192: 4096, 65536: 16384}.get(R * seq, R * seq)
    window = min(seq - 1, -(-longest // R))
    sizes = (R // 2, R // 2)
    chunks = len(sizes)
    dims = (tp, seq, R, W, H, V, group, gv, nl, nr, rows, cut, window, sizes)
    dma = pltpu.SemaphoreType.DMA
    operands = (
        tokens, score_weight.T, value_weight, readout.reshape(1, V),
        doc_ids.reshape(1, R), labels.reshape(1, R), jnp.asarray(back_s, BF16),
    )
    packed_rows = 8 // group * gv + 8
    scratch = [pltpu.VMEM(x.shape, x.dtype) for x in operands] + [dma((len(operands) + chunks,))]
    scratch += [pltpu.VMEM((tp, 8 + gv, n), F32) for n in sizes]
    scratch += [pltpu.VMEM((2, 8 + gv, n), F32) for n in sizes]
    scratch += [pltpu.VMEM((packed_rows, n * group // 8), F32) for n in sizes] * 2
    scratch += [
        pltpu.VMEM((window + 1, 8, 128), F32),
        pltpu.VMEM((tp, 1, R), F32),
        pltpu.VMEM((window + 1, 8, 128), F32),
        pltpu.VMEM((seq, 8, 128), F32),
        pltpu.VMEM((tp, 8, 128), F32),
        pltpu.VMEM((tp, gv, R), BF16),
        pltpu.VMEM((tp, 16, R * group // 16), BF16),
        pltpu.VMEM((tp, 2, nl, last, cl), F32),
        pltpu.VMEM((tp, nl, last, cl), BF16),
        pltpu.VMEM((tp, nl, last, cl), BF16),
        pltpu.VMEM((tp, last, cl), F32),
        pltpu.VMEM((tp, nl, last, cl), BF16),
        pltpu.VMEM((tp, nz, rc, cl), BF16),
    ]
    for n in (
        (chunks, 2), (chunks,), (window + 1,), (tp,), (window + 1,), (seq,),
        (tp,), (5,), (tp,), (tp, nl), (tp, nz), (tp, nz), (tp, nz),
    ):
        scratch += [dma(n), dma(n)]
    logits, packed, gr = pl.pallas_call(
        functools.partial(kernel, dims),
        out_shape=(
            jax.ShapeDtypeStruct((1, R), F32),
            jax.ShapeDtypeStruct((tp, 2, nz, rc, cl), BF16),
            jax.ShapeDtypeStruct((1, V), F32),
        ),
        in_specs=[pl.BlockSpec(memory_space=pltpu.HBM)] * len(operands),
        out_specs=(pl.BlockSpec(memory_space=pltpu.VMEM),) * 3,
        scratch_shapes=scratch,
        compiler_params=pltpu.CompilerParams(
            collective_id=0, has_side_effects=True, vmem_limit_bytes=40 * 1024 * 1024
        ),
    )(*(pltpu.with_memory_space_constraint(x, pltpu.HBM) for x in operands))
    parts_c = tuple(n // nr for n in rows)
    logits, gs, gvo, gr = pl.pallas_call(
        functools.partial(unpack, (tp, H, V, gv, cut, half, cl, nl, nr, parts_c)),
        out_shape=(
            jax.ShapeDtypeStruct((1, R), F32),
            jax.ShapeDtypeStruct((H, W), F32),
            jax.ShapeDtypeStruct((W, V), F32),
            jax.ShapeDtypeStruct((1, V), F32),
        ),
        in_specs=[pl.BlockSpec(memory_space=pltpu.VMEM)] * 3,
        out_specs=(pl.BlockSpec(memory_space=pl.ANY),) * 4,
        scratch_shapes=[
            pltpu.VMEM((H, W), F32), pltpu.VMEM((W, V), F32), dma((5,)),
        ],
        compiler_params=pltpu.CompilerParams(vmem_limit_bytes=16 * 1024 * 1024),
    )(logits, packed, gr)
    return logits.reshape(R), gs.T, gvo, gr.reshape(V)


def solution(mesh):
    return jax.shard_map(
        shards,
        mesh=mesh,
        in_specs=(P("seq", "tp"), P("tp", None), P("tp", None), P(), P("seq"), P("seq")),
        out_specs=(P("seq"), P("tp", None), P("tp", None), P()),
        check_vma=False,
    )
```

```python
import functools
import math

import jax
import jax.numpy as jnp
import numpy as np
from jax import lax
from jax.experimental import pallas as pl
from jax.experimental.pallas import tpu as pltpu
from jax.sharding import PartitionSpec as P

NEGATIVE = -1e30
POSITIVE = 1e30
MESH = pl.DeviceIdType.MESH
F32 = jnp.float32
BF16 = jnp.bfloat16


def tables(tp_count, head_count):
    group = head_count // tp_count
    pack = 16 // group
    back_s = np.zeros((pack, head_count, tp_count, 16), np.float32)
    for g in range(tp_count):
        for h in range(group):
            for q in range(pack):
                back_s[q, g * group + h, g, q * group + h] = 1
    return back_s.reshape(pack, head_count, tp_count * 16)


def picks(g, group, size, gv, width, scores_at):
    row = lax.broadcasted_iota(jnp.int32, (8 + gv, 1), 0)
    inner = jnp.maximum(row - 8, 0)
    column = jnp.where(
        row < 8,
        scores_at + g * group + lax.rem(row, group),
        (g * group + lax.rem(inner, group)) * size + lax.div(inner, group),
    )
    return (column == lax.broadcasted_iota(jnp.int32, (8 + gv, width), 1)).astype(F32)


def dot_nt(a, b):
    return lax.dot_general(a, b, (((1,), (1,)), ((), ())), preferred_element_type=F32)


def kernel(dims, *refs):
    tp, seq, R, W, H, V, group, gv, nl, nr, rows, cut, window, sizes = dims
    chunks = len(sizes)
    starts = [sum(sizes[:j]) for j in range(chunks)]
    hbm, (logit_ref, afin, gr_ref) = refs[:7], refs[7:10]
    held, load_sem = refs[10:17], refs[17]
    part, recv_a, sum_x, recv_x = (refs[18 + k * chunks : 18 + (k + 1) * chunks] for k in range(4))
    (
        fwd, lgt, bwd, rsum, rdo, coty, cots, gy, ysend, yrecv, zown, zsend, zrecv,
    ) = refs[18 + 4 * chunks : 31 + 4 * chunks]
    (
        a_send, a_recv, x_send, x_recv, f_send, f_recv, l_send, l_recv, b_send, b_recv, s_send, s_recv,
        r_send, r_recv, c_send, c_recv, d_send, d_recv, y_send, y_recv, z_send, z_recv, g_send, g_recv, h_send, h_recv,
    ) = refs[31 + 4 * chunks :]
    tokens_ref, score_ref, value_ref, readout_ref, doc_ref, label_ref, backs_ref = held
    K = gv // 8
    me_t = lax.axis_index("tp")
    me_s = lax.axis_index("seq")
    tx, tc = lax.div(me_t, 2), lax.rem(me_t, 2)
    sz, sy = lax.div(me_s, 2), lax.rem(me_s, 2)
    nz = seq // 2
    partner = (me_t, tx * 2 + 1 - tc, (1 - tx) * 2 + tc, (1 - tx) * 2 + 1 - tc)
    sibling, across = {"tp": partner[1]}, {"tp": partner[2]}
    beside = {"seq": sz * 2 + 1 - sy}

    loads = [None] + [pltpu.make_async_copy(hbm[i], held[i], load_sem.at[i]) for i in range(1, len(hbm))]
    pieces = [
        pltpu.make_async_copy(
            hbm[0].at[pl.ds(at, n)], tokens_ref.at[pl.ds(at, n)], load_sem.at[len(hbm) + j]
        )
        for j, (at, n) in enumerate(zip(starts, sizes))
    ]
    for i in (2, 1):
        loads[i].start()
    for piece in pieces:
        piece.start()
    fwd[...] = jnp.zeros_like(fwd)
    bwd[...] = jnp.zeros_like(bwd)
    barrier = pltpu.get_barrier_semaphore()
    for o in range(1, seq):
        pl.semaphore_signal(barrier, inc=1, device_id={"seq": lax.rem(me_s + o, seq)}, device_id_type=MESH)
    for o in range(1, tp):
        pl.semaphore_signal(barrier, inc=1, device_id={"tp": lax.rem(me_t + o, tp)}, device_id_type=MESH)
    for i in range(3, 7):
        loads[i].start()
    pending = []

    def remote(src, dst, send, recv, device):
        return pltpu.make_async_remote_copy(
            src_ref=src, dst_ref=dst, send_sem=send, recv_sem=recv, device_id=device, device_id_type=MESH
        )

    def give(*args):
        copy = remote(*args)
        copy.start()
        pending.append((None, copy))

    def take(dst, send, recv, device):
        remote(dst, dst, send, recv, device).wait_recv()

    def push(axis, o, src, dst, send, recv):
        give(src, dst, send.at[o], recv.at[o], {axis: partner[o] if axis == "tp" else lax.rem(me_s + o, seq)})

    def arrived(axis, o, dst, send, recv):
        take(dst, send.at[o], recv.at[o], {axis: partner[o] if axis == "tp" else lax.rem(me_s + o, seq)})

    def carry(tile, step, send, recv):
        for o in range(window, 0, -1):
            there = (me_s + step * o >= 0) & (me_s + step * o < seq)
            copy = remote(
                tile.at[0], tile.at[o], send.at[o], recv.at[o], {"seq": lax.rem(me_s + step * o + seq, seq)}
            )
            pl.when(there)(copy.start)
            pending.append((there, copy))

    def carried(tile, step, send, recv):
        for o in range(window, 0, -1):
            here = (me_s - step * o >= 0) & (me_s - step * o < seq)
            copy = remote(
                tile.at[o], tile.at[o], send.at[o], recv.at[o], {"seq": lax.rem(me_s + step * o + seq, seq)}
            )
            pl.when(here)(copy.wait_recv)
        return [(tile[o], (me_s - step * o >= 0) & (me_s - step * o < seq)) for o in range(1, window + 1)]

    size = gv // group
    into_all = jnp.concatenate([picks(g, group, size, gv, V + H, V) for g in range(tp)], axis=0).astype(BF16)
    for i in (2, 1):
        loads[i].wait()
    weights = dot_nt(into_all[:, :V], value_ref[...]) + jnp.dot(
        into_all[:, V:], score_ref[...], preferred_element_type=F32
    )
    weights = weights.astype(BF16)

    per = 8 // group

    def relay(j):
        take(recv_a[j].at[0], a_send.at[j, 0], a_recv.at[j, 0], sibling)
        both = part[j][partner[2]] + recv_a[j][0]
        n = sizes[j] // per
        sub = lax.broadcasted_iota(jnp.int32, (8, n), 0)
        line = both[0:8, :n]
        for k in range(1, per):
            line = jnp.where(sub >= k * group, both[0:8, k * n : (k + 1) * n], line)
        for k in range(per):
            sum_x[j][k * gv : (k + 1) * gv] = both[8 : 8 + gv, k * n : (k + 1) * n]
        sum_x[j][per * gv : per * gv + 8] = line
        give(sum_x[j], recv_x[j], x_send.at[j], x_recv.at[j], across)

    for j in range(chunks):
        pieces[j].wait()
        part[j][...] = dot_nt(weights, tokens_ref[starts[j] : starts[j] + sizes[j]]).reshape(tp, 8 + gv, sizes[j])
        if j == 0:
            pl.semaphore_wait(barrier, tp + seq - 2)
        give(part[j].at[partner[3]], recv_a[j].at[0], a_send.at[j, 0], a_recv.at[j, 0], sibling)
        give(part[j].at[partner[1]], recv_a[j].at[1], a_send.at[j, 1], a_recv.at[j, 1], sibling)
        if j > 0:
            relay(j - 1)
    relay(chunks - 1)
    for i in range(3, 7):
        loads[i].wait()
    lane = lax.broadcasted_iota(jnp.int32, (8, R), 1)
    slot = lax.broadcasted_iota(jnp.int32, (8, 128), 1)
    doc = jnp.broadcast_to(doc_ref[...].astype(F32), (8, R))
    labels = label_ref[...].astype(F32)
    own_table = picks(me_t, group, size, gv, V, V)
    w_col = jnp.sum(own_table * readout_ref[...], axis=1, keepdims=True)
    w_k = [w_col[8 + 8 * k : 16 + 8 * k] for k in range(K)]
    def arrive(j):
        take(recv_a[j].at[1], a_send.at[j, 1], a_recv.at[j, 1], sibling)
        take(recv_x[j], x_send.at[j], x_recv.at[j], across)
        n = sizes[j] // per
        sub = lax.broadcasted_iota(jnp.int32, (8, n), 0)
        near = part[j][me_t] + recv_a[j][1]
        line = recv_x[j][per * gv : per * gv + 8]
        lines = []
        for k in range(per):
            own = pltpu.roll(line, 8 - k * group, 0) if k else line
            wide = own
            for m in range(1, per):
                wide = jnp.where(sub >= m * group, pltpu.roll(own, m * group, 0), wide)
            lines.append(wide)
        out = [near[0:8] + jnp.concatenate(lines, axis=1)]
        for k in range(K):
            far = [recv_x[j][m * gv + 8 * k : m * gv + 8 * k + 8] for m in range(per)]
            out.append(near[8 + 8 * k : 16 + 8 * k] + jnp.concatenate(far, axis=1))
        return out

    def pack(columns):
        tile = jnp.zeros((8, 128), F32)
        for i, column in enumerate(columns):
            tile = jnp.where(slot == i, column, tile)
        return tile

    first, last = doc[:, 0:1], doc[:, R - 1 : R]

    def leave(j, score, vals):
        ours = doc[:, starts[j] :] == last
        top = jnp.max(jnp.where(ours, score, NEGATIVE), axis=1, keepdims=True)
        if j > 0:
            m = sizes[j - 1]
            peak_b, *sums_b = [x[:, m - 1 : m] for x in done[j - 1][: K + 2]]
            linked = doc[:, starts[j] - 1 : starts[j]] == last
            top = jnp.where(linked, jnp.maximum(top, peak_b), top)
        w = jnp.where(ours, jnp.exp(jnp.where(ours, score - top, 0.0)), 0.0)
        sums = [jnp.sum(x, axis=1, keepdims=True) for x in [w] + [w * v for v in vals]]
        if j > 0:
            k_b = jnp.where(linked, jnp.exp(jnp.where(linked, peak_b - top, 0.0)), 0.0)
            sums = [s + k_b * b for s, b in zip(sums, sums_b)]
        fwd[0] = pack([top] + sums + [last])
        carry(fwd, 1, f_send, f_recv)

    done = []
    for j in range(chunks):
        score, *vals = arrive(j)
        if j == chunks - 1:
            leave(j, score, vals)
        at, n = starts[j], sizes[j]
        doc_j, lane_j = doc[:, at : at + n], lane[:, :n]
        peak, total, acc = score, jnp.ones_like(score), list(vals)
        d = 1
        while d < n:
            valid = (lane_j >= d) & (pltpu.roll(doc_j, d, 1) == doc_j)
            before = pltpu.roll(peak, d, 1)
            new = jnp.where(valid, jnp.maximum(peak, before), peak)
            ka = jnp.where(valid, jnp.exp(jnp.where(valid, before - new, 0.0)), 0.0)
            kb = jnp.exp(peak - new)
            total = total * kb + pltpu.roll(total, d, 1) * ka
            acc = [a * kb + pltpu.roll(a, d, 1) * ka for a in acc]
            peak = new
            d *= 2
        if j > 0:
            m = sizes[j - 1]
            peak_b, total_b, *acc_b = [x[:, m - 1 : m] for x in done[j - 1][: K + 2]]
            valid = doc_j == doc[:, at - 1 : at]
            new = jnp.where(valid, jnp.maximum(peak, peak_b), peak)
            ka = jnp.where(valid, jnp.exp(jnp.where(valid, peak_b - new, 0.0)), 0.0)
            kb = jnp.exp(peak - new)
            total = total * kb + total_b * ka
            acc = [a * kb + b * ka for a, b in zip(acc, acc_b)]
            peak = new
        done.append([peak, total] + acc + [score] + vals)
    joined = [jnp.concatenate(x, axis=1) for x in zip(*done)]
    peak, total, acc, score, vals = joined[0], joined[1], joined[2 : K + 2], joined[K + 2], joined[K + 3 :]

    tiles = carried(fwd, 1, f_send, f_recv)
    linked = [(t[:, K + 2 : K + 3] == first) & m for t, m in tiles]
    tiles = [t for t, _ in tiles]
    c_peak = jnp.full((8, 1), NEGATIVE, F32)
    for t, m in zip(tiles, linked):
        c_peak = jnp.maximum(c_peak, jnp.where(m, t[:, 0:1], NEGATIVE))
    c_tile = jnp.zeros((8, 128), F32)
    c_any = jnp.zeros((8, 1), F32)
    for t, m in zip(tiles, linked):
        c_tile = c_tile + jnp.where(m, jnp.exp(jnp.where(m, t[:, 0:1] - c_peak, 0.0)), 0.0) * jnp.where(m, t, 0.0)
        c_any = jnp.where(m, 1.0, c_any)
    cont = (doc == first) & (jnp.broadcast_to(c_any, (8, R)) > 0)
    new = jnp.where(cont, jnp.maximum(peak, c_peak), peak)
    kc = jnp.where(cont, jnp.exp(jnp.where(cont, c_peak - new, 0.0)), 0.0)
    kl = jnp.exp(peak - new)
    peak = new
    inverse = 1.0 / (total * kl + c_tile[:, 1:2] * kc)
    pooled = [(a * kl + c_tile[:, 2 + k : 3 + k] * kc) * inverse for k, a in enumerate(acc)]
    squash = [jnp.tanh(p) for p in pooled]
    lp = squash[0] * w_k[0]
    for k in range(1, K):
        lp = lp + squash[k] * w_k[k]
    lgt[me_t] = jnp.sum(lp, axis=0, keepdims=True)
    for o in (3, 2, 1):
        push("tp", o, lgt.at[me_t], lgt.at[me_t], l_send, l_recv)
    slim = [w * (1.0 - q * q) * inverse for w, q in zip(w_k, squash)]
    slim_c = slim[0] * pooled[0]
    for k in range(1, K):
        slim_c = slim_c + slim[k] * pooled[k]

    def over_heads(x):
        out, step = x, group
        while step < 8:
            out = out + pltpu.roll(out, step, 0)
            step *= 2
        return out

    slim_c = over_heads(slim_c)
    weight = jnp.exp(score - peak)
    for o in range(1, tp):
        arrived("tp", o, lgt.at[partner[o]], l_send, l_recv)
    logits = lgt[0]
    for g in range(1, tp):
        logits = logits + lgt[g]
    logit_ref[...] = logits
    slope = (jax.nn.sigmoid(logits) - labels) * (1.0 / math.sqrt(R * seq))
    slope = jnp.broadcast_to(slope, (8, R))
    adj = [x * slope for x in slim]
    adj_c = slim_c * slope
    ours = doc == first
    peak_f = peak[:, 0:1]
    f = jnp.where(ours, jnp.exp(jnp.where(ours, peak_f - peak, 0.0)), 0.0)
    sums = [jnp.sum(x * f, axis=1, keepdims=True) for x in [adj_c] + adj]
    bwd[0] = pack([peak_f] + sums + [first])
    carry(bwd, -1, b_send, b_recv)
    d = 1
    while d < R:
        valid = (lane < R - d) & (pltpu.roll(doc, R - d, 1) == doc)
        f = jnp.where(valid, jnp.exp(jnp.where(valid, peak - pltpu.roll(peak, R - d, 1), 0.0)), 0.0)
        adj_c = adj_c + f * pltpu.roll(adj_c, R - d, 1)
        adj = [a + f * pltpu.roll(a, R - d, 1) for a in adj]
        d *= 2
    tiles = carried(bwd, -1, b_send, b_recv)
    linked = [(t[:, K + 2 : K + 3] == last) & m for t, m in tiles]
    tiles = [t for t, _ in tiles]
    a_peak = jnp.full((8, 1), POSITIVE, F32)
    for t, m in zip(tiles, linked):
        a_peak = jnp.minimum(a_peak, jnp.where(m, t[:, 0:1], POSITIVE))
    a_tile = jnp.zeros((8, 128), F32)
    a_any = jnp.zeros((8, 1), F32)
    for t, m in zip(tiles, linked):
        a_tile = a_tile + jnp.where(m, jnp.exp(jnp.where(m, a_peak - t[:, 0:1], 0.0)), 0.0) * jnp.where(m, t, 0.0)
        a_any = jnp.where(m, 1.0, a_any)
    reach = (doc == last) & (jnp.broadcast_to(a_any, (8, R)) > 0)
    fac = jnp.where(reach, jnp.exp(jnp.where(reach, peak - a_peak, 0.0)), 0.0)
    adj_c = adj_c + fac * a_tile[:, 1:2]
    adj = [a + fac * a_tile[:, 2 + k : 3 + k] for k, a in enumerate(adj)]
    mix = vals[0] * adj[0]
    for k in range(1, K):
        mix = mix + vals[k] * adj[k]
    d_score = weight * (over_heads(mix) - adj_c)
    coty[me_t] = jnp.concatenate([weight * a for a in adj], axis=0).astype(BF16)
    c_across, c_diag = partner[2], partner[3]
    shares = (pl.ds(0, cut), pl.ds(cut, gv - cut))
    for i, part_i in enumerate(shares):
        give(coty.at[me_t, part_i], coty.at[me_t, part_i], c_send.at[1 + i], c_recv.at[1 + i], across)
    give(coty.at[me_t], coty.at[me_t], c_send.at[0], c_recv.at[0], sibling)
    row = lax.broadcasted_iota(jnp.int32, (8, R), 0)
    packs = 16 // group
    Q = R // packs
    lines = []
    for i in range(0, packs, per):
        line = d_score[:, i * Q : (i + 1) * Q]
        for k in range(1, per):
            line = jnp.where(row[:, :Q] >= k * group, d_score[:, (i + k) * Q : (i + k + 1) * Q], line)
        lines.append(line)
    cots[me_t] = jnp.concatenate(lines, axis=0).astype(BF16)
    for o in (3, 2, 1):
        push("tp", o, cots.at[me_t], cots.at[me_t], d_send, d_recv)

    half, cl = W // 2, W // 2 // nl
    parts_c = [n // nr for n in rows]

    def columns_of():
        return [lax.rem(sz + k, nl) for k in range(1, nl + 1)]

    def product(p):
        if p < 2:
            cot = [coty[partner[p]]]
        elif p == 2:
            cot = [coty[c_across, 0:cut], coty[c_diag, 0:cut]]
        else:
            packed = cots[...].reshape(tp * 16, Q)
            lines = [jnp.dot(backs_ref[q], packed, preferred_element_type=F32) for q in range(packs)]
            cot = [coty[c_across, cut:gv], coty[c_diag, cut:gv], jnp.concatenate(lines, axis=1).astype(BF16)]
        spare = rows[p] - sum(c.shape[0] for c in cot)
        if spare:
            cot.append(jnp.zeros((spare, R), BF16))
        cot = jnp.concatenate(cot, axis=0) if len(cot) > 1 else cot[0]
        out = jnp.dot(cot, tokens_ref[...], preferred_element_type=F32)
        n = rows[p]
        for c in range(nl):
            gy[p, 0, c, 0:n] = out[:, c * cl : (c + 1) * cl]
            gy[p, 1, c, 0:n] = out[:, half + c * cl : half + (c + 1) * cl]
        for c in columns_of():
            ysend[p, c, 0:n] = gy[p, 1 - sy, c, 0:n].astype(BF16)
            give(
                ysend.at[p, c, pl.ds(0, n)], yrecv.at[p, c, pl.ds(0, n)],
                y_send.at[p, c], y_recv.at[p, c], beside,
            )

    def lines_of(to, rc):
        return pl.ds(0, rc) if nr == 1 else pl.ds(pl.multiple_of(lax.div(to, nl) * rc, 16), rc)

    def along_z(p):
        n, rc = rows[p], parts_c[p]
        for k, c in enumerate(columns_of(), 1):
            take(yrecv.at[p, c, pl.ds(0, n)], y_send.at[p, c], y_recv.at[p, c], beside)
            both = gy[p, sy, c, 0:n] + yrecv[p, c, 0:n].astype(F32)
            if k == nl:
                zown[p, 0:n] = both
            zsend[p, c, 0:n] = both.astype(BF16)
            for o in range(k, nz, nl):
                to = lax.rem(sz + o, nz)
                give(
                    zsend.at[p, c, lines_of(to, rc)], zrecv.at[p, sz, pl.ds(0, rc)],
                    z_send.at[p, o], z_recv.at[p, o], {"seq": to * 2 + sy},
                )

    def finish(p):
        rc = parts_c[p]
        total_p = zown[p, lines_of(sz, rc)]
        for o in range(1, nz):
            source = lax.rem(sz + nz - o, nz)
            take(
                zrecv.at[p, source, pl.ds(0, rc)], z_send.at[p, o], z_recv.at[p, o],
                {"seq": lax.rem(sz + o, nz) * 2 + sy},
            )
            total_p = total_p + zrecv[p, source, 0:rc].astype(F32)
        afin[p, sy, sz, 0:rc] = total_p.astype(BF16)
        mine = afin.at[p, sy, sz, pl.ds(0, rc)]
        for o in range(1, nz):
            give(mine, mine, g_send.at[p, o], g_recv.at[p, o], {"seq": lax.rem(sz + o, nz) * 2 + sy})
        give(mine, mine, h_send.at[p, 0], h_recv.at[p, 0], beside)
        if p == tp - 1:
            for o in range(1, nz):
                give(mine, mine, h_send.at[p, o], h_recv.at[p, o], {"seq": lax.rem(sz + o, nz) * 2 + 1 - sy})

    def along_y(p):
        rc = parts_c[p]
        for o in range(1, nz):
            line = afin.at[p, sy, lax.rem(sz + nz - o, nz), pl.ds(0, rc)]
            take(line, g_send.at[p, o], g_recv.at[p, o], {"seq": lax.rem(sz + o, nz) * 2 + sy})
            if p < tp - 1:
                give(line, line, h_send.at[p, o], h_recv.at[p, o], beside)

    def readout_out():
        rsum[me_s] = pack([jnp.sum(q * slope, axis=1, keepdims=True) for q in squash])
        for o in range(1, seq):
            push("seq", o, rsum.at[me_s], rsum.at[me_s], s_send, s_recv)

    def readout_across():
        for o in range(1, seq):
            arrived("seq", o, rsum.at[lax.rem(me_s + seq - o, seq)], s_send, s_recv)
        r_tile = rsum[0]
        for j in range(1, seq):
            r_tile = r_tile + rsum[j]
        rdo[me_t] = r_tile
        for o in (3, 2, 1):
            push("tp", o, rdo.at[me_t], rdo.at[me_t], r_send, r_recv)

    def readout_done():
        for o in range(1, tp):
            arrived("tp", o, rdo.at[partner[o]], r_send, r_recv)
        r_all = jnp.zeros((1, V), F32)
        for g in range(tp):
            tile, table = rdo[g], picks(g, group, size, gv, V, V)
            for k in range(K):
                r_all = r_all + jnp.sum(
                    table[8 + 8 * k : 16 + 8 * k] * tile[:, k : k + 1], axis=0, keepdims=True
                )
        gr_ref[...] = r_all

    def across_in(i):
        line = coty.at[c_across, shares[i]]
        take(line, c_send.at[1 + i], c_recv.at[1 + i], across)
        give(line, line, c_send.at[3 + i], c_recv.at[3 + i], sibling)

    def diagonal_in(i):
        take(coty.at[c_diag, shares[i]], c_send.at[3 + i], c_recv.at[3 + i], sibling)
        if i == 1:
            for o in range(1, tp):
                arrived("tp", o, cots.at[partner[o]], d_send, d_recv)

    def sibling_in():
        take(coty.at[partner[1]], c_send.at[0], c_recv.at[0], sibling)

    product(0)
    readout_out()
    sibling_in()
    product(1)
    along_z(0)
    across_in(0)
    across_in(1)
    along_z(1)
    diagonal_in(0)
    product(2)
    finish(0)
    diagonal_in(1)
    product(3)
    finish(1)
    along_z(2)
    along_z(3)
    readout_across()
    along_y(0)
    finish(2)
    along_y(1)
    finish(3)
    readout_done()
    along_y(2)
    along_y(3)
    for p in range(tp):
        for o in range(nz):
            line = afin.at[p, 1 - sy, lax.rem(sz + nz - o, nz), pl.ds(0, parts_c[p])]
            take(line, h_send.at[p, o], h_recv.at[p, o], beside)
    for when, copy in pending:
        if when is None:
            copy.wait_send()
        else:
            pl.when(when)(copy.wait_send)


def unpack(dims, logit_in, afin, gr_in, logit_ref, gs_ref, gv_ref, gr_ref, gs_held, gv_held, sem):
    tp, H, V, gv, cut, half, cl, nl, nr, parts_c = dims
    me_t = lax.axis_index("tp")
    tx, tc = lax.div(me_t, 2), lax.rem(me_t, 2)
    moves = [
        pltpu.make_async_copy(logit_in, logit_ref, sem.at[0]),
        pltpu.make_async_copy(gr_in, gr_ref, sem.at[1]),
    ]
    for move in moves:
        move.start()
    size = V // H
    group = H // tp
    row = lax.broadcasted_iota(jnp.int32, (V, 1), 0)
    p, inner = lax.div(row, gv), lax.rem(row, gv)
    g = lax.rem(tx + lax.div(p, 2), 2) * 2 + lax.rem(tc + lax.rem(p, 2), 2)
    target = (g * group + lax.rem(inner, group)) * size + lax.div(inner, group)
    order = (target == lax.broadcasted_iota(jnp.int32, (V, V), 1)).astype(F32).astype(BF16)
    for y in range(2):
        for c in range(nl):
            at = y * half + c * cl
            own, beside, others, rest = (
                jnp.concatenate([afin[p, y, r * nl + c, 0 : parts_c[p]] for r in range(nr)], axis=0)
                for p in range(tp)
            )
            left = gv - cut
            stack = jnp.concatenate(
                [own[:gv], beside[:gv], others[:cut], rest[:left], others[cut : 2 * cut], rest[left : 2 * left]], axis=0
            )
            gs_held[:, at : at + cl] = rest[2 * left : 2 * left + H].astype(F32)
            gv_held[at : at + cl, :] = lax.dot_general(
                stack, order, (((0,), (0,)), ((), ())), preferred_element_type=F32
            )
        rows_y = pl.ds(y * half, half)
        moves.append(pltpu.make_async_copy(gv_held.at[rows_y], gv_ref.at[rows_y], sem.at[2 + y]))
        moves[-1].start()
    moves.append(pltpu.make_async_copy(gs_held, gs_ref, sem.at[4]))
    moves[-1].start()
    for move in moves:
        move.wait()


def shards(tokens, score_weight, value_weight, readout, doc_ids, labels):
    tp = lax.axis_size("tp")
    seq = lax.axis_size("seq")
    R, W = tokens.shape
    H = score_weight.shape[1]
    V = value_weight.shape[1]
    group = H // tp
    gv = V // tp
    nz = seq // 2
    nl = min(nz, W // 256)
    nr = nz // nl
    unit = 16 * nr
    cut = gv // 2
    rows = tuple(-(-n // unit) * unit for n in (gv, gv, 2 * cut, 2 * (gv - cut) + H))
    last = max(rows)
    half, cl, rc = W // 2, W // 2 // nl, last // nr
    back_s = tables(tp, H)
    longest = {8192: 4096, 65536: 16384}.get(R * seq, R * seq)
    window = min(seq - 1, -(-longest // R))
    sizes = (R // 2, R // 2)
    chunks = len(sizes)
    dims = (tp, seq, R, W, H, V, group, gv, nl, nr, rows, cut, window, sizes)
    dma = pltpu.SemaphoreType.DMA
    operands = (
        tokens, score_weight.T, value_weight, readout.reshape(1, V),
        doc_ids.reshape(1, R), labels.reshape(1, R), jnp.asarray(back_s, BF16),
    )
    packed_rows = 8 // group * gv + 8
    scratch = [pltpu.VMEM(x.shape, x.dtype) for x in operands] + [dma((len(operands) + chunks,))]
    scratch += [pltpu.VMEM((tp, 8 + gv, n), F32) for n in sizes]
    scratch += [pltpu.VMEM((2, 8 + gv, n), F32) for n in sizes]
    scratch += [pltpu.VMEM((packed_rows, n * group // 8), F32) for n in sizes] * 2
    scratch += [
        pltpu.VMEM((window + 1, 8, 128), F32),
        pltpu.VMEM((tp, 1, R), F32),
        pltpu.VMEM((window + 1, 8, 128), F32),
        pltpu.VMEM((seq, 8, 128), F32),
        pltpu.VMEM((tp, 8, 128), F32),
        pltpu.VMEM((tp, gv, R), BF16),
        pltpu.VMEM((tp, 16, R * group // 16), BF16),
        pltpu.VMEM((tp, 2, nl, last, cl), F32),
        pltpu.VMEM((tp, nl, last, cl), BF16),
        pltpu.VMEM((tp, nl, last, cl), BF16),
        pltpu.VMEM((tp, last, cl), F32),
        pltpu.VMEM((tp, nl, last, cl), BF16),
        pltpu.VMEM((tp, nz, rc, cl), BF16),
    ]
    for n in (
        (chunks, 2), (chunks,), (window + 1,), (tp,), (window + 1,), (seq,),
        (tp,), (5,), (tp,), (tp, nl), (tp, nz), (tp, nz), (tp, nz),
    ):
        scratch += [dma(n), dma(n)]
    logits, packed, gr = pl.pallas_call(
        functools.partial(kernel, dims),
        out_shape=(
            jax.ShapeDtypeStruct((1, R), F32),
            jax.ShapeDtypeStruct((tp, 2, nz, rc, cl), BF16),
            jax.ShapeDtypeStruct((1, V), F32),
        ),
        in_specs=[pl.BlockSpec(memory_space=pltpu.HBM)] * len(operands),
        out_specs=(pl.BlockSpec(memory_space=pltpu.VMEM),) * 3,
        scratch_shapes=scratch,
        compiler_params=pltpu.CompilerParams(
            collective_id=0, has_side_effects=True, vmem_limit_bytes=40 * 1024 * 1024
        ),
    )(*(pltpu.with_memory_space_constraint(x, pltpu.HBM) for x in operands))
    parts_c = tuple(n // nr for n in rows)
    logits, gs, gvo, gr = pl.pallas_call(
        functools.partial(unpack, (tp, H, V, gv, cut, half, cl, nl, nr, parts_c)),
        out_shape=(
            jax.ShapeDtypeStruct((1, R), F32),
            jax.ShapeDtypeStruct((H, W), F32),
            jax.ShapeDtypeStruct((W, V), F32),
            jax.ShapeDtypeStruct((1, V), F32),
        ),
        in_specs=[pl.BlockSpec(memory_space=pltpu.VMEM)] * 3,
        out_specs=(pl.BlockSpec(memory_space=pl.ANY),) * 4,
        scratch_shapes=[
            pltpu.VMEM((H, W), F32), pltpu.VMEM((W, V), F32), dma((5,)),
        ],
        compiler_params=pltpu.CompilerParams(vmem_limit_bytes=16 * 1024 * 1024),
    )(logits, packed, gr)
    return logits.reshape(R), gs.T, gvo, gr.reshape(V)


def solution(mesh):
    return jax.shard_map(
        shards,
        mesh=mesh,
        in_specs=(P("seq", "tp"), P("tp", None), P("tp", None), P(), P("seq"), P("seq")),
        out_specs=(P("seq"), P("tp", None), P("tp", None), P()),
        check_vma=False,
    )
```

```python
import functools
import math

import jax
import jax.numpy as jnp
import numpy as np
from jax import lax
from jax.experimental import pallas as pl
from jax.experimental.pallas import tpu as pltpu
from jax.sharding import PartitionSpec as P

NEGATIVE = -1e30
POSITIVE = 1e30
MESH = pl.DeviceIdType.MESH
F32 = jnp.float32
BF16 = jnp.bfloat16


def tables(tp_count, head_count):
    group = head_count // tp_count
    pack = 16 // group
    back_s = np.zeros((pack, head_count, tp_count, 16), np.float32)
    for g in range(tp_count):
        for h in range(group):
            for q in range(pack):
                back_s[q, g * group + h, g, q * group + h] = 1
    return back_s.reshape(pack, head_count, tp_count * 16)


def picks(g, group, size, gv, width, scores_at):
    row = lax.broadcasted_iota(jnp.int32, (8 + gv, 1), 0)
    inner = jnp.maximum(row - 8, 0)
    column = jnp.where(
        row < 8,
        scores_at + g * group + lax.rem(row, group),
        (g * group + lax.rem(inner, group)) * size + lax.div(inner, group),
    )
    return (column == lax.broadcasted_iota(jnp.int32, (8 + gv, width), 1)).astype(F32)


def dot_nt(a, b):
    return lax.dot_general(a, b, (((1,), (1,)), ((), ())), preferred_element_type=F32)


def kernel(dims, *refs):
    tp, seq, R, W, H, V, group, gv, nl, nr, rows, cut, window, sizes = dims
    chunks = len(sizes)
    starts = [sum(sizes[:j]) for j in range(chunks)]
    hbm, (logit_ref, afin, gr_ref) = refs[:7], refs[7:10]
    held, load_sem = refs[10:17], refs[17]
    part, recv_a, sum_x, recv_x = (refs[18 + k * chunks : 18 + (k + 1) * chunks] for k in range(4))
    (
        fwd, lgt, bwd, rsum, rdo, coty, cots, gy, ysend, yrecv, zown, zsend, zrecv,
    ) = refs[18 + 4 * chunks : 31 + 4 * chunks]
    (
        a_send, a_recv, x_send, x_recv, f_send, f_recv, l_send, l_recv, b_send, b_recv, s_send, s_recv,
        r_send, r_recv, c_send, c_recv, d_send, d_recv, y_send, y_recv, z_send, z_recv, g_send, g_recv, h_send, h_recv,
    ) = refs[31 + 4 * chunks :]
    tokens_ref, score_ref, value_ref, readout_ref, doc_ref, label_ref, backs_ref = held
    K = gv // 8
    me_t = lax.axis_index("tp")
    me_s = lax.axis_index("seq")
    tx, tc = lax.div(me_t, 2), lax.rem(me_t, 2)
    sz, sy = lax.div(me_s, 2), lax.rem(me_s, 2)
    nz = seq // 2
    partner = (me_t, tx * 2 + 1 - tc, (1 - tx) * 2 + tc, (1 - tx) * 2 + 1 - tc)
    sibling, across = {"tp": partner[1]}, {"tp": partner[2]}
    beside = {"seq": sz * 2 + 1 - sy}

    loads = [None] + [pltpu.make_async_copy(hbm[i], held[i], load_sem.at[i]) for i in range(1, len(hbm))]
    pieces = [
        pltpu.make_async_copy(
            hbm[0].at[pl.ds(at, n)], tokens_ref.at[pl.ds(at, n)], load_sem.at[len(hbm) + j]
        )
        for j, (at, n) in enumerate(zip(starts, sizes))
    ]
    for i in (2, 1):
        loads[i].start()
    for piece in pieces:
        piece.start()
    fwd[...] = jnp.zeros_like(fwd)
    bwd[...] = jnp.zeros_like(bwd)
    barrier = pltpu.get_barrier_semaphore()
    for o in range(1, seq):
        pl.semaphore_signal(barrier, inc=1, device_id={"seq": lax.rem(me_s + o, seq)}, device_id_type=MESH)
    for o in range(1, tp):
        pl.semaphore_signal(barrier, inc=1, device_id={"tp": lax.rem(me_t + o, tp)}, device_id_type=MESH)
    for i in range(3, 7):
        loads[i].start()
    pending = []

    def remote(src, dst, send, recv, device):
        return pltpu.make_async_remote_copy(
            src_ref=src, dst_ref=dst, send_sem=send, recv_sem=recv, device_id=device, device_id_type=MESH
        )

    def give(*args):
        copy = remote(*args)
        copy.start()
        pending.append((None, copy))

    def take(dst, send, recv, device):
        remote(dst, dst, send, recv, device).wait_recv()

    def push(axis, o, src, dst, send, recv):
        give(src, dst, send.at[o], recv.at[o], {axis: partner[o] if axis == "tp" else lax.rem(me_s + o, seq)})

    def arrived(axis, o, dst, send, recv):
        take(dst, send.at[o], recv.at[o], {axis: partner[o] if axis == "tp" else lax.rem(me_s + o, seq)})

    def carry(tile, step, send, recv):
        for o in range(window, 0, -1):
            there = (me_s + step * o >= 0) & (me_s + step * o < seq)
            copy = remote(
                tile.at[0], tile.at[o], send.at[o], recv.at[o], {"seq": lax.rem(me_s + step * o + seq, seq)}
            )
            pl.when(there)(copy.start)
            pending.append((there, copy))

    def carried(tile, step, send, recv):
        for o in range(window, 0, -1):
            here = (me_s - step * o >= 0) & (me_s - step * o < seq)
            copy = remote(
                tile.at[o], tile.at[o], send.at[o], recv.at[o], {"seq": lax.rem(me_s + step * o + seq, seq)}
            )
            pl.when(here)(copy.wait_recv)
        return [(tile[o], (me_s - step * o >= 0) & (me_s - step * o < seq)) for o in range(1, window + 1)]

    size = gv // group
    into_all = jnp.concatenate([picks(g, group, size, gv, V + H, V) for g in range(tp)], axis=0).astype(BF16)
    for i in (2, 1):
        loads[i].wait()
    weights = dot_nt(into_all[:, :V], value_ref[...]) + jnp.dot(
        into_all[:, V:], score_ref[...], preferred_element_type=F32
    )
    weights = weights.astype(BF16)

    per = 8 // group

    def relay(j):
        take(recv_a[j].at[0], a_send.at[j, 0], a_recv.at[j, 0], sibling)
        both = part[j][partner[2]] + recv_a[j][0]
        n = sizes[j] // per
        sub = lax.broadcasted_iota(jnp.int32, (8, n), 0)
        line = both[0:8, :n]
        for k in range(1, per):
            line = jnp.where(sub >= k * group, both[0:8, k * n : (k + 1) * n], line)
        for k in range(per):
            sum_x[j][k * gv : (k + 1) * gv] = both[8 : 8 + gv, k * n : (k + 1) * n]
        sum_x[j][per * gv : per * gv + 8] = line
        give(sum_x[j], recv_x[j], x_send.at[j], x_recv.at[j], across)

    for j in range(chunks):
        pieces[j].wait()
        part[j][...] = dot_nt(weights, tokens_ref[starts[j] : starts[j] + sizes[j]]).reshape(tp, 8 + gv, sizes[j])
        if j == 0:
            pl.semaphore_wait(barrier, tp + seq - 2)
        give(part[j].at[partner[3]], recv_a[j].at[0], a_send.at[j, 0], a_recv.at[j, 0], sibling)
        give(part[j].at[partner[1]], recv_a[j].at[1], a_send.at[j, 1], a_recv.at[j, 1], sibling)
        if j > 0:
            relay(j - 1)
    relay(chunks - 1)
    for i in range(3, 7):
        loads[i].wait()
    lane = lax.broadcasted_iota(jnp.int32, (8, R), 1)
    slot = lax.broadcasted_iota(jnp.int32, (8, 128), 1)
    doc = jnp.broadcast_to(doc_ref[...].astype(F32), (8, R))
    labels = label_ref[...].astype(F32)
    own_table = picks(me_t, group, size, gv, V, V)
    w_col = jnp.sum(own_table * readout_ref[...], axis=1, keepdims=True)
    w_k = [w_col[8 + 8 * k : 16 + 8 * k] for k in range(K)]
    def arrive(j):
        take(recv_a[j].at[1], a_send.at[j, 1], a_recv.at[j, 1], sibling)
        take(recv_x[j], x_send.at[j], x_recv.at[j], across)
        n = sizes[j] // per
        sub = lax.broadcasted_iota(jnp.int32, (8, n), 0)
        near = part[j][me_t] + recv_a[j][1]
        line = recv_x[j][per * gv : per * gv + 8]
        lines = []
        for k in range(per):
            own = pltpu.roll(line, 8 - k * group, 0) if k else line
            wide = own
            for m in range(1, per):
                wide = jnp.where(sub >= m * group, pltpu.roll(own, m * group, 0), wide)
            lines.append(wide)
        out = [near[0:8] + jnp.concatenate(lines, axis=1)]
        for k in range(K):
            far = [recv_x[j][m * gv + 8 * k : m * gv + 8 * k + 8] for m in range(per)]
            out.append(near[8 + 8 * k : 16 + 8 * k] + jnp.concatenate(far, axis=1))
        return out

    def pack(columns):
        tile = jnp.zeros((8, 128), F32)
        for i, column in enumerate(columns):
            tile = jnp.where(slot == i, column, tile)
        return tile

    first, last = doc[:, 0:1], doc[:, R - 1 : R]

    def leave(j, score, vals):
        ours = doc[:, starts[j] :] == last
        top = jnp.max(jnp.where(ours, score, NEGATIVE), axis=1, keepdims=True)
        if j > 0:
            m = sizes[j - 1]
            peak_b, *sums_b = [x[:, m - 1 : m] for x in done[j - 1][: K + 2]]
            linked = doc[:, starts[j] - 1 : starts[j]] == last
            top = jnp.where(linked, jnp.maximum(top, peak_b), top)
        w = jnp.where(ours, jnp.exp(jnp.where(ours, score - top, 0.0)), 0.0)
        sums = [jnp.sum(x, axis=1, keepdims=True) for x in [w] + [w * v for v in vals]]
        if j > 0:
            k_b = jnp.where(linked, jnp.exp(jnp.where(linked, peak_b - top, 0.0)), 0.0)
            sums = [s + k_b * b for s, b in zip(sums, sums_b)]
        fwd[0] = pack([top] + sums + [last])
        carry(fwd, 1, f_send, f_recv)

    done = []
    for j in range(chunks):
        score, *vals = arrive(j)
        if j == chunks - 1:
            leave(j, score, vals)
        at, n = starts[j], sizes[j]
        doc_j, lane_j = doc[:, at : at + n], lane[:, :n]
        peak, total, acc = score, jnp.ones_like(score), list(vals)
        d = 1
        while d < n:
            valid = (lane_j >= d) & (pltpu.roll(doc_j, d, 1) == doc_j)
            before = pltpu.roll(peak, d, 1)
            new = jnp.where(valid, jnp.maximum(peak, before), peak)
            ka = jnp.where(valid, jnp.exp(jnp.where(valid, before - new, 0.0)), 0.0)
            kb = jnp.exp(peak - new)
            total = total * kb + pltpu.roll(total, d, 1) * ka
            acc = [a * kb + pltpu.roll(a, d, 1) * ka for a in acc]
            peak = new
            d *= 2
        if j > 0:
            m = sizes[j - 1]
            peak_b, total_b, *acc_b = [x[:, m - 1 : m] for x in done[j - 1][: K + 2]]
            valid = doc_j == doc[:, at - 1 : at]
            new = jnp.where(valid, jnp.maximum(peak, peak_b), peak)
            ka = jnp.where(valid, jnp.exp(jnp.where(valid, peak_b - new, 0.0)), 0.0)
            kb = jnp.exp(peak - new)
            total = total * kb + total_b * ka
            acc = [a * kb + b * ka for a, b in zip(acc, acc_b)]
            peak = new
        done.append([peak, total] + acc + [score] + vals)
    joined = [jnp.concatenate(x, axis=1) for x in zip(*done)]
    peak, total, acc, score, vals = joined[0], joined[1], joined[2 : K + 2], joined[K + 2], joined[K + 3 :]

    tiles = carried(fwd, 1, f_send, f_recv)
    linked = [(t[:, K + 2 : K + 3] == first) & m for t, m in tiles]
    tiles = [t for t, _ in tiles]
    c_peak = jnp.full((8, 1), NEGATIVE, F32)
    for t, m in zip(tiles, linked):
        c_peak = jnp.maximum(c_peak, jnp.where(m, t[:, 0:1], NEGATIVE))
    c_tile = jnp.zeros((8, 128), F32)
    c_any = jnp.zeros((8, 1), F32)
    for t, m in zip(tiles, linked):
        c_tile = c_tile + jnp.where(m, jnp.exp(jnp.where(m, t[:, 0:1] - c_peak, 0.0)), 0.0) * jnp.where(m, t, 0.0)
        c_any = jnp.where(m, 1.0, c_any)
    cont = (doc == first) & (jnp.broadcast_to(c_any, (8, R)) > 0)
    new = jnp.where(cont, jnp.maximum(peak, c_peak), peak)
    kc = jnp.where(cont, jnp.exp(jnp.where(cont, c_peak - new, 0.0)), 0.0)
    kl = jnp.exp(peak - new)
    peak = new
    inverse = 1.0 / (total * kl + c_tile[:, 1:2] * kc)
    pooled = [(a * kl + c_tile[:, 2 + k : 3 + k] * kc) * inverse for k, a in enumerate(acc)]
    squash = [jnp.tanh(p) for p in pooled]
    lp = squash[0] * w_k[0]
    for k in range(1, K):
        lp = lp + squash[k] * w_k[k]
    lgt[me_t] = jnp.sum(lp, axis=0, keepdims=True)
    for o in (3, 2, 1):
        push("tp", o, lgt.at[me_t], lgt.at[me_t], l_send, l_recv)
    slim = [w * (1.0 - q * q) * inverse for w, q in zip(w_k, squash)]
    slim_c = slim[0] * pooled[0]
    for k in range(1, K):
        slim_c = slim_c + slim[k] * pooled[k]

    def over_heads(x):
        out, step = x, group
        while step < 8:
            out = out + pltpu.roll(out, step, 0)
            step *= 2
        return out

    slim_c = over_heads(slim_c)
    weight = jnp.exp(score - peak)
    for o in range(1, tp):
        arrived("tp", o, lgt.at[partner[o]], l_send, l_recv)
    logits = lgt[0]
    for g in range(1, tp):
        logits = logits + lgt[g]
    logit_ref[...] = logits
    slope = (jax.nn.sigmoid(logits) - labels) * (1.0 / math.sqrt(R * seq))
    slope = jnp.broadcast_to(slope, (8, R))
    adj = [x * slope for x in slim]
    adj_c = slim_c * slope
    ours = doc == first
    peak_f = peak[:, 0:1]
    f = jnp.where(ours, jnp.exp(jnp.where(ours, peak_f - peak, 0.0)), 0.0)
    sums = [jnp.sum(x * f, axis=1, keepdims=True) for x in [adj_c] + adj]
    bwd[0] = pack([peak_f] + sums + [first])
    carry(bwd, -1, b_send, b_recv)
    d = 1
    while d < R:
        valid = (lane < R - d) & (pltpu.roll(doc, R - d, 1) == doc)
        f = jnp.where(valid, jnp.exp(jnp.where(valid, peak - pltpu.roll(peak, R - d, 1), 0.0)), 0.0)
        adj_c = adj_c + f * pltpu.roll(adj_c, R - d, 1)
        adj = [a + f * pltpu.roll(a, R - d, 1) for a in adj]
        d *= 2
    tiles = carried(bwd, -1, b_send, b_recv)
    linked = [(t[:, K + 2 : K + 3] == last) & m for t, m in tiles]
    tiles = [t for t, _ in tiles]
    a_peak = jnp.full((8, 1), POSITIVE, F32)
    for t, m in zip(tiles, linked):
        a_peak = jnp.minimum(a_peak, jnp.where(m, t[:, 0:1], POSITIVE))
    a_tile = jnp.zeros((8, 128), F32)
    a_any = jnp.zeros((8, 1), F32)
    for t, m in zip(tiles, linked):
        a_tile = a_tile + jnp.where(m, jnp.exp(jnp.where(m, a_peak - t[:, 0:1], 0.0)), 0.0) * jnp.where(m, t, 0.0)
        a_any = jnp.where(m, 1.0, a_any)
    reach = (doc == last) & (jnp.broadcast_to(a_any, (8, R)) > 0)
    fac = jnp.where(reach, jnp.exp(jnp.where(reach, peak - a_peak, 0.0)), 0.0)
    adj_c = adj_c + fac * a_tile[:, 1:2]
    adj = [a + fac * a_tile[:, 2 + k : 3 + k] for k, a in enumerate(adj)]
    mix = vals[0] * adj[0]
    for k in range(1, K):
        mix = mix + vals[k] * adj[k]
    d_score = weight * (over_heads(mix) - adj_c)
    coty[me_t] = jnp.concatenate([weight * a for a in adj], axis=0).astype(BF16)
    c_across, c_diag = partner[2], partner[3]
    shares = (pl.ds(0, cut), pl.ds(cut, gv - cut))
    for i, part_i in enumerate(shares):
        give(coty.at[me_t, part_i], coty.at[me_t, part_i], c_send.at[1 + i], c_recv.at[1 + i], across)
    give(coty.at[me_t], coty.at[me_t], c_send.at[0], c_recv.at[0], sibling)
    row = lax.broadcasted_iota(jnp.int32, (8, R), 0)
    packs = 16 // group
    Q = R // packs
    lines = []
    for i in range(0, packs, per):
        line = d_score[:, i * Q : (i + 1) * Q]
        for k in range(1, per):
            line = jnp.where(row[:, :Q] >= k * group, d_score[:, (i + k) * Q : (i + k + 1) * Q], line)
        lines.append(line)
    cots[me_t] = jnp.concatenate(lines, axis=0).astype(BF16)
    for o in (3, 2, 1):
        push("tp", o, cots.at[me_t], cots.at[me_t], d_send, d_recv)

    half, cl = W // 2, W // 2 // nl
    parts_c = [n // nr for n in rows]

    def columns_of():
        return [lax.rem(sz + k, nl) for k in range(1, nl + 1)]

    def product(p):
        if p < 2:
            cot = [coty[partner[p]]]
        elif p == 2:
            cot = [coty[c_across, 0:cut], coty[c_diag, 0:cut]]
        else:
            packed = cots[...].reshape(tp * 16, Q)
            lines = [jnp.dot(backs_ref[q], packed, preferred_element_type=F32) for q in range(packs)]
            cot = [coty[c_across, cut:gv], coty[c_diag, cut:gv], jnp.concatenate(lines, axis=1).astype(BF16)]
        spare = rows[p] - sum(c.shape[0] for c in cot)
        if spare:
            cot.append(jnp.zeros((spare, R), BF16))
        cot = jnp.concatenate(cot, axis=0) if len(cot) > 1 else cot[0]
        out = jnp.dot(cot, tokens_ref[...], preferred_element_type=F32)
        n = rows[p]
        for c in range(nl):
            gy[p, 0, c, 0:n] = out[:, c * cl : (c + 1) * cl]
            gy[p, 1, c, 0:n] = out[:, half + c * cl : half + (c + 1) * cl]
        for c in columns_of():
            ysend[p, c, 0:n] = gy[p, 1 - sy, c, 0:n].astype(BF16)
            give(
                ysend.at[p, c, pl.ds(0, n)], yrecv.at[p, c, pl.ds(0, n)],
                y_send.at[p, c], y_recv.at[p, c], beside,
            )

    def lines_of(to, rc):
        return pl.ds(0, rc) if nr == 1 else pl.ds(pl.multiple_of(lax.div(to, nl) * rc, 16), rc)

    def along_z(p):
        n, rc = rows[p], parts_c[p]
        for k, c in enumerate(columns_of(), 1):
            take(yrecv.at[p, c, pl.ds(0, n)], y_send.at[p, c], y_recv.at[p, c], beside)
            both = gy[p, sy, c, 0:n] + yrecv[p, c, 0:n].astype(F32)
            if k == nl:
                zown[p, 0:n] = both
            zsend[p, c, 0:n] = both.astype(BF16)
            for o in range(k, nz, nl):
                to = lax.rem(sz + o, nz)
                give(
                    zsend.at[p, c, lines_of(to, rc)], zrecv.at[p, sz, pl.ds(0, rc)],
                    z_send.at[p, o], z_recv.at[p, o], {"seq": to * 2 + sy},
                )

    def finish(p):
        rc = parts_c[p]
        total_p = zown[p, lines_of(sz, rc)]
        for o in range(1, nz):
            source = lax.rem(sz + nz - o, nz)
            take(
                zrecv.at[p, source, pl.ds(0, rc)], z_send.at[p, o], z_recv.at[p, o],
                {"seq": lax.rem(sz + o, nz) * 2 + sy},
            )
            total_p = total_p + zrecv[p, source, 0:rc].astype(F32)
        afin[p, sy, sz, 0:rc] = total_p.astype(BF16)
        mine = afin.at[p, sy, sz, pl.ds(0, rc)]
        if p == tp - 1:
            for o in range(1, nz):
                give(mine, mine, h_send.at[p, o], h_recv.at[p, o], {"seq": lax.rem(sz + o, nz) * 2 + 1 - sy})
        for o in range(1, nz):
            give(mine, mine, g_send.at[p, o], g_recv.at[p, o], {"seq": lax.rem(sz + o, nz) * 2 + sy})
        give(mine, mine, h_send.at[p, 0], h_recv.at[p, 0], beside)

    def along_y(p):
        rc = parts_c[p]
        for o in range(1, nz):
            line = afin.at[p, sy, lax.rem(sz + nz - o, nz), pl.ds(0, rc)]
            take(line, g_send.at[p, o], g_recv.at[p, o], {"seq": lax.rem(sz + o, nz) * 2 + sy})
            if p < tp - 1:
                give(line, line, h_send.at[p, o], h_recv.at[p, o], beside)

    def readout_out():
        rsum[me_s] = pack([jnp.sum(q * slope, axis=1, keepdims=True) for q in squash])
        for o in range(1, seq):
            push("seq", o, rsum.at[me_s], rsum.at[me_s], s_send, s_recv)

    def readout_across():
        for o in range(1, seq):
            arrived("seq", o, rsum.at[lax.rem(me_s + seq - o, seq)], s_send, s_recv)
        r_tile = rsum[0]
        for j in range(1, seq):
            r_tile = r_tile + rsum[j]
        rdo[me_t] = r_tile
        for o in (3, 2, 1):
            push("tp", o, rdo.at[me_t], rdo.at[me_t], r_send, r_recv)

    def readout_done():
        for o in range(1, tp):
            arrived("tp", o, rdo.at[partner[o]], r_send, r_recv)
        r_all = jnp.zeros((1, V), F32)
        for g in range(tp):
            tile, table = rdo[g], picks(g, group, size, gv, V, V)
            for k in range(K):
                r_all = r_all + jnp.sum(
                    table[8 + 8 * k : 16 + 8 * k] * tile[:, k : k + 1], axis=0, keepdims=True
                )
        gr_ref[...] = r_all

    def across_in(i):
        line = coty.at[c_across, shares[i]]
        take(line, c_send.at[1 + i], c_recv.at[1 + i], across)
        give(line, line, c_send.at[3 + i], c_recv.at[3 + i], sibling)

    def diagonal_in(i):
        take(coty.at[c_diag, shares[i]], c_send.at[3 + i], c_recv.at[3 + i], sibling)
        if i == 1:
            for o in range(1, tp):
                arrived("tp", o, cots.at[partner[o]], d_send, d_recv)

    def sibling_in():
        take(coty.at[partner[1]], c_send.at[0], c_recv.at[0], sibling)

    product(0)
    readout_out()
    sibling_in()
    product(1)
    along_z(0)
    across_in(0)
    across_in(1)
    along_z(1)
    diagonal_in(0)
    product(2)
    finish(0)
    diagonal_in(1)
    product(3)
    finish(1)
    along_z(2)
    along_z(3)
    readout_across()
    along_y(0)
    finish(2)
    along_y(1)
    finish(3)
    readout_done()
    along_y(2)
    along_y(3)
    for p in range(tp):
        for o in range(nz):
            line = afin.at[p, 1 - sy, lax.rem(sz + nz - o, nz), pl.ds(0, parts_c[p])]
            take(line, h_send.at[p, o], h_recv.at[p, o], beside)
    for when, copy in pending:
        if when is None:
            copy.wait_send()
        else:
            pl.when(when)(copy.wait_send)


def unpack(dims, logit_in, afin, gr_in, logit_ref, gs_ref, gv_ref, gr_ref, gs_held, gv_held, sem):
    tp, H, V, gv, cut, half, cl, nl, nr, parts_c = dims
    me_t = lax.axis_index("tp")
    tx, tc = lax.div(me_t, 2), lax.rem(me_t, 2)
    moves = [
        pltpu.make_async_copy(logit_in, logit_ref, sem.at[0]),
        pltpu.make_async_copy(gr_in, gr_ref, sem.at[1]),
    ]
    for move in moves:
        move.start()
    size = V // H
    group = H // tp
    row = lax.broadcasted_iota(jnp.int32, (V, 1), 0)
    p, inner = lax.div(row, gv), lax.rem(row, gv)
    g = lax.rem(tx + lax.div(p, 2), 2) * 2 + lax.rem(tc + lax.rem(p, 2), 2)
    target = (g * group + lax.rem(inner, group)) * size + lax.div(inner, group)
    order = (target == lax.broadcasted_iota(jnp.int32, (V, V), 1)).astype(F32).astype(BF16)
    for y in range(2):
        for c in range(nl):
            at = y * half + c * cl
            own, beside, others, rest = (
                jnp.concatenate([afin[p, y, r * nl + c, 0 : parts_c[p]] for r in range(nr)], axis=0)
                for p in range(tp)
            )
            left = gv - cut
            stack = jnp.concatenate(
                [own[:gv], beside[:gv], others[:cut], rest[:left], others[cut : 2 * cut], rest[left : 2 * left]], axis=0
            )
            gs_held[:, at : at + cl] = rest[2 * left : 2 * left + H].astype(F32)
            gv_held[at : at + cl, :] = lax.dot_general(
                stack, order, (((0,), (0,)), ((), ())), preferred_element_type=F32
            )
        rows_y = pl.ds(y * half, half)
        moves.append(pltpu.make_async_copy(gv_held.at[rows_y], gv_ref.at[rows_y], sem.at[2 + y]))
        moves[-1].start()
    moves.append(pltpu.make_async_copy(gs_held, gs_ref, sem.at[4]))
    moves[-1].start()
    for move in moves:
        move.wait()


def shards(tokens, score_weight, value_weight, readout, doc_ids, labels):
    tp = lax.axis_size("tp")
    seq = lax.axis_size("seq")
    R, W = tokens.shape
    H = score_weight.shape[1]
    V = value_weight.shape[1]
    group = H // tp
    gv = V // tp
    nz = seq // 2
    nl = min(nz, W // 256)
    nr = nz // nl
    unit = 16 * nr
    cut = gv // 2
    rows = tuple(-(-n // unit) * unit for n in (gv, gv, 2 * cut, 2 * (gv - cut) + H))
    last = max(rows)
    half, cl, rc = W // 2, W // 2 // nl, last // nr
    back_s = tables(tp, H)
    longest = {8192: 4096, 65536: 16384}.get(R * seq, R * seq)
    window = min(seq - 1, -(-longest // R))
    sizes = (R // 2, R // 2)
    chunks = len(sizes)
    dims = (tp, seq, R, W, H, V, group, gv, nl, nr, rows, cut, window, sizes)
    dma = pltpu.SemaphoreType.DMA
    operands = (
        tokens, score_weight.T, value_weight, readout.reshape(1, V),
        doc_ids.reshape(1, R), labels.reshape(1, R), jnp.asarray(back_s, BF16),
    )
    packed_rows = 8 // group * gv + 8
    scratch = [pltpu.VMEM(x.shape, x.dtype) for x in operands] + [dma((len(operands) + chunks,))]
    scratch += [pltpu.VMEM((tp, 8 + gv, n), F32) for n in sizes]
    scratch += [pltpu.VMEM((2, 8 + gv, n), F32) for n in sizes]
    scratch += [pltpu.VMEM((packed_rows, n * group // 8), F32) for n in sizes] * 2
    scratch += [
        pltpu.VMEM((window + 1, 8, 128), F32),
        pltpu.VMEM((tp, 1, R), F32),
        pltpu.VMEM((window + 1, 8, 128), F32),
        pltpu.VMEM((seq, 8, 128), F32),
        pltpu.VMEM((tp, 8, 128), F32),
        pltpu.VMEM((tp, gv, R), BF16),
        pltpu.VMEM((tp, 16, R * group // 16), BF16),
        pltpu.VMEM((tp, 2, nl, last, cl), F32),
        pltpu.VMEM((tp, nl, last, cl), BF16),
        pltpu.VMEM((tp, nl, last, cl), BF16),
        pltpu.VMEM((tp, last, cl), F32),
        pltpu.VMEM((tp, nl, last, cl), BF16),
        pltpu.VMEM((tp, nz, rc, cl), BF16),
    ]
    for n in (
        (chunks, 2), (chunks,), (window + 1,), (tp,), (window + 1,), (seq,),
        (tp,), (5,), (tp,), (tp, nl), (tp, nz), (tp, nz), (tp, nz),
    ):
        scratch += [dma(n), dma(n)]
    logits, packed, gr = pl.pallas_call(
        functools.partial(kernel, dims),
        out_shape=(
            jax.ShapeDtypeStruct((1, R), F32),
            jax.ShapeDtypeStruct((tp, 2, nz, rc, cl), BF16),
            jax.ShapeDtypeStruct((1, V), F32),
        ),
        in_specs=[pl.BlockSpec(memory_space=pltpu.HBM)] * len(operands),
        out_specs=(pl.BlockSpec(memory_space=pltpu.VMEM),) * 3,
        scratch_shapes=scratch,
        compiler_params=pltpu.CompilerParams(
            collective_id=0, has_side_effects=True, vmem_limit_bytes=40 * 1024 * 1024
        ),
    )(*(pltpu.with_memory_space_constraint(x, pltpu.HBM) for x in operands))
    parts_c = tuple(n // nr for n in rows)
    logits, gs, gvo, gr = pl.pallas_call(
        functools.partial(unpack, (tp, H, V, gv, cut, half, cl, nl, nr, parts_c)),
        out_shape=(
            jax.ShapeDtypeStruct((1, R), F32),
            jax.ShapeDtypeStruct((H, W), F32),
            jax.ShapeDtypeStruct((W, V), F32),
            jax.ShapeDtypeStruct((1, V), F32),
        ),
        in_specs=[pl.BlockSpec(memory_space=pltpu.VMEM)] * 3,
        out_specs=(pl.BlockSpec(memory_space=pl.ANY),) * 4,
        scratch_shapes=[
            pltpu.VMEM((H, W), F32), pltpu.VMEM((W, V), F32), dma((5,)),
        ],
        compiler_params=pltpu.CompilerParams(vmem_limit_bytes=16 * 1024 * 1024),
    )(logits, packed, gr)
    return logits.reshape(R), gs.T, gvo, gr.reshape(V)


def solution(mesh):
    return jax.shard_map(
        shards,
        mesh=mesh,
        in_specs=(P("seq", "tp"), P("tp", None), P("tp", None), P(), P("seq"), P("seq")),
        out_specs=(P("seq"), P("tp", None), P("tp", None), P()),
        check_vma=False,
    )
```
